512 devices in a mesh: lon: 32 (over x, y), lat: 4 (over z_lo, core), lev: 4 (over z_hi).
Axes of the slice: x: 4, y: 8, z: 8 (z_hi: 4, z_lo: 2; z = z_hi * 2 + z_lo), core: 2. Of those that a mesh axis runs over, the one named last changes fastest.
Arguments:
- adjoint_field: float32 [12, 12, 128, 4096], P(None, 'lev', 'lat', 'lon'), may hold values from -6 to 6
- east_courant: float32 [12, 128, 4096], P('lev', 'lat', 'lon'), may hold values from -0.2 to 0.2
- north_courant: float32 [12, 128, 4096], P('lev', 'lat', 'lon'), may hold values from -0.2 to 0.2
- pole_courant: float32 [12, 4096], P('lev', 'lon'), may hold values from -0.2 to 0.2
- mix_fraction: float32 [12, 128, 4096], P('lev', 'lat', 'lon'), may hold values from 0.05 to 0.6
- detrain_share: float32 [12, 128, 4096], P('lev', 'lat', 'lon'), may hold values from 0.1 to 3
- sounding_owner: int32 [2, 32768, 1], P(None, ('lon', 'lat')), may hold values from 0 to 127; in each aligned block of 256 rows (0 to 255, 256 to 511, ..., all dimensions but the last counted through in order) at most 4 rows name the same one
- sounding_cell: int32 [2, 32768], P(None, ('lon', 'lat')), may hold values from 0 to 4095
- sounding_count: int32 [2, 128], P(None, ('lon', 'lat')), may hold values from 1 to 256, 20480 in all within a row
- sounding_forcing: float32 [2, 12, 32768], P(None, 'lev', ('lon', 'lat')), may hold values from -6 to 6
Outputs:
- earlier_adjoint: float32 [12, 12, 128, 4096], P(None, 'lev', 'lat', 'lon')
The draws below stay inside these ranges and needn't reach their ends.
Inputs may be any that keep to these rules, and one draw needn't show every extreme that they name: `sounding_owner`: in each aligned block of 256 slots of one step (the slots of one device) no owner is named more than 4 times, a bound that some block reaches. `sounding_count`: each step's counts sum to 20480; at each step some device has exactly 256.
All inputs are finite; a program needn't handle non-finite values.
Results may differ from the reference program's by a relative error of at most 0.0001.
Values sent between devices are 32-bit elements; how exact they have to be, the bound alone decides.
A program may use at most 128 MiB of HBM per device.

```python
import math
import jax
import jax.numpy as jnp
import numpy as np
from jax import lax

NTR = 12
CLAT = 32
CLON = 128
STEPS = 2
S_DEV = 256
OWNERS = 128
CAP = 4
SOUNDINGS = 32768
LIVE = 20480
NLEV = 12
NLAT = 128
NLON = 4096
N_LAT = 4


def with_ends(values, rng, least, largest):
    place = [jax.random.randint(jax.random.fold_in(rng, axis), (), 0, length) for axis, length in enumerate(values.shape)]
    longest = values.shape.index(max(values.shape))
    neighbour = place[:longest] + [(place[longest] + 1) % values.shape[longest]] + place[longest + 1:]
    return values.at[tuple(place)].set(least).at[tuple(neighbour)].set(largest)


def block_scale(own_key, dims, pieces, least, top_value):
    loudness, own = 1.0, jax.random.fold_in(own_key, 6)
    for dim, shards_of in pieces:
        steps = jnp.exp(jax.random.uniform(jax.random.fold_in(own, dim), (shards_of,), jnp.float32, least / len(pieces), top_value / len(pieces)))
        loudness = loudness * jnp.repeat(steps, dims[dim] // shards_of).reshape([-1 if axis == dim else 1 for axis in range(len(dims))])
    return loudness


def profile(amount, total, reach, slope):
    loads = [(1 << 20) // math.isqrt(rank ** slope) + 1 for rank in range(2, amount + 1)]
    surplus, counts = total - reach - (amount - 1), [1] * (amount - 1)
    while surplus > 0:
        free = [i for i in range(amount - 1) if counts[i] < reach]
        mass, left = sum([loads[i] for i in free]), surplus
        for i in free:
            addition = min(reach - counts[i], max(1, left * loads[i] // mass), surplus)
            counts[i] = counts[i] + addition
            surplus = surplus - addition
    return np.array([reach] + counts)


def uneven_parts(stream_key, number_of, total, limit, skew):
    if number_of == 2:
        one = jax.random.randint(stream_key, (), max(1, total - limit), min(limit, total - 1) + 1)
        return jnp.stack([one, total - one])
    sizes = jnp.asarray(profile(number_of, total, limit, skew), jnp.int32)
    couples = (number_of - 1) // 2
    source_of, taker = sizes[1:1 + 2 * couples:2], sizes[2:2 + 2 * couples:2]
    room = jnp.minimum(source_of - 1, limit - taker)
    shifted = jax.random.randint(jax.random.fold_in(stream_key, 1), (couples,), 0, 1 << 20) % (room + 1)
    sizes = sizes.at[1:1 + 2 * couples:2].set(source_of - shifted).at[2:2 + 2 * couples:2].set(taker + shifted)
    return sizes[jax.random.permutation(jax.random.fold_in(stream_key, 2), number_of)]


def deal_out(own_key, own, number, rows, amount, top, most, lean):
    ranking = jax.random.permutation(own_key, amount)
    heavy_load, common = portions_of(amount, rows * top, most, lean, True), portions_of(amount, rows * top, most, lean, False)
    places = jnp.arange(amount)

    def named(tallies, turn):
        used = int((tallies > 0).sum())
        fixed = max(1, used // 4)
        passed = fixed + (places - fixed + turn * (used - fixed)) % max(1, amount - fixed)
        return jnp.zeros((amount,), jnp.int32).at[ranking[jnp.where(places < fixed, places, passed)]].set(jnp.asarray(tallies, jnp.int32))

    tallies = jnp.where(number % 4 == 0, named(heavy_load, number // 4), named(common, number - number // 4 - 1))
    mixed = jax.random.permutation(jax.random.fold_in(own, 3), amount)
    donor, taker = mixed[0:amount // 2 * 2:2], mixed[1:amount // 2 * 2:2]
    margin = jnp.minimum(tallies[donor] - 1, most - tallies[taker]) // 2
    margin = jnp.where((donor == ranking[0]) | (taker == ranking[0]) | (tallies[taker] == 0), 0, jnp.maximum(margin, 0))
    passed = jax.random.randint(jax.random.fold_in(own, 4), (amount // 2,), 0, 1 << 20) % (margin + 1)
    tallies = tallies.at[donor].add(-passed).at[taker].add(passed)
    labels = jnp.searchsorted(jnp.cumsum(tallies), jnp.arange(rows * top), side="right").astype(jnp.int32)
    grid = labels.reshape(top, rows).T
    grid = grid[jax.random.permutation(jax.random.fold_in(own, 1), rows)]
    turn = jax.random.randint(jax.random.fold_in(own, 2), (rows, 1), 0, top)
    return jnp.take_along_axis(grid, (jnp.arange(top)[None, :] + turn) % top, axis=1)


def portions_of(number_of, total, most, lean, full):
    portions = [(1 << 20) // math.isqrt(rank ** lean) + 1 for rank in range(1, number_of + 1)]
    largest = most if full else min(most, max(-(-total // number_of), total * portions[0] // sum(portions)))
    least = 1 if total - largest >= number_of - 1 else 0
    counts, rest = [largest] + [least] * (number_of - 1), total - largest - least * (number_of - 1)
    while rest > 0:
        movable = [i for i in range(1, number_of) if counts[i] < largest] or [i for i in range(1, number_of) if counts[i] < most]
        whole, budget = sum([portions[i] for i in movable]), rest
        for i in movable:
            addition = min(most - counts[i], max(1, budget * portions[i] // whole), rest)
            counts[i] = counts[i] + addition
            rest = rest - addition
    return np.array(counts)


def centred(key, shape, scale, most, cuts=(), held_as=jnp.bfloat16):
    drawn = scale * jax.random.normal(key, shape, jnp.float32)
    if cuts:
        drawn = drawn * block_scale(key, shape, cuts, -0.22, 0.18)
    return jnp.clip(drawn, -most, most).astype(held_as)


def setup_inputs(seed: int = 0) -> dict:
    streams_of = jax.random.split(jax.random.key(seed), 11)
    adjoint_field = centred(streams_of[0], (NTR, NLEV, NLAT, NLON), 1.0, 6.0, ((1, 4), (2, 4), (3, 32)), jnp.float32)
    east_courant = jnp.clip(jax.random.uniform(streams_of[1], (NLEV, NLAT, NLON), jnp.float32, -0.2, 0.2) * block_scale(streams_of[1], (NLEV, NLAT, NLON), ((0, 4), (1, 4), (2, 32)), -0.4, 0.0), -0.2, 0.2)
    north_courant = jnp.clip(jax.random.uniform(streams_of[2], (NLEV, NLAT, NLON), jnp.float32, -0.2, 0.2) * block_scale(streams_of[2], (NLEV, NLAT, NLON), ((0, 4), (1, 4), (2, 32)), -0.4, 0.0), -0.2, 0.2)
    pole_courant = jnp.clip(jax.random.uniform(streams_of[3], (NLEV, NLON), jnp.float32, -0.2, 0.2) * block_scale(streams_of[3], (NLEV, NLON), ((0, 4), (1, 32)), -0.4, 0.0), -0.2, 0.2)
    mix_fraction = jnp.clip(0.05 + 0.55 * jax.random.uniform(streams_of[4], (NLEV, NLAT, NLON), jnp.float32) ** block_scale(streams_of[4], (NLEV, NLAT, NLON), ((0, 4), (1, 4), (2, 32)), -0.2, 0.2), 0.05, 0.6)
    detrain_share = jnp.clip(jnp.exp(math.log(3.0) - 3.4011974 * jax.random.uniform(streams_of[5], (NLEV, NLAT, NLON), jnp.float32) ** block_scale(streams_of[5], (NLEV, NLAT, NLON), ((0, 4), (1, 4), (2, 32)), -0.2, 0.2)), 0.1, 3.0)
    sounding_owner_keys = jax.random.split(jax.random.fold_in(streams_of[6], 1), STEPS * SOUNDINGS // S_DEV)
    sounding_owner_turns = jax.random.permutation(jax.random.fold_in(streams_of[6], 3), STEPS * SOUNDINGS // S_DEV)
    sounding_owner = jax.vmap(lambda own, number: deal_out(jax.random.fold_in(streams_of[6], 2), own, number, S_DEV, OWNERS, 1, CAP, 2))(sounding_owner_keys, sounding_owner_turns).reshape((STEPS, SOUNDINGS, 1))
    sounding_cell = with_ends(jax.random.randint(streams_of[7], (STEPS, SOUNDINGS), 0, CLAT * CLON), jax.random.fold_in(streams_of[7], 1), 0, (CLAT * CLON) - 1).astype(jnp.int32)
    sounding_count = jax.vmap(lambda own: uneven_parts(own, OWNERS, LIVE, S_DEV, 2))(jax.random.split(streams_of[8], STEPS)).reshape((STEPS, OWNERS)).astype(jnp.int32)
    sounding_forcing = centred(streams_of[9], (STEPS, NLEV, SOUNDINGS), 1.0, 6.0, ((1, 4), (2, 128)), jnp.float32)
    return dict(adjoint_field=adjoint_field, east_courant=east_courant, north_courant=north_courant, pole_courant=pole_courant, mix_fraction=mix_fraction, detrain_share=detrain_share, sounding_owner=sounding_owner, sounding_cell=sounding_cell, sounding_count=sounding_count, sounding_forcing=sounding_forcing)


def reference(adjoint_field, east_courant, north_courant, pole_courant, mix_fraction, detrain_share, sounding_owner, sounding_cell, sounding_count, sounding_forcing):
    half_circle = NLON // 2
    upwind_east = jnp.maximum(east_courant, 0.0)
    upwind_west = -jnp.minimum(jnp.roll(east_courant, 1, axis=2), 0.0)
    lat_index = jnp.arange(NLAT, dtype=jnp.int32)[None, :, None]
    partner_top = jnp.roll(north_courant[:, -1, :], half_circle, axis=1)
    partner_pole = jnp.roll(pole_courant, half_circle, axis=1)
    upwind_north = jnp.maximum(north_courant, 0.0) + jnp.where(lat_index == NLAT - 1, -jnp.minimum(partner_top, 0.0)[:, None, :], 0.0)
    south_wind = jnp.concatenate([jnp.zeros_like(north_courant[:, :1, :]), north_courant[:, :-1, :]], axis=1)
    upwind_south = jnp.where(lat_index == 0, (jnp.maximum(pole_courant, 0.0) - jnp.minimum(partner_pole, 0.0))[:, None, :], -jnp.minimum(south_wind, 0.0))

    slot_index = jnp.arange(SOUNDINGS, dtype=jnp.int32)
    holder = (slot_index // S_DEV).astype(jnp.int32)
    live_slots = (slot_index % S_DEV)[None, :] < sounding_count[:, holder]
    owner_ids = sounding_owner[:, :, 0]
    grid_row = (owner_ids % N_LAT) * CLAT + sounding_cell // CLON
    grid_col = (owner_ids // N_LAT) * CLON + sounding_cell % CLON
    flat_index = (grid_row * NLON + grid_col).astype(jnp.int32)
    values = jnp.where(live_slots[:, None, :], sounding_forcing, 0.0)
    step_ids = jnp.arange(STEPS, dtype=jnp.int32)[:, None]
    forcing_grid = jnp.zeros((STEPS, NLEV, NLAT * NLON), jnp.float32).at[step_ids, :, flat_index].add(jnp.swapaxes(values, 1, 2))
    forcing_grid = forcing_grid.reshape(STEPS, NLEV, NLAT, NLON)
    column_total = jnp.sum(detrain_share, axis=0)

    def one_tracer(adjoint):
        for position in range(STEPS):
            step_now = STEPS - 1 - position
            adjoint = adjoint + forcing_grid[step_now]
            column_sum = jnp.sum(detrain_share * adjoint, axis=0)
            adjoint = (1.0 - mix_fraction) * adjoint + mix_fraction * (column_sum / column_total)[None]
            east_side = jnp.roll(adjoint, -1, axis=2)
            west_side = jnp.roll(adjoint, 1, axis=2)
            north_side = jnp.concatenate([adjoint[:, 1:, :], jnp.roll(adjoint[:, -1:, :], half_circle, axis=2)], axis=1)
            south_side = jnp.concatenate([jnp.roll(adjoint[:, :1, :], half_circle, axis=2), adjoint[:, :-1, :]], axis=1)
            adjoint = adjoint + upwind_east * (east_side - adjoint) + upwind_west * (west_side - adjoint) + upwind_north * (north_side - adjoint) + upwind_south * (south_side - adjoint)
        return adjoint

    return lax.map(one_tracer, adjoint_field)
```

```python
import jax
import jax.numpy as jnp
from jax import lax
from jax.sharding import PartitionSpec as P


def from_behind(value, axis, steps):
    count = lax.axis_size(axis)
    pairs = [(source, (source + steps) % count) for source in range(count)]
    return lax.ppermute(value, axis, pairs)


def from_behind_2(block, axis, distance):
    devices = range(lax.axis_size(axis))
    route = [(i - distance, i) for i in devices if i - distance in devices]
    return lax.ppermute(block, axis, route)


def extended(x, sides, width, wrap):
    for axis, dim in sides:
        size, length = (lax.axis_size(axis), x.shape[dim])
        up = [(i, (i + 1) % size) for i in range(size if wrap else size - 1)]
        down = [(j, i) for i, j in up]
        last = lax.slice_in_dim(x, length - width, length, axis=dim)
        initial = lax.slice_in_dim(x, 0, width, axis=dim)
        before = lax.ppermute(last, axis, up)
        after = lax.ppermute(initial, axis, down)
        x = jnp.concatenate([before, x, after], axis=dim)
    return x


def mix_sum(partial_sum):
    return lax.psum(partial_sum, "lev")


def on_device(
    adjoint_field,
    east_courant,
    north_courant,
    pole_courant,
    mix_fraction,
    detrain_share,
    sounding_owner,
    sounding_cell,
    sounding_count,
    sounding_forcing,
):
    lon_count = lax.axis_size("lon")
    lat_count = lax.axis_size("lat")
    lat_place = lax.axis_index("lat")
    owner_self = lax.axis_index("lon") * lat_count + lat_place
    tracers, lev_dev, lat_rows, lon_cols = adjoint_field.shape
    step_count = sounding_forcing.shape[0]
    slot_count = sounding_forcing.shape[2]
    grid_cells = lat_rows * lon_cols
    owner_count = lon_count * lat_count
    cap = 4
    live_slots = jnp.arange(slot_count, dtype=jnp.int32)[None, :] < sounding_count
    values = jnp.where(live_slots[:, None, :], sounding_forcing, 0.0)
    owner_ids = sounding_owner[:, :, 0]
    slot_iota = jnp.arange(slot_count, dtype=jnp.int32)
    earlier = slot_iota[None, :, None] < slot_iota[None, None, :]
    same_owner = owner_ids[:, :, None] == owner_ids[:, None, :]
    rank = jnp.sum(jnp.logical_and(earlier, same_owner), axis=1, dtype=jnp.int32)
    position = owner_ids * cap + rank
    bucket_iota = jnp.arange(owner_count * cap, dtype=jnp.int32)
    chosen = position[:, :, None] == bucket_iota[None, None, :]
    bucket_values = jnp.sum(
        jnp.where(chosen[:, None, :, :], values[:, :, :, None], 0.0), axis=2
    )
    bucket_cell = jnp.max(
        jnp.where(chosen, sounding_cell[:, :, None] + 1, 0), axis=1
    ).astype(jnp.float32) - 1.0
    packed = jnp.concatenate([bucket_values, bucket_cell[:, None, :]], axis=1)
    packed = packed.reshape(step_count, lev_dev + 1, owner_count, cap)
    packed = jnp.transpose(packed, (2, 0, 1, 3))
    arrived = lax.all_to_all(packed, ("lon", "lat"), 0, 0, tiled=True)
    arrived = jnp.transpose(arrived, (1, 2, 0, 3)).reshape(
        step_count, lev_dev + 1, owner_count * cap
    )
    cell_iota = jnp.arange(grid_cells, dtype=jnp.int32).astype(jnp.float32)
    hit = (arrived[:, lev_dev, :, None] == cell_iota[None, None, :]).astype(jnp.float32)
    forcing_grid = jnp.einsum(
        "tke,tec->tkc", arrived[:, :lev_dev, :], hit, precision=lax.Precision.HIGHEST
    )
    forcing_grid = forcing_grid.reshape(step_count, lev_dev, lat_rows, lon_cols)
    west_column = from_behind(east_courant[:, :, -1:], "lon", 1)
    west_wind = jnp.concatenate([west_column, east_courant[:, :, :-1]], axis=2)
    south_row = from_behind_2(north_courant[:, -1:, :], "lat", 1)
    south_wind = jnp.concatenate([south_row, north_courant[:, :-1, :]], axis=1)
    pole_pair = jnp.stack([north_courant[:, -1, :], pole_courant], axis=0)
    partner_winds = from_behind(pole_pair, "lon", lon_count // 2)
    row_index = jnp.arange(lat_rows, dtype=jnp.int32)[None, :, None]
    at_top = jnp.logical_and(lat_place == lat_count - 1, row_index == lat_rows - 1)
    at_bottom = jnp.logical_and(lat_place == 0, row_index == 0)
    upwind_east = jnp.maximum(east_courant, 0.0)
    upwind_west = -jnp.minimum(west_wind, 0.0)
    upwind_north = jnp.maximum(north_courant, 0.0) + jnp.where(
        at_top, -jnp.minimum(partner_winds[0], 0.0)[:, None, :], 0.0
    )
    upwind_south = jnp.where(
        at_bottom,
        (jnp.maximum(pole_courant, 0.0) - jnp.minimum(partner_winds[1], 0.0))[:, None, :],
        -jnp.minimum(south_wind, 0.0),
    )
    total_detrain = lax.psum(jnp.sum(detrain_share, axis=0), "lev")
    adjoint = adjoint_field
    for position in range(step_count):
        step_now = step_count - 1 - position
        adjoint = adjoint + forcing_grid[step_now][None]
        partial_sum = jnp.sum(detrain_share[None] * adjoint, axis=1)
        column_sum = mix_sum(partial_sum)
        adjoint = (1.0 - mix_fraction)[None] * adjoint + mix_fraction[None] * (
            column_sum / total_detrain
        )[:, None]
        across = extended(adjoint, (("lon", 3),), 1, True)
        east_side = across[:, :, :, 2:]
        west_side = across[:, :, :, :-2]
        upright = extended(adjoint, (("lat", 2),), 1, False)
        north_side = upright[:, :, 2:, :]
        south_side = upright[:, :, :-2, :]
        edge_row = jnp.where(lat_place == 0, adjoint[:, :, :1, :], adjoint[:, :, -1:, :])
        partner_row = from_behind(edge_row, "lon", lon_count // 2)
        north_side = jnp.where(at_top, partner_row, north_side)
        south_side = jnp.where(at_bottom, partner_row, south_side)
        adjoint = (
            adjoint
            + upwind_east * (east_side - adjoint)
            + upwind_west * (west_side - adjoint)
            + upwind_north * (north_side - adjoint)
            + upwind_south * (south_side - adjoint)
        )
    return adjoint


def solution(mesh):
    return jax.shard_map(
        on_device,
        mesh=mesh,
        in_specs=(
            P(None, "lev", "lat", "lon"),
            P("lev", "lat", "lon"),
            P("lev", "lat", "lon"),
            P("lev", "lon"),
            P("lev", "lat", "lon"),
            P("lev", "lat", "lon"),
            P(None, ("lon", "lat"), None),
            P(None, ("lon", "lat")),
            P(None, ("lon", "lat")),
            P(None, "lev", ("lon", "lat")),
        ),
        out_specs=P(None, "lev", "lat", "lon"),
        check_vma=False,
    )
```

```python
import functools

import jax
import jax.numpy as jnp
from jax import lax
from jax.experimental import pallas as pl
from jax.experimental.pallas import tpu as pltpu
from jax.sharding import PartitionSpec as P

MESH = pl.DeviceIdType.MESH


def lev_sum_body(n, part_ref, out_ref, slots, send_sem, recv_sem):
    me = lax.axis_index("lev")
    barrier = pltpu.get_barrier_semaphore()
    for d in range(1, n):
        pl.semaphore_signal(
            barrier, inc=1, device_id={"lev": lax.rem(me + d, n)}, device_id_type=MESH
        )
    pl.semaphore_wait(barrier, n - 1)
    sends = []
    for d in range(1, n):
        copy = pltpu.make_async_remote_copy(
            src_ref=part_ref,
            dst_ref=slots.at[me],
            send_sem=send_sem.at[d - 1],
            recv_sem=recv_sem.at[me],
            device_id={"lev": lax.rem(me + d, n)},
            device_id_type=MESH,
        )
        copy.start()
        sends.append(copy)
    slots[me] = part_ref[...]
    for d in range(1, n):
        sender = lax.rem(me + n - d, n)
        pltpu.make_async_remote_copy(
            src_ref=part_ref,
            dst_ref=slots.at[sender],
            send_sem=send_sem.at[d - 1],
            recv_sem=recv_sem.at[sender],
            device_id={"lev": sender},
            device_id_type=MESH,
        ).wait_recv()
    for copy in sends:
        copy.wait_send()
    total = slots[0]
    for s in range(1, n):
        total = total + slots[s]
    out_ref[...] = total


def lev_sum(x, collective_id):
    n = lax.axis_size("lev")
    return pl.pallas_call(
        functools.partial(lev_sum_body, n),
        out_shape=jax.ShapeDtypeStruct(x.shape, x.dtype),
        in_specs=[pl.BlockSpec(memory_space=pltpu.VMEM)],
        out_specs=pl.BlockSpec(memory_space=pltpu.VMEM),
        scratch_shapes=[
            pltpu.VMEM((n,) + x.shape, x.dtype),
            pltpu.SemaphoreType.DMA((n - 1,)),
            pltpu.SemaphoreType.DMA((n,)),
        ],
        compiler_params=pltpu.CompilerParams(
            collective_id=collective_id, has_side_effects=True
        ),
    )(x)


def from_behind(value, axis, steps):
    count = lax.axis_size(axis)
    pairs = [(source, (source + steps) % count) for source in range(count)]
    return lax.ppermute(value, axis, pairs)


def from_behind_2(block, axis, distance):
    devices = range(lax.axis_size(axis))
    route = [(i - distance, i) for i in devices if i - distance in devices]
    return lax.ppermute(block, axis, route)


def extended(x, sides, width, wrap):
    for axis, dim in sides:
        size, length = (lax.axis_size(axis), x.shape[dim])
        up = [(i, (i + 1) % size) for i in range(size if wrap else size - 1)]
        down = [(j, i) for i, j in up]
        last = lax.slice_in_dim(x, length - width, length, axis=dim)
        initial = lax.slice_in_dim(x, 0, width, axis=dim)
        before = lax.ppermute(last, axis, up)
        after = lax.ppermute(initial, axis, down)
        x = jnp.concatenate([before, x, after], axis=dim)
    return x


def mix_sum(partial_sum):
    return lax.psum(partial_sum, "lev")


def on_device(
    adjoint_field,
    east_courant,
    north_courant,
    pole_courant,
    mix_fraction,
    detrain_share,
    sounding_owner,
    sounding_cell,
    sounding_count,
    sounding_forcing,
):
    lon_count = lax.axis_size("lon")
    lat_count = lax.axis_size("lat")
    lat_place = lax.axis_index("lat")
    owner_self = lax.axis_index("lon") * lat_count + lat_place
    tracers, lev_dev, lat_rows, lon_cols = adjoint_field.shape
    step_count = sounding_forcing.shape[0]
    slot_count = sounding_forcing.shape[2]
    grid_cells = lat_rows * lon_cols
    owner_count = lon_count * lat_count
    cap = 4
    live_slots = jnp.arange(slot_count, dtype=jnp.int32)[None, :] < sounding_count
    values = jnp.where(live_slots[:, None, :], sounding_forcing, 0.0)
    owner_ids = sounding_owner[:, :, 0]
    slot_iota = jnp.arange(slot_count, dtype=jnp.int32)
    earlier = slot_iota[None, :, None] < slot_iota[None, None, :]
    same_owner = owner_ids[:, :, None] == owner_ids[:, None, :]
    rank = jnp.sum(jnp.logical_and(earlier, same_owner), axis=1, dtype=jnp.int32)
    position = owner_ids * cap + rank
    bucket_iota = jnp.arange(owner_count * cap, dtype=jnp.int32)
    chosen = position[:, :, None] == bucket_iota[None, None, :]
    bucket_values = jnp.sum(
        jnp.where(chosen[:, None, :, :], values[:, :, :, None], 0.0), axis=2
    )
    bucket_cell = jnp.max(
        jnp.where(chosen, sounding_cell[:, :, None] + 1, 0), axis=1
    ).astype(jnp.float32) - 1.0
    packed = jnp.concatenate([bucket_values, bucket_cell[:, None, :]], axis=1)
    packed = packed.reshape(step_count, lev_dev + 1, owner_count, cap)
    packed = jnp.transpose(packed, (2, 0, 1, 3))
    arrived = lax.all_to_all(packed, ("lon", "lat"), 0, 0, tiled=True)
    arrived = jnp.transpose(arrived, (1, 2, 0, 3)).reshape(
        step_count, lev_dev + 1, owner_count * cap
    )
    cell_iota = jnp.arange(grid_cells, dtype=jnp.int32).astype(jnp.float32)
    hit = (arrived[:, lev_dev, :, None] == cell_iota[None, None, :]).astype(jnp.float32)
    forcing_grid = jnp.einsum(
        "tke,tec->tkc", arrived[:, :lev_dev, :], hit, precision=lax.Precision.HIGHEST
    )
    forcing_grid = forcing_grid.reshape(step_count, lev_dev, lat_rows, lon_cols)
    west_column = from_behind(east_courant[:, :, -1:], "lon", 1)
    west_wind = jnp.concatenate([west_column, east_courant[:, :, :-1]], axis=2)
    south_row = from_behind_2(north_courant[:, -1:, :], "lat", 1)
    south_wind = jnp.concatenate([south_row, north_courant[:, :-1, :]], axis=1)
    pole_pair = jnp.stack([north_courant[:, -1, :], pole_courant], axis=0)
    partner_winds = from_behind(pole_pair, "lon", lon_count // 2)
    row_index = jnp.arange(lat_rows, dtype=jnp.int32)[None, :, None]
    at_top = jnp.logical_and(lat_place == lat_count - 1, row_index == lat_rows - 1)
    at_bottom = jnp.logical_and(lat_place == 0, row_index == 0)
    upwind_east = jnp.maximum(east_courant, 0.0)
    upwind_west = -jnp.minimum(west_wind, 0.0)
    upwind_north = jnp.maximum(north_courant, 0.0) + jnp.where(
        at_top, -jnp.minimum(partner_winds[0], 0.0)[:, None, :], 0.0
    )
    upwind_south = jnp.where(
        at_bottom,
        (jnp.maximum(pole_courant, 0.0) - jnp.minimum(partner_winds[1], 0.0))[:, None, :],
        -jnp.minimum(south_wind, 0.0),
    )
    detrain_part = jnp.sum(detrain_share, axis=0)
    adjoint = adjoint_field
    for position in range(step_count):
        step_now = step_count - 1 - position
        adjoint = adjoint + forcing_grid[step_now][None]
        partial_sum = jnp.sum(detrain_share[None] * adjoint, axis=1)
        if position == 0:
            reduced = lev_sum(
                jnp.concatenate([partial_sum, detrain_part[None]], axis=0), 0
            )
            column_sum, total_detrain = reduced[:tracers], reduced[tracers]
        else:
            column_sum = lev_sum(partial_sum, 1)
        adjoint = (1.0 - mix_fraction)[None] * adjoint + mix_fraction[None] * (
            column_sum / total_detrain
        )[:, None]
        across = extended(adjoint, (("lon", 3),), 1, True)
        east_side = across[:, :, :, 2:]
        west_side = across[:, :, :, :-2]
        upright = extended(adjoint, (("lat", 2),), 1, False)
        north_side = upright[:, :, 2:, :]
        south_side = upright[:, :, :-2, :]
        edge_row = jnp.where(lat_place == 0, adjoint[:, :, :1, :], adjoint[:, :, -1:, :])
        partner_row = from_behind(edge_row, "lon", lon_count // 2)
        north_side = jnp.where(at_top, partner_row, north_side)
        south_side = jnp.where(at_bottom, partner_row, south_side)
        adjoint = (
            adjoint
            + upwind_east * (east_side - adjoint)
            + upwind_west * (west_side - adjoint)
            + upwind_north * (north_side - adjoint)
            + upwind_south * (south_side - adjoint)
        )
    return adjoint


def solution(mesh):
    return jax.shard_map(
        on_device,
        mesh=mesh,
        in_specs=(
            P(None, "lev", "lat", "lon"),
            P("lev", "lat", "lon"),
            P("lev", "lat", "lon"),
            P("lev", "lon"),
            P("lev", "lat", "lon"),
            P("lev", "lat", "lon"),
            P(None, ("lon", "lat"), None),
            P(None, ("lon", "lat")),
            P(None, ("lon", "lat")),
            P(None, "lev", ("lon", "lat")),
        ),
        out_specs=P(None, "lev", "lat", "lon"),
        check_vma=False,
    )
```

```python
import functools

import jax
import jax.numpy as jnp
from jax import lax
from jax.experimental import pallas as pl
from jax.experimental.pallas import tpu as pltpu
from jax.sharding import PartitionSpec as P

MESH = pl.DeviceIdType.MESH


def lev_sum_body(n, part_ref, out_ref, slots, send_sem, recv_sem):
    me = lax.axis_index("lev")
    barrier = pltpu.get_barrier_semaphore()
    for d in range(1, n):
        pl.semaphore_signal(
            barrier, inc=1, device_id={"lev": lax.rem(me + d, n)}, device_id_type=MESH
        )
    pl.semaphore_wait(barrier, n - 1)
    sends = []
    for d in range(1, n):
        copy = pltpu.make_async_remote_copy(
            src_ref=part_ref,
            dst_ref=slots.at[me],
            send_sem=send_sem.at[d - 1],
            recv_sem=recv_sem.at[me],
            device_id={"lev": lax.rem(me + d, n)},
            device_id_type=MESH,
        )
        copy.start()
        sends.append(copy)
    slots[me] = part_ref[...]
    for d in range(1, n):
        sender = lax.rem(me + n - d, n)
        pltpu.make_async_remote_copy(
            src_ref=part_ref,
            dst_ref=slots.at[sender],
            send_sem=send_sem.at[d - 1],
            recv_sem=recv_sem.at[sender],
            device_id={"lev": sender},
            device_id_type=MESH,
        ).wait_recv()
    for copy in sends:
        copy.wait_send()
    total = slots[0]
    for s in range(1, n):
        total = total + slots[s]
    out_ref[...] = total


def halo_body(lon_n, lat_n, col_last, col_first, row_last, row_first,
              west_out, east_out, north_out, south_out, cols, rows, send_sem, col_sem, row_sem):
    lon = lax.axis_index("lon")
    lat = lax.axis_index("lat")
    half = lon_n // 2
    top = lat // (lat_n - 1)
    inner = (lat + lat_n - 1) // lat_n
    east = {"lon": lax.rem(lon + 1, lon_n)}
    west = {"lon": lax.rem(lon + lon_n - 1, lon_n)}
    up = {"lon": lax.rem(lon + half * top, lon_n), "lat": lat + 1 - top}
    down = {"lon": lax.rem(lon + half * (1 - inner), lon_n), "lat": lat - inner}
    up_slot = 1 - top
    down_slot = 1 - inner
    barrier = pltpu.get_barrier_semaphore()
    for peer in (east, west, up, down):
        pl.semaphore_signal(barrier, inc=1, device_id=peer, device_id_type=MESH)
    pl.semaphore_wait(barrier, 4)
    plan = (
        (col_last, cols.at[0], col_sem.at[0], east),
        (col_first, cols.at[1], col_sem.at[1], west),
        (row_last, rows.at[up_slot], row_sem.at[up_slot], up),
        (row_first, rows.at[down_slot], row_sem.at[down_slot], down),
    )
    sends = []
    for i, (src, dst, sem, peer) in enumerate(plan):
        copy = pltpu.make_async_remote_copy(
            src_ref=src, dst_ref=dst, send_sem=send_sem.at[i], recv_sem=sem,
            device_id=peer, device_id_type=MESH,
        )
        copy.start()
        sends.append(copy)
    arrivals = (
        (col_last, cols.at[0], col_sem.at[0]),
        (col_first, cols.at[1], col_sem.at[1]),
        (row_last, rows.at[0], row_sem.at[0]),
        (row_first, rows.at[1], row_sem.at[1]),
    )
    for src, dst, sem in arrivals:
        pltpu.make_async_remote_copy(
            src_ref=src, dst_ref=dst, send_sem=send_sem.at[0], recv_sem=sem,
            device_id=east, device_id_type=MESH,
        ).wait_recv()
    for copy in sends:
        copy.wait_send()
    west_out[...] = cols[0]
    east_out[...] = cols[1]
    north_out[...] = rows[0]
    south_out[...] = rows[1]


def halo_swap(col_last, col_first, row_last, row_first, collective_id):
    lon_n, lat_n = lax.axis_size("lon"), lax.axis_size("lat")
    vmem = pl.BlockSpec(memory_space=pltpu.VMEM)
    return pl.pallas_call(
        functools.partial(halo_body, lon_n, lat_n),
        out_shape=(
            jax.ShapeDtypeStruct(col_last.shape, col_last.dtype),
            jax.ShapeDtypeStruct(col_last.shape, col_last.dtype),
            jax.ShapeDtypeStruct(row_last.shape, row_last.dtype),
            jax.ShapeDtypeStruct(row_last.shape, row_last.dtype),
        ),
        in_specs=[vmem] * 4,
        out_specs=(vmem,) * 4,
        scratch_shapes=[
            pltpu.VMEM((2,) + col_last.shape, col_last.dtype),
            pltpu.VMEM((2,) + row_last.shape, row_last.dtype),
            pltpu.SemaphoreType.DMA((4,)),
            pltpu.SemaphoreType.DMA((2,)),
            pltpu.SemaphoreType.DMA((2,)),
        ],
        compiler_params=pltpu.CompilerParams(
            collective_id=collective_id, has_side_effects=True
        ),
    )(col_last, col_first, row_last, row_first)


def lev_sum(x, collective_id):
    n = lax.axis_size("lev")
    return pl.pallas_call(
        functools.partial(lev_sum_body, n),
        out_shape=jax.ShapeDtypeStruct(x.shape, x.dtype),
        in_specs=[pl.BlockSpec(memory_space=pltpu.VMEM)],
        out_specs=pl.BlockSpec(memory_space=pltpu.VMEM),
        scratch_shapes=[
            pltpu.VMEM((n,) + x.shape, x.dtype),
            pltpu.SemaphoreType.DMA((n - 1,)),
            pltpu.SemaphoreType.DMA((n,)),
        ],
        compiler_params=pltpu.CompilerParams(
            collective_id=collective_id, has_side_effects=True
        ),
    )(x)


def from_behind(value, axis, steps):
    count = lax.axis_size(axis)
    pairs = [(source, (source + steps) % count) for source in range(count)]
    return lax.ppermute(value, axis, pairs)


def from_behind_2(block, axis, distance):
    devices = range(lax.axis_size(axis))
    route = [(i - distance, i) for i in devices if i - distance in devices]
    return lax.ppermute(block, axis, route)


def extended(x, sides, width, wrap):
    for axis, dim in sides:
        size, length = (lax.axis_size(axis), x.shape[dim])
        up = [(i, (i + 1) % size) for i in range(size if wrap else size - 1)]
        down = [(j, i) for i, j in up]
        last = lax.slice_in_dim(x, length - width, length, axis=dim)
        initial = lax.slice_in_dim(x, 0, width, axis=dim)
        before = lax.ppermute(last, axis, up)
        after = lax.ppermute(initial, axis, down)
        x = jnp.concatenate([before, x, after], axis=dim)
    return x


def mix_sum(partial_sum):
    return lax.psum(partial_sum, "lev")


def on_device(
    adjoint_field,
    east_courant,
    north_courant,
    pole_courant,
    mix_fraction,
    detrain_share,
    sounding_owner,
    sounding_cell,
    sounding_count,
    sounding_forcing,
):
    lon_count = lax.axis_size("lon")
    lat_count = lax.axis_size("lat")
    lat_place = lax.axis_index("lat")
    owner_self = lax.axis_index("lon") * lat_count + lat_place
    tracers, lev_dev, lat_rows, lon_cols = adjoint_field.shape
    step_count = sounding_forcing.shape[0]
    slot_count = sounding_forcing.shape[2]
    grid_cells = lat_rows * lon_cols
    owner_count = lon_count * lat_count
    cap = 4
    live_slots = jnp.arange(slot_count, dtype=jnp.int32)[None, :] < sounding_count
    values = jnp.where(live_slots[:, None, :], sounding_forcing, 0.0)
    owner_ids = sounding_owner[:, :, 0]
    slot_iota = jnp.arange(slot_count, dtype=jnp.int32)
    earlier = slot_iota[None, :, None] < slot_iota[None, None, :]
    same_owner = owner_ids[:, :, None] == owner_ids[:, None, :]
    rank = jnp.sum(jnp.logical_and(earlier, same_owner), axis=1, dtype=jnp.int32)
    position = owner_ids * cap + rank
    bucket_iota = jnp.arange(owner_count * cap, dtype=jnp.int32)
    chosen = position[:, :, None] == bucket_iota[None, None, :]
    bucket_values = jnp.sum(
        jnp.where(chosen[:, None, :, :], values[:, :, :, None], 0.0), axis=2
    )
    bucket_cell = jnp.max(
        jnp.where(chosen, sounding_cell[:, :, None] + 1, 0), axis=1
    ).astype(jnp.float32) - 1.0
    packed = jnp.concatenate([bucket_values, bucket_cell[:, None, :]], axis=1)
    packed = packed.reshape(step_count, lev_dev + 1, owner_count, cap)
    packed = jnp.transpose(packed, (2, 0, 1, 3))
    arrived = lax.all_to_all(packed, ("lon", "lat"), 0, 0, tiled=True)
    arrived = jnp.transpose(arrived, (1, 2, 0, 3)).reshape(
        step_count, lev_dev + 1, owner_count * cap
    )
    cell_iota = jnp.arange(grid_cells, dtype=jnp.int32).astype(jnp.float32)
    hit = (arrived[:, lev_dev, :, None] == cell_iota[None, None, :]).astype(jnp.float32)
    forcing_grid = jnp.einsum(
        "tke,tec->tkc", arrived[:, :lev_dev, :], hit, precision=lax.Precision.HIGHEST
    )
    forcing_grid = forcing_grid.reshape(step_count, lev_dev, lat_rows, lon_cols)
    west_column = from_behind(east_courant[:, :, -1:], "lon", 1)
    west_wind = jnp.concatenate([west_column, east_courant[:, :, :-1]], axis=2)
    south_row = from_behind_2(north_courant[:, -1:, :], "lat", 1)
    south_wind = jnp.concatenate([south_row, north_courant[:, :-1, :]], axis=1)
    pole_pair = jnp.stack([north_courant[:, -1, :], pole_courant], axis=0)
    partner_winds = from_behind(pole_pair, "lon", lon_count // 2)
    row_index = jnp.arange(lat_rows, dtype=jnp.int32)[None, :, None]
    at_top = jnp.logical_and(lat_place == lat_count - 1, row_index == lat_rows - 1)
    at_bottom = jnp.logical_and(lat_place == 0, row_index == 0)
    upwind_east = jnp.maximum(east_courant, 0.0)
    upwind_west = -jnp.minimum(west_wind, 0.0)
    upwind_north = jnp.maximum(north_courant, 0.0) + jnp.where(
        at_top, -jnp.minimum(partner_winds[0], 0.0)[:, None, :], 0.0
    )
    upwind_south = jnp.where(
        at_bottom,
        (jnp.maximum(pole_courant, 0.0) - jnp.minimum(partner_winds[1], 0.0))[:, None, :],
        -jnp.minimum(south_wind, 0.0),
    )
    detrain_part = jnp.sum(detrain_share, axis=0)
    adjoint = adjoint_field
    for position in range(step_count):
        step_now = step_count - 1 - position
        adjoint = adjoint + forcing_grid[step_now][None]
        partial_sum = jnp.sum(detrain_share[None] * adjoint, axis=1)
        if position == 0:
            reduced = lev_sum(
                jnp.concatenate([partial_sum, detrain_part[None]], axis=0), 0
            )
            column_sum, total_detrain = reduced[:tracers], reduced[tracers]
        else:
            column_sum = lev_sum(partial_sum, 1)
        adjoint = (1.0 - mix_fraction)[None] * adjoint + mix_fraction[None] * (
            column_sum / total_detrain
        )[:, None]
        planes = tracers * lev_dev
        west_halo, east_halo, north_halo, south_halo = halo_swap(
            adjoint[:, :, :, -1].reshape(planes, lat_rows),
            adjoint[:, :, :, 0].reshape(planes, lat_rows),
            adjoint[:, :, -1, :].reshape(planes, lon_cols),
            adjoint[:, :, 0, :].reshape(planes, lon_cols),
            2 + position,
        )
        east_side = jnp.concatenate(
            [adjoint[:, :, :, 1:], east_halo.reshape(tracers, lev_dev, lat_rows, 1)], axis=3
        )
        west_side = jnp.concatenate(
            [west_halo.reshape(tracers, lev_dev, lat_rows, 1), adjoint[:, :, :, :-1]], axis=3
        )
        north_side = jnp.concatenate(
            [adjoint[:, :, 1:, :], north_halo.reshape(tracers, lev_dev, 1, lon_cols)], axis=2
        )
        south_side = jnp.concatenate(
            [south_halo.reshape(tracers, lev_dev, 1, lon_cols), adjoint[:, :, :-1, :]], axis=2
        )
        adjoint = (
            adjoint
            + upwind_east * (east_side - adjoint)
            + upwind_west * (west_side - adjoint)
            + upwind_north * (north_side - adjoint)
            + upwind_south * (south_side - adjoint)
        )
    return adjoint


def solution(mesh):
    return jax.shard_map(
        on_device,
        mesh=mesh,
        in_specs=(
            P(None, "lev", "lat", "lon"),
            P("lev", "lat", "lon"),
            P("lev", "lat", "lon"),
            P("lev", "lon"),
            P("lev", "lat", "lon"),
            P("lev", "lat", "lon"),
            P(None, ("lon", "lat"), None),
            P(None, ("lon", "lat")),
            P(None, ("lon", "lat")),
            P(None, "lev", ("lon", "lat")),
        ),
        out_specs=P(None, "lev", "lat", "lon"),
        check_vma=False,
    )
```

```python
import functools

import jax
import jax.numpy as jnp
from jax import lax
from jax.experimental import pallas as pl
from jax.experimental.pallas import tpu as pltpu
from jax.sharding import PartitionSpec as P

MESH = pl.DeviceIdType.MESH


def lev_sum_body(n, part_ref, out_ref, slots, send_sem, recv_sem):
    me = lax.axis_index("lev")
    barrier = pltpu.get_barrier_semaphore()
    for d in range(1, n):
        pl.semaphore_signal(
            barrier, inc=1, device_id={"lev": lax.rem(me + d, n)}, device_id_type=MESH
        )
    pl.semaphore_wait(barrier, n - 1)
    sends = []
    for d in range(1, n):
        copy = pltpu.make_async_remote_copy(
            src_ref=part_ref,
            dst_ref=slots.at[me],
            send_sem=send_sem.at[d - 1],
            recv_sem=recv_sem.at[me],
            device_id={"lev": lax.rem(me + d, n)},
            device_id_type=MESH,
        )
        copy.start()
        sends.append(copy)
    slots[me] = part_ref[...]
    for d in range(1, n):
        sender = lax.rem(me + n - d, n)
        pltpu.make_async_remote_copy(
            src_ref=part_ref,
            dst_ref=slots.at[sender],
            send_sem=send_sem.at[d - 1],
            recv_sem=recv_sem.at[sender],
            device_id={"lev": sender},
            device_id_type=MESH,
        ).wait_recv()
    for copy in sends:
        copy.wait_send()
    total = slots[0]
    for s in range(1, n):
        total = total + slots[s]
    out_ref[...] = total


def halo_body(lon_n, lat_n, col_last, col_first, row_last, row_first,
              west_out, east_out, north_out, south_out, cols, rows, send_sem, col_sem, row_sem):
    lon = lax.axis_index("lon")
    lat = lax.axis_index("lat")
    half = lon_n // 2
    top = lat // (lat_n - 1)
    inner = (lat + lat_n - 1) // lat_n
    east = {"lon": lax.rem(lon + 1, lon_n)}
    west = {"lon": lax.rem(lon + lon_n - 1, lon_n)}
    up = {"lon": lax.rem(lon + half * top, lon_n), "lat": lat + 1 - top}
    down = {"lon": lax.rem(lon + half * (1 - inner), lon_n), "lat": lat - inner}
    up_slot = 1 - top
    down_slot = 1 - inner
    barrier = pltpu.get_barrier_semaphore()
    for peer in (east, west, up, down):
        pl.semaphore_signal(barrier, inc=1, device_id=peer, device_id_type=MESH)
    pl.semaphore_wait(barrier, 4)
    plan = (
        (col_last, cols.at[0], col_sem.at[0], east),
        (col_first, cols.at[1], col_sem.at[1], west),
        (row_last, rows.at[up_slot], row_sem.at[up_slot], up),
        (row_first, rows.at[down_slot], row_sem.at[down_slot], down),
    )
    sends = []
    for i, (src, dst, sem, peer) in enumerate(plan):
        copy = pltpu.make_async_remote_copy(
            src_ref=src, dst_ref=dst, send_sem=send_sem.at[i], recv_sem=sem,
            device_id=peer, device_id_type=MESH,
        )
        copy.start()
        sends.append(copy)
    arrivals = (
        (col_last, cols.at[0], col_sem.at[0]),
        (col_first, cols.at[1], col_sem.at[1]),
        (row_last, rows.at[0], row_sem.at[0]),
        (row_first, rows.at[1], row_sem.at[1]),
    )
    for src, dst, sem in arrivals:
        pltpu.make_async_remote_copy(
            src_ref=src, dst_ref=dst, send_sem=send_sem.at[0], recv_sem=sem,
            device_id=east, device_id_type=MESH,
        ).wait_recv()
    for copy in sends:
        copy.wait_send()
    west_out[...] = cols[0]
    east_out[...] = cols[1]
    north_out[...] = rows[0]
    south_out[...] = rows[1]


def halo_swap(col_last, col_first, row_last, row_first, collective_id):
    lon_n, lat_n = lax.axis_size("lon"), lax.axis_size("lat")
    vmem = pl.BlockSpec(memory_space=pltpu.VMEM)
    return pl.pallas_call(
        functools.partial(halo_body, lon_n, lat_n),
        out_shape=(
            jax.ShapeDtypeStruct(col_last.shape, col_last.dtype),
            jax.ShapeDtypeStruct(col_last.shape, col_last.dtype),
            jax.ShapeDtypeStruct(row_last.shape, row_last.dtype),
            jax.ShapeDtypeStruct(row_last.shape, row_last.dtype),
        ),
        in_specs=[vmem] * 4,
        out_specs=(vmem,) * 4,
        scratch_shapes=[
            pltpu.VMEM((2,) + col_last.shape, col_last.dtype),
            pltpu.VMEM((2,) + row_last.shape, row_last.dtype),
            pltpu.SemaphoreType.DMA((4,)),
            pltpu.SemaphoreType.DMA((2,)),
            pltpu.SemaphoreType.DMA((2,)),
        ],
        compiler_params=pltpu.CompilerParams(
            collective_id=collective_id, has_side_effects=True
        ),
    )(col_last, col_first, row_last, row_first)


def lev_sum(x, collective_id):
    n = lax.axis_size("lev")
    return pl.pallas_call(
        functools.partial(lev_sum_body, n),
        out_shape=jax.ShapeDtypeStruct(x.shape, x.dtype),
        in_specs=[pl.BlockSpec(memory_space=pltpu.VMEM)],
        out_specs=pl.BlockSpec(memory_space=pltpu.VMEM),
        scratch_shapes=[
            pltpu.VMEM((n,) + x.shape, x.dtype),
            pltpu.SemaphoreType.DMA((n - 1,)),
            pltpu.SemaphoreType.DMA((n,)),
        ],
        compiler_params=pltpu.CompilerParams(
            collective_id=collective_id, has_side_effects=True
        ),
    )(x)


def from_behind(value, axis, steps):
    count = lax.axis_size(axis)
    pairs = [(source, (source + steps) % count) for source in range(count)]
    return lax.ppermute(value, axis, pairs)


def from_behind_2(block, axis, distance):
    devices = range(lax.axis_size(axis))
    route = [(i - distance, i) for i in devices if i - distance in devices]
    return lax.ppermute(block, axis, route)


def extended(x, sides, width, wrap):
    for axis, dim in sides:
        size, length = (lax.axis_size(axis), x.shape[dim])
        up = [(i, (i + 1) % size) for i in range(size if wrap else size - 1)]
        down = [(j, i) for i, j in up]
        last = lax.slice_in_dim(x, length - width, length, axis=dim)
        initial = lax.slice_in_dim(x, 0, width, axis=dim)
        before = lax.ppermute(last, axis, up)
        after = lax.ppermute(initial, axis, down)
        x = jnp.concatenate([before, x, after], axis=dim)
    return x


def mix_sum(partial_sum):
    return lax.psum(partial_sum, "lev")


def on_device(
    adjoint_field,
    east_courant,
    north_courant,
    pole_courant,
    mix_fraction,
    detrain_share,
    sounding_owner,
    sounding_cell,
    sounding_count,
    sounding_forcing,
):
    lon_count = lax.axis_size("lon")
    lat_count = lax.axis_size("lat")
    lat_place = lax.axis_index("lat")
    owner_self = lax.axis_index("lon") * lat_count + lat_place
    tracers, lev_dev, lat_rows, lon_cols = adjoint_field.shape
    step_count = sounding_forcing.shape[0]
    slot_count = sounding_forcing.shape[2]
    grid_cells = lat_rows * lon_cols
    owner_count = lon_count * lat_count
    cap = 4
    live_slots = jnp.arange(slot_count, dtype=jnp.int32)[None, :] < sounding_count
    values = jnp.where(live_slots[:, None, :], sounding_forcing, 0.0)
    owner_ids = sounding_owner[:, :, 0]
    slot_iota = jnp.arange(slot_count, dtype=jnp.int32)
    earlier = slot_iota[None, :, None] < slot_iota[None, None, :]
    same_owner = owner_ids[:, :, None] == owner_ids[:, None, :]
    rank = jnp.sum(jnp.logical_and(earlier, same_owner), axis=1, dtype=jnp.int32)
    position = owner_ids * cap + rank
    bucket_iota = jnp.arange(owner_count * cap, dtype=jnp.int32)
    chosen = position[:, :, None] == bucket_iota[None, None, :]
    bucket_values = jnp.sum(
        jnp.where(chosen[:, None, :, :], values[:, :, :, None], 0.0), axis=2
    )
    bucket_cell = jnp.max(
        jnp.where(chosen, sounding_cell[:, :, None] + 1, 0), axis=1
    ).astype(jnp.float32) - 1.0
    packed = jnp.concatenate([bucket_values, bucket_cell[:, None, :]], axis=1)
    packed = packed.reshape(step_count, lev_dev + 1, owner_count, cap)
    packed = jnp.transpose(packed, (2, 0, 1, 3))
    arrived = lax.all_to_all(packed, ("lon", "lat"), 0, 0, tiled=True)
    arrived = jnp.transpose(arrived, (1, 2, 0, 3)).reshape(
        step_count, lev_dev + 1, owner_count * cap
    )
    cell_iota = jnp.arange(grid_cells, dtype=jnp.int32).astype(jnp.float32)
    hit = (arrived[:, lev_dev, :, None] == cell_iota[None, None, :]).astype(jnp.float32)
    forcing_grid = jnp.einsum(
        "tke,tec->tkc", arrived[:, :lev_dev, :], hit, precision=lax.Precision.HIGHEST
    )
    forcing_grid = forcing_grid.reshape(step_count, lev_dev, lat_rows, lon_cols)
    row_index = jnp.arange(lat_rows, dtype=jnp.int32)[None, :, None]
    at_top = jnp.logical_and(lat_place == lat_count - 1, row_index == lat_rows - 1)
    at_bottom = jnp.logical_and(lat_place == 0, row_index == 0)
    upwind_east = jnp.maximum(east_courant, 0.0)
    detrain_part = jnp.sum(detrain_share, axis=0)
    adjoint = adjoint_field
    for position in range(step_count):
        step_now = step_count - 1 - position
        adjoint = adjoint + forcing_grid[step_now][None]
        partial_sum = jnp.sum(detrain_share[None] * adjoint, axis=1)
        if position == 0:
            reduced = lev_sum(
                jnp.concatenate([partial_sum, detrain_part[None]], axis=0), 0
            )
            column_sum, total_detrain = reduced[:tracers], reduced[tracers]
        else:
            column_sum = lev_sum(partial_sum, 1)
        adjoint = (1.0 - mix_fraction)[None] * adjoint + mix_fraction[None] * (
            column_sum / total_detrain
        )[:, None]
        planes = tracers * lev_dev
        col_last = adjoint[:, :, :, -1].reshape(planes, lat_rows)
        col_first = adjoint[:, :, :, 0].reshape(planes, lat_rows)
        row_last = adjoint[:, :, -1, :].reshape(planes, lon_cols)
        row_first = adjoint[:, :, 0, :].reshape(planes, lon_cols)
        if position == 0:
            col_last = jnp.concatenate([col_last, east_courant[:, :, -1]], axis=0)
            col_first = jnp.concatenate([col_first, east_courant[:, :, 0]], axis=0)
            row_last = jnp.concatenate([row_last, north_courant[:, -1, :]], axis=0)
            row_first = jnp.concatenate([row_first, pole_courant], axis=0)
        west_halo, east_halo, north_halo, south_halo = halo_swap(
            col_last, col_first, row_last, row_first, 2 + position
        )
        if position == 0:
            west_wind = jnp.concatenate(
                [west_halo[planes:, :, None], east_courant[:, :, :-1]], axis=2
            )
            partner_top = north_halo[planes:]
            south_wind = jnp.concatenate(
                [south_halo[planes:, None, :], north_courant[:, :-1, :]], axis=1
            )
            partner_pole = south_halo[planes:]
            upwind_west = -jnp.minimum(west_wind, 0.0)
            upwind_north = jnp.maximum(north_courant, 0.0) + jnp.where(
                at_top, -jnp.minimum(partner_top, 0.0)[:, None, :], 0.0
            )
            upwind_south = jnp.where(
                at_bottom,
                (jnp.maximum(pole_courant, 0.0) - jnp.minimum(partner_pole, 0.0))[:, None, :],
                -jnp.minimum(south_wind, 0.0),
            )
            west_halo, east_halo = west_halo[:planes], east_halo[:planes]
            north_halo, south_halo = north_halo[:planes], south_halo[:planes]
        east_side = jnp.concatenate(
            [adjoint[:, :, :, 1:], east_halo.reshape(tracers, lev_dev, lat_rows, 1)], axis=3
        )
        west_side = jnp.concatenate(
            [west_halo.reshape(tracers, lev_dev, lat_rows, 1), adjoint[:, :, :, :-1]], axis=3
        )
        north_side = jnp.concatenate(
            [adjoint[:, :, 1:, :], north_halo.reshape(tracers, lev_dev, 1, lon_cols)], axis=2
        )
        south_side = jnp.concatenate(
            [south_halo.reshape(tracers, lev_dev, 1, lon_cols), adjoint[:, :, :-1, :]], axis=2
        )
        adjoint = (
            adjoint
            + upwind_east * (east_side - adjoint)
            + upwind_west * (west_side - adjoint)
            + upwind_north * (north_side - adjoint)
            + upwind_south * (south_side - adjoint)
        )
    return adjoint


def solution(mesh):
    return jax.shard_map(
        on_device,
        mesh=mesh,
        in_specs=(
            P(None, "lev", "lat", "lon"),
            P("lev", "lat", "lon"),
            P("lev", "lat", "lon"),
            P("lev", "lon"),
            P("lev", "lat", "lon"),
            P("lev", "lat", "lon"),
            P(None, ("lon", "lat"), None),
            P(None, ("lon", "lat")),
            P(None, ("lon", "lat")),
            P(None, "lev", ("lon", "lat")),
        ),
        out_specs=P(None, "lev", "lat", "lon"),
        check_vma=False,
    )
```

```python
import functools

import jax
import jax.numpy as jnp
from jax import lax
from jax.experimental import pallas as pl
from jax.experimental.pallas import tpu as pltpu
from jax.sharding import PartitionSpec as P

MESH = pl.DeviceIdType.MESH


def lev_sum_body(n, part_ref, out_ref, slots, send_sem, recv_sem):
    me = lax.axis_index("lev")
    barrier = pltpu.get_barrier_semaphore()
    for d in range(1, n):
        pl.semaphore_signal(
            barrier, inc=1, device_id={"lev": lax.rem(me + d, n)}, device_id_type=MESH
        )
    pl.semaphore_wait(barrier, n - 1)
    sends = []
    for d in range(1, n):
        copy = pltpu.make_async_remote_copy(
            src_ref=part_ref,
            dst_ref=slots.at[me],
            send_sem=send_sem.at[d - 1],
            recv_sem=recv_sem.at[me],
            device_id={"lev": lax.rem(me + d, n)},
            device_id_type=MESH,
        )
        copy.start()
        sends.append(copy)
    slots[me] = part_ref[...]
    for d in range(1, n):
        sender = lax.rem(me + n - d, n)
        pltpu.make_async_remote_copy(
            src_ref=part_ref,
            dst_ref=slots.at[sender],
            send_sem=send_sem.at[d - 1],
            recv_sem=recv_sem.at[sender],
            device_id={"lev": sender},
            device_id_type=MESH,
        ).wait_recv()
    for copy in sends:
        copy.wait_send()
    total = slots[0]
    for s in range(1, n):
        total = total + slots[s]
    out_ref[...] = total


def halo_body(lon_n, lat_n, col_last, col_first, row_last, row_first,
              west_out, east_out, north_out, south_out, cols, rows, send_sem, col_sem, row_sem):
    lon = lax.axis_index("lon")
    lat = lax.axis_index("lat")
    half = lon_n // 2
    top = lat // (lat_n - 1)
    inner = (lat + lat_n - 1) // lat_n
    east = {"lon": lax.rem(lon + 1, lon_n)}
    west = {"lon": lax.rem(lon + lon_n - 1, lon_n)}
    up = {"lon": lax.rem(lon + half * top, lon_n), "lat": lat + 1 - top}
    down = {"lon": lax.rem(lon + half * (1 - inner), lon_n), "lat": lat - inner}
    up_slot = 1 - top
    down_slot = 1 - inner
    barrier = pltpu.get_barrier_semaphore()
    for peer in (east, west, up, down):
        pl.semaphore_signal(barrier, inc=1, device_id=peer, device_id_type=MESH)
    pl.semaphore_wait(barrier, 4)
    plan = (
        (col_last, cols.at[0], col_sem.at[0], east),
        (col_first, cols.at[1], col_sem.at[1], west),
        (row_last, rows.at[up_slot], row_sem.at[up_slot], up),
        (row_first, rows.at[down_slot], row_sem.at[down_slot], down),
    )
    sends = []
    for i, (src, dst, sem, peer) in enumerate(plan):
        copy = pltpu.make_async_remote_copy(
            src_ref=src, dst_ref=dst, send_sem=send_sem.at[i], recv_sem=sem,
            device_id=peer, device_id_type=MESH,
        )
        copy.start()
        sends.append(copy)
    arrivals = (
        (col_last, cols.at[0], col_sem.at[0]),
        (col_first, cols.at[1], col_sem.at[1]),
        (row_last, rows.at[0], row_sem.at[0]),
        (row_first, rows.at[1], row_sem.at[1]),
    )
    for src, dst, sem in arrivals:
        pltpu.make_async_remote_copy(
            src_ref=src, dst_ref=dst, send_sem=send_sem.at[0], recv_sem=sem,
            device_id=east, device_id_type=MESH,
        ).wait_recv()
    for copy in sends:
        copy.wait_send()
    west_out[...] = cols[0]
    east_out[...] = cols[1]
    north_out[...] = rows[0]
    south_out[...] = rows[1]


def halo_swap(col_last, col_first, row_last, row_first, collective_id):
    lon_n, lat_n = lax.axis_size("lon"), lax.axis_size("lat")
    vmem = pl.BlockSpec(memory_space=pltpu.VMEM)
    return pl.pallas_call(
        functools.partial(halo_body, lon_n, lat_n),
        out_shape=(
            jax.ShapeDtypeStruct(col_last.shape, col_last.dtype),
            jax.ShapeDtypeStruct(col_last.shape, col_last.dtype),
            jax.ShapeDtypeStruct(row_last.shape, row_last.dtype),
            jax.ShapeDtypeStruct(row_last.shape, row_last.dtype),
        ),
        in_specs=[vmem] * 4,
        out_specs=(vmem,) * 4,
        scratch_shapes=[
            pltpu.VMEM((2,) + col_last.shape, col_last.dtype),
            pltpu.VMEM((2,) + row_last.shape, row_last.dtype),
            pltpu.SemaphoreType.DMA((4,)),
            pltpu.SemaphoreType.DMA((2,)),
            pltpu.SemaphoreType.DMA((2,)),
        ],
        compiler_params=pltpu.CompilerParams(
            collective_id=collective_id, has_side_effects=True
        ),
    )(col_last, col_first, row_last, row_first)


def exchange_body(lev_n, owners, lat_n, rows_ref, part_ref, rows_out, sum_out,
                  got, slots, row_send, row_recv, lev_send, lev_recv):
    lat = lax.axis_index("lat")
    lev = lax.axis_index("lev")
    me = lax.axis_index("lon") * lat_n + lat

    def place(peer):
        return {"lon": peer // lat_n, "lat": lax.rem(peer, lat_n)}

    barrier = pltpu.get_barrier_semaphore()

    def greet(d, carry):
        peer = lax.rem(me + d, owners)
        pl.semaphore_signal(barrier, inc=1, device_id=place(peer), device_id_type=MESH)
        return carry

    lax.fori_loop(1, owners, greet, 0)
    for d in range(1, lev_n):
        pl.semaphore_signal(
            barrier, inc=1, device_id={"lev": lax.rem(lev + d, lev_n)}, device_id_type=MESH
        )
    pl.semaphore_wait(barrier, owners - 1 + lev_n - 1)
    for d in range(1, lev_n):
        pltpu.make_async_remote_copy(
            src_ref=part_ref,
            dst_ref=slots.at[lev],
            send_sem=lev_send.at[d - 1],
            recv_sem=lev_recv.at[lev],
            device_id={"lev": lax.rem(lev + d, lev_n)},
            device_id_type=MESH,
        ).start()

    def row_copy(peer, target):
        return pltpu.make_async_remote_copy(
            src_ref=rows_ref.at[pl.ds(peer, 1)],
            dst_ref=got.at[pl.ds(target, 1)],
            send_sem=row_send.at[peer],
            recv_sem=row_recv.at[target],
            device_id=place(peer),
            device_id_type=MESH,
        )

    def send(d, carry):
        row_copy(lax.rem(me + d, owners), me).start()
        return carry

    lax.fori_loop(1, owners, send, 0)
    got[pl.ds(me, 1), :] = rows_ref[pl.ds(me, 1), :]
    slots[lev] = part_ref[...]

    def finish(d, carry):
        source = lax.rem(me + owners - d, owners)
        row_copy(lax.rem(me + d, owners), me).wait_send()
        row_copy(source, source).wait_recv()
        return carry

    lax.fori_loop(1, owners, finish, 0)
    for d in range(1, lev_n):
        sender = lax.rem(lev + lev_n - d, lev_n)
        copy = pltpu.make_async_remote_copy(
            src_ref=part_ref,
            dst_ref=slots.at[sender],
            send_sem=lev_send.at[d - 1],
            recv_sem=lev_recv.at[sender],
            device_id={"lev": sender},
            device_id_type=MESH,
        )
        copy.wait_recv()
        copy.wait_send()
    total = slots[0]
    for s in range(1, lev_n):
        total = total + slots[s]
    sum_out[...] = total
    rows_out[...] = got[...]


def exchange(rows, part, collective_id):
    lev_n = lax.axis_size("lev")
    lat_n = lax.axis_size("lat")
    owners = lax.axis_size("lon") * lat_n
    vmem = pl.BlockSpec(memory_space=pltpu.VMEM)
    return pl.pallas_call(
        functools.partial(exchange_body, lev_n, owners, lat_n),
        out_shape=(
            jax.ShapeDtypeStruct(rows.shape, rows.dtype),
            jax.ShapeDtypeStruct(part.shape, part.dtype),
        ),
        in_specs=[vmem, vmem],
        out_specs=(vmem, vmem),
        scratch_shapes=[
            pltpu.VMEM(rows.shape, rows.dtype),
            pltpu.VMEM((lev_n,) + part.shape, part.dtype),
            pltpu.SemaphoreType.DMA((owners,)),
            pltpu.SemaphoreType.DMA((owners,)),
            pltpu.SemaphoreType.DMA((lev_n - 1,)),
            pltpu.SemaphoreType.DMA((lev_n,)),
        ],
        compiler_params=pltpu.CompilerParams(
            collective_id=collective_id, has_side_effects=True
        ),
    )(rows, part)


def lev_sum(x, collective_id):
    n = lax.axis_size("lev")
    return pl.pallas_call(
        functools.partial(lev_sum_body, n),
        out_shape=jax.ShapeDtypeStruct(x.shape, x.dtype),
        in_specs=[pl.BlockSpec(memory_space=pltpu.VMEM)],
        out_specs=pl.BlockSpec(memory_space=pltpu.VMEM),
        scratch_shapes=[
            pltpu.VMEM((n,) + x.shape, x.dtype),
            pltpu.SemaphoreType.DMA((n - 1,)),
            pltpu.SemaphoreType.DMA((n,)),
        ],
        compiler_params=pltpu.CompilerParams(
            collective_id=collective_id, has_side_effects=True
        ),
        cost_estimate=pl.CostEstimate(
            flops=n * x.size, bytes_accessed=(2 * n + 2) * x.size * 4, transcendentals=0
        ),
    )(x)


def from_behind(value, axis, steps):
    count = lax.axis_size(axis)
    pairs = [(source, (source + steps) % count) for source in range(count)]
    return lax.ppermute(value, axis, pairs)


def from_behind_2(block, axis, distance):
    devices = range(lax.axis_size(axis))
    route = [(i - distance, i) for i in devices if i - distance in devices]
    return lax.ppermute(block, axis, route)


def extended(x, sides, width, wrap):
    for axis, dim in sides:
        size, length = (lax.axis_size(axis), x.shape[dim])
        up = [(i, (i + 1) % size) for i in range(size if wrap else size - 1)]
        down = [(j, i) for i, j in up]
        last = lax.slice_in_dim(x, length - width, length, axis=dim)
        initial = lax.slice_in_dim(x, 0, width, axis=dim)
        before = lax.ppermute(last, axis, up)
        after = lax.ppermute(initial, axis, down)
        x = jnp.concatenate([before, x, after], axis=dim)
    return x


def mix_sum(partial_sum):
    return lax.psum(partial_sum, "lev")


def on_device(
    adjoint_field,
    east_courant,
    north_courant,
    pole_courant,
    mix_fraction,
    detrain_share,
    sounding_owner,
    sounding_cell,
    sounding_count,
    sounding_forcing,
):
    lon_count = lax.axis_size("lon")
    lat_count = lax.axis_size("lat")
    lat_place = lax.axis_index("lat")
    owner_self = lax.axis_index("lon") * lat_count + lat_place
    tracers, lev_dev, lat_rows, lon_cols = adjoint_field.shape
    step_count = sounding_forcing.shape[0]
    slot_count = sounding_forcing.shape[2]
    grid_cells = lat_rows * lon_cols
    detrain_part = jnp.sum(detrain_share, axis=0)
    owner_count = lon_count * lat_count
    cap = 4
    live_slots = jnp.arange(slot_count, dtype=jnp.int32)[None, :] < sounding_count
    values = jnp.where(live_slots[:, None, :], sounding_forcing, 0.0)
    owner_ids = sounding_owner[:, :, 0]
    slot_iota = jnp.arange(slot_count, dtype=jnp.int32)
    earlier = slot_iota[None, :, None] < slot_iota[None, None, :]
    same_owner = owner_ids[:, :, None] == owner_ids[:, None, :]
    rank = jnp.sum(jnp.logical_and(earlier, same_owner), axis=1, dtype=jnp.int32)
    position = owner_ids * cap + rank
    bucket_iota = jnp.arange(owner_count * cap, dtype=jnp.int32)
    chosen = position[:, :, None] == bucket_iota[None, None, :]
    bucket_values = jnp.sum(
        jnp.where(chosen[:, None, :, :], values[:, :, :, None], 0.0), axis=2
    )
    bucket_cell = jnp.max(
        jnp.where(chosen, sounding_cell[:, :, None] + 1, 0), axis=1
    ).astype(jnp.float32) - 1.0
    packed = jnp.concatenate([bucket_values, bucket_cell[:, None, :]], axis=1)
    packed = packed.reshape(step_count, lev_dev + 1, owner_count, cap)
    packed = jnp.transpose(packed, (2, 0, 1, 3))
    row_width = step_count * (lev_dev + 1) * cap
    rows = jnp.pad(packed.reshape(owner_count, row_width), ((0, 0), (0, 128 - row_width)))
    early_part = jnp.concatenate(
        [jnp.sum(detrain_share[None] * adjoint_field, axis=1), detrain_part[None]], axis=0
    )
    arrived, early = exchange(rows, early_part, 0)
    arrived = arrived[:, :row_width].reshape(owner_count, step_count, lev_dev + 1, cap)
    arrived = jnp.transpose(arrived, (1, 2, 0, 3)).reshape(
        step_count, lev_dev + 1, owner_count * cap
    )
    cell_iota = jnp.arange(grid_cells, dtype=jnp.int32).astype(jnp.float32)
    hit = (arrived[:, lev_dev, :, None] == cell_iota[None, None, :]).astype(jnp.float32)
    forcing_grid = jnp.einsum(
        "tke,tec->tkc", arrived[:, :lev_dev, :], hit, precision=lax.Precision.HIGHEST
    )
    forcing_grid = forcing_grid.reshape(step_count, lev_dev, lat_rows, lon_cols)
    row_index = jnp.arange(lat_rows, dtype=jnp.int32)[None, :, None]
    at_top = jnp.logical_and(lat_place == lat_count - 1, row_index == lat_rows - 1)
    at_bottom = jnp.logical_and(lat_place == 0, row_index == 0)
    upwind_east = jnp.maximum(east_courant, 0.0)
    forcing_part = jnp.sum(detrain_share * forcing_grid[step_count - 1], axis=0)
    forcing_sum = lev_sum(forcing_part[None], 4)[0]
    adjoint = adjoint_field
    for position in range(step_count):
        step_now = step_count - 1 - position
        adjoint = adjoint + forcing_grid[step_now][None]
        if position == 0:
            column_sum = early[:tracers] + forcing_sum[None]
            total_detrain = early[tracers]
        else:
            partial_sum = jnp.sum(detrain_share[None] * adjoint, axis=1)
            column_sum = lev_sum(partial_sum, 1)
        adjoint = (1.0 - mix_fraction)[None] * adjoint + mix_fraction[None] * (
            column_sum / total_detrain
        )[:, None]
        planes = tracers * lev_dev
        col_last = adjoint[:, :, :, -1].reshape(planes, lat_rows)
        col_first = adjoint[:, :, :, 0].reshape(planes, lat_rows)
        row_last = adjoint[:, :, -1, :].reshape(planes, lon_cols)
        row_first = adjoint[:, :, 0, :].reshape(planes, lon_cols)
        if position == 0:
            col_last = jnp.concatenate([col_last, east_courant[:, :, -1]], axis=0)
            col_first = jnp.concatenate([col_first, east_courant[:, :, 0]], axis=0)
            row_last = jnp.concatenate([row_last, north_courant[:, -1, :]], axis=0)
            row_first = jnp.concatenate([row_first, pole_courant], axis=0)
        west_halo, east_halo, north_halo, south_halo = halo_swap(
            col_last, col_first, row_last, row_first, 2 + position
        )
        if position == 0:
            west_wind = jnp.concatenate(
                [west_halo[planes:, :, None], east_courant[:, :, :-1]], axis=2
            )
            partner_top = north_halo[planes:]
            south_wind = jnp.concatenate(
                [south_halo[planes:, None, :], north_courant[:, :-1, :]], axis=1
            )
            partner_pole = south_halo[planes:]
            upwind_west = -jnp.minimum(west_wind, 0.0)
            upwind_north = jnp.maximum(north_courant, 0.0) + jnp.where(
                at_top, -jnp.minimum(partner_top, 0.0)[:, None, :], 0.0
            )
            upwind_south = jnp.where(
                at_bottom,
                (jnp.maximum(pole_courant, 0.0) - jnp.minimum(partner_pole, 0.0))[:, None, :],
                -jnp.minimum(south_wind, 0.0),
            )
            west_halo, east_halo = west_halo[:planes], east_halo[:planes]
            north_halo, south_halo = north_halo[:planes], south_halo[:planes]
        east_side = jnp.concatenate(
            [adjoint[:, :, :, 1:], east_halo.reshape(tracers, lev_dev, lat_rows, 1)], axis=3
        )
        west_side = jnp.concatenate(
            [west_halo.reshape(tracers, lev_dev, lat_rows, 1), adjoint[:, :, :, :-1]], axis=3
        )
        north_side = jnp.concatenate(
            [adjoint[:, :, 1:, :], north_halo.reshape(tracers, lev_dev, 1, lon_cols)], axis=2
        )
        south_side = jnp.concatenate(
            [south_halo.reshape(tracers, lev_dev, 1, lon_cols), adjoint[:, :, :-1, :]], axis=2
        )
        adjoint = (
            adjoint
            + upwind_east * (east_side - adjoint)
            + upwind_west * (west_side - adjoint)
            + upwind_north * (north_side - adjoint)
            + upwind_south * (south_side - adjoint)
        )
    return adjoint


def solution(mesh):
    return jax.shard_map(
        on_device,
        mesh=mesh,
        in_specs=(
            P(None, "lev", "lat", "lon"),
            P("lev", "lat", "lon"),
            P("lev", "lat", "lon"),
            P("lev", "lon"),
            P("lev", "lat", "lon"),
            P("lev", "lat", "lon"),
            P(None, ("lon", "lat"), None),
            P(None, ("lon", "lat")),
            P(None, ("lon", "lat")),
            P(None, "lev", ("lon", "lat")),
        ),
        out_specs=P(None, "lev", "lat", "lon"),
        check_vma=False,
    )
```

```python
import functools

import jax
import jax.numpy as jnp
from jax import lax
from jax.experimental import pallas as pl
from jax.experimental.pallas import tpu as pltpu
from jax.sharding import PartitionSpec as P

MESH = pl.DeviceIdType.MESH


def lev_sum_body(n, part_ref, out_ref, pieces, reduced, sends, recvs, gsends, grecvs):
    lev = lax.axis_index("lev")
    barrier = pltpu.get_barrier_semaphore()
    for d in range(1, n):
        pl.semaphore_signal(
            barrier, inc=1, device_id={"lev": lax.rem(lev + d, n)}, device_id_type=MESH
        )
    pl.semaphore_wait(barrier, n - 1)
    scatter_start(n, part_ref, pieces, sends, recvs)
    scatter_finish_gather_start(n, part_ref, pieces, reduced, sends, recvs, gsends, grecvs)
    gather_finish(n, out_ref, reduced, gsends, grecvs)


def halo_body(lon_n, lat_n, col_last, col_first, row_last, row_first,
              west_out, east_out, north_out, south_out, cols, rows, send_sem, col_sem, row_sem):
    lon = lax.axis_index("lon")
    lat = lax.axis_index("lat")
    half = lon_n // 2
    top = lat // (lat_n - 1)
    inner = (lat + lat_n - 1) // lat_n
    east = {"lon": lax.rem(lon + 1, lon_n)}
    west = {"lon": lax.rem(lon + lon_n - 1, lon_n)}
    up = {"lon": lax.rem(lon + half * top, lon_n), "lat": lat + 1 - top}
    down = {"lon": lax.rem(lon + half * (1 - inner), lon_n), "lat": lat - inner}
    up_slot = 1 - top
    down_slot = 1 - inner
    barrier = pltpu.get_barrier_semaphore()
    for peer in (east, west, up, down):
        pl.semaphore_signal(barrier, inc=1, device_id=peer, device_id_type=MESH)
    pl.semaphore_wait(barrier, 4)
    plan = (
        (col_last, cols.at[0], col_sem.at[0], east),
        (col_first, cols.at[1], col_sem.at[1], west),
        (row_last, rows.at[up_slot], row_sem.at[up_slot], up),
        (row_first, rows.at[down_slot], row_sem.at[down_slot], down),
    )
    sends = []
    for i, (src, dst, sem, peer) in enumerate(plan):
        copy = pltpu.make_async_remote_copy(
            src_ref=src, dst_ref=dst, send_sem=send_sem.at[i], recv_sem=sem,
            device_id=peer, device_id_type=MESH,
        )
        copy.start()
        sends.append(copy)
    arrivals = (
        (col_last, cols.at[0], col_sem.at[0]),
        (col_first, cols.at[1], col_sem.at[1]),
        (row_last, rows.at[0], row_sem.at[0]),
        (row_first, rows.at[1], row_sem.at[1]),
    )
    for src, dst, sem in arrivals:
        pltpu.make_async_remote_copy(
            src_ref=src, dst_ref=dst, send_sem=send_sem.at[0], recv_sem=sem,
            device_id=east, device_id_type=MESH,
        ).wait_recv()
    for copy in sends:
        copy.wait_send()
    west_out[...] = cols[0]
    east_out[...] = cols[1]
    north_out[...] = rows[0]
    south_out[...] = rows[1]


def halo_swap(col_last, col_first, row_last, row_first, collective_id):
    lon_n, lat_n = lax.axis_size("lon"), lax.axis_size("lat")
    vmem = pl.BlockSpec(memory_space=pltpu.VMEM)
    return pl.pallas_call(
        functools.partial(halo_body, lon_n, lat_n),
        out_shape=(
            jax.ShapeDtypeStruct(col_last.shape, col_last.dtype),
            jax.ShapeDtypeStruct(col_last.shape, col_last.dtype),
            jax.ShapeDtypeStruct(row_last.shape, row_last.dtype),
            jax.ShapeDtypeStruct(row_last.shape, row_last.dtype),
        ),
        in_specs=[vmem] * 4,
        out_specs=(vmem,) * 4,
        scratch_shapes=[
            pltpu.VMEM((2,) + col_last.shape, col_last.dtype),
            pltpu.VMEM((2,) + row_last.shape, row_last.dtype),
            pltpu.SemaphoreType.DMA((4,)),
            pltpu.SemaphoreType.DMA((2,)),
            pltpu.SemaphoreType.DMA((2,)),
        ],
        compiler_params=pltpu.CompilerParams(
            collective_id=collective_id, has_side_effects=True
        ),
    )(col_last, col_first, row_last, row_first)


def lev_copy(src, dst, send, recv, peer):
    return pltpu.make_async_remote_copy(
        src_ref=src, dst_ref=dst, send_sem=send, recv_sem=recv,
        device_id={"lev": peer}, device_id_type=MESH,
    )


def scatter_start(n, part_ref, pieces, sends, recvs):
    lev = lax.axis_index("lev")
    rows = part_ref.shape[1] // n
    for d in range(1, n):
        peer = lax.rem(lev + d, n)
        lev_copy(
            part_ref.at[:, pl.ds(pl.multiple_of(peer * rows, rows), rows), :],
            pieces.at[lev], sends.at[d - 1], recvs.at[lev], peer,
        ).start()
    pieces[lev] = part_ref[:, pl.ds(pl.multiple_of(lev * rows, rows), rows), :]


def scatter_finish_gather_start(n, part_ref, pieces, reduced, sends, recvs, gsends, grecvs):
    lev = lax.axis_index("lev")
    rows = part_ref.shape[1] // n
    for d in range(1, n):
        sender = lax.rem(lev + n - d, n)
        peer = lax.rem(lev + d, n)
        lev_copy(
            part_ref.at[:, pl.ds(0, rows), :], pieces.at[sender],
            sends.at[d - 1], recvs.at[sender], sender,
        ).wait_recv()
        lev_copy(
            part_ref.at[:, pl.ds(0, rows), :], pieces.at[sender],
            sends.at[d - 1], recvs.at[sender], peer,
        ).wait_send()
    total = pieces[0]
    for s in range(1, n):
        total = total + pieces[s]
    reduced[lev] = total
    for d in range(1, n):
        peer = lax.rem(lev + d, n)
        lev_copy(reduced.at[lev], reduced.at[lev], gsends.at[d - 1], grecvs.at[lev], peer).start()


def gather_finish(n, out_ref, reduced, gsends, grecvs):
    lev = lax.axis_index("lev")
    rows = out_ref.shape[1] // n
    for d in range(1, n):
        sender = lax.rem(lev + n - d, n)
        lev_copy(reduced.at[sender], reduced.at[sender], gsends.at[d - 1], grecvs.at[sender], sender).wait_recv()
        lev_copy(reduced.at[lev], reduced.at[lev], gsends.at[d - 1], grecvs.at[lev], lax.rem(lev + d, n)).wait_send()
    for q in range(n):
        out_ref[:, q * rows:(q + 1) * rows, :] = reduced[q]


def lev_scratch(n, shape, dtype):
    piece = (shape[0], shape[1] // n, shape[2])
    return [
        pltpu.VMEM((n,) + piece, dtype),
        pltpu.VMEM((n,) + piece, dtype),
        pltpu.SemaphoreType.DMA((n - 1,)),
        pltpu.SemaphoreType.DMA((n,)),
        pltpu.SemaphoreType.DMA((n - 1,)),
        pltpu.SemaphoreType.DMA((n,)),
    ]


def exchange_body(lev_n, owners, lat_n, rows_ref, part_ref, rows_out, sum_out,
                  got, row_send, row_recv, pieces, reduced, sends, recvs, gsends, grecvs):
    lat = lax.axis_index("lat")
    lev = lax.axis_index("lev")
    me = lax.axis_index("lon") * lat_n + lat

    def place(peer):
        return {"lon": peer // lat_n, "lat": lax.rem(peer, lat_n)}

    barrier = pltpu.get_barrier_semaphore()

    def greet(d, carry):
        peer = lax.rem(me + d, owners)
        pl.semaphore_signal(barrier, inc=1, device_id=place(peer), device_id_type=MESH)
        return carry

    lax.fori_loop(1, owners, greet, 0)
    for d in range(1, lev_n):
        pl.semaphore_signal(
            barrier, inc=1, device_id={"lev": lax.rem(lev + d, lev_n)}, device_id_type=MESH
        )
    pl.semaphore_wait(barrier, owners - 1 + lev_n - 1)
    scatter_start(lev_n, part_ref, pieces, sends, recvs)

    def row_copy(peer, target):
        return pltpu.make_async_remote_copy(
            src_ref=rows_ref.at[pl.ds(peer, 1)],
            dst_ref=got.at[pl.ds(target, 1)],
            send_sem=row_send.at[peer],
            recv_sem=row_recv.at[target],
            device_id=place(peer),
            device_id_type=MESH,
        )

    def send(d, carry):
        row_copy(lax.rem(me + d, owners), me).start()
        return carry

    lax.fori_loop(1, owners, send, 0)
    got[pl.ds(me, 1), :] = rows_ref[pl.ds(me, 1), :]
    scatter_finish_gather_start(lev_n, part_ref, pieces, reduced, sends, recvs, gsends, grecvs)

    def finish(d, carry):
        source = lax.rem(me + owners - d, owners)
        row_copy(lax.rem(me + d, owners), me).wait_send()
        row_copy(source, source).wait_recv()
        return carry

    lax.fori_loop(1, owners, finish, 0)
    gather_finish(lev_n, sum_out, reduced, gsends, grecvs)
    rows_out[...] = got[...]


def exchange(rows, part, collective_id):
    lev_n = lax.axis_size("lev")
    lat_n = lax.axis_size("lat")
    owners = lax.axis_size("lon") * lat_n
    vmem = pl.BlockSpec(memory_space=pltpu.VMEM)
    return pl.pallas_call(
        functools.partial(exchange_body, lev_n, owners, lat_n),
        out_shape=(
            jax.ShapeDtypeStruct(rows.shape, rows.dtype),
            jax.ShapeDtypeStruct(part.shape, part.dtype),
        ),
        in_specs=[vmem, vmem],
        out_specs=(vmem, vmem),
        scratch_shapes=[
            pltpu.VMEM(rows.shape, rows.dtype),
            pltpu.SemaphoreType.DMA((owners,)),
            pltpu.SemaphoreType.DMA((owners,)),
        ] + lev_scratch(lev_n, part.shape, part.dtype),
        compiler_params=pltpu.CompilerParams(
            collective_id=collective_id, has_side_effects=True
        ),
    )(rows, part)


def lev_sum(x, collective_id):
    n = lax.axis_size("lev")
    return pl.pallas_call(
        functools.partial(lev_sum_body, n),
        out_shape=jax.ShapeDtypeStruct(x.shape, x.dtype),
        in_specs=[pl.BlockSpec(memory_space=pltpu.VMEM)],
        out_specs=pl.BlockSpec(memory_space=pltpu.VMEM),
        scratch_shapes=lev_scratch(n, x.shape, x.dtype),
        compiler_params=pltpu.CompilerParams(
            collective_id=collective_id, has_side_effects=True
        ),
        cost_estimate=pl.CostEstimate(
            flops=n * x.size, bytes_accessed=(2 * n + 2) * x.size * 4, transcendentals=0
        ),
    )(x)


def from_behind(value, axis, steps):
    count = lax.axis_size(axis)
    pairs = [(source, (source + steps) % count) for source in range(count)]
    return lax.ppermute(value, axis, pairs)


def from_behind_2(block, axis, distance):
    devices = range(lax.axis_size(axis))
    route = [(i - distance, i) for i in devices if i - distance in devices]
    return lax.ppermute(block, axis, route)


def extended(x, sides, width, wrap):
    for axis, dim in sides:
        size, length = (lax.axis_size(axis), x.shape[dim])
        up = [(i, (i + 1) % size) for i in range(size if wrap else size - 1)]
        down = [(j, i) for i, j in up]
        last = lax.slice_in_dim(x, length - width, length, axis=dim)
        initial = lax.slice_in_dim(x, 0, width, axis=dim)
        before = lax.ppermute(last, axis, up)
        after = lax.ppermute(initial, axis, down)
        x = jnp.concatenate([before, x, after], axis=dim)
    return x


def mix_sum(partial_sum):
    return lax.psum(partial_sum, "lev")


def on_device(
    adjoint_field,
    east_courant,
    north_courant,
    pole_courant,
    mix_fraction,
    detrain_share,
    sounding_owner,
    sounding_cell,
    sounding_count,
    sounding_forcing,
):
    lon_count = lax.axis_size("lon")
    lat_count = lax.axis_size("lat")
    lat_place = lax.axis_index("lat")
    owner_self = lax.axis_index("lon") * lat_count + lat_place
    tracers, lev_dev, lat_rows, lon_cols = adjoint_field.shape
    step_count = sounding_forcing.shape[0]
    slot_count = sounding_forcing.shape[2]
    grid_cells = lat_rows * lon_cols
    detrain_part = jnp.sum(detrain_share, axis=0)
    owner_count = lon_count * lat_count
    cap = 4
    live_slots = jnp.arange(slot_count, dtype=jnp.int32)[None, :] < sounding_count
    values = jnp.where(live_slots[:, None, :], sounding_forcing, 0.0)
    owner_ids = sounding_owner[:, :, 0]
    slot_iota = jnp.arange(slot_count, dtype=jnp.int32)
    earlier = slot_iota[None, :, None] < slot_iota[None, None, :]
    same_owner = owner_ids[:, :, None] == owner_ids[:, None, :]
    rank = jnp.sum(jnp.logical_and(earlier, same_owner), axis=1, dtype=jnp.int32)
    position = owner_ids * cap + rank
    bucket_iota = jnp.arange(owner_count * cap, dtype=jnp.int32)
    chosen = position[:, :, None] == bucket_iota[None, None, :]
    bucket_values = jnp.sum(
        jnp.where(chosen[:, None, :, :], values[:, :, :, None], 0.0), axis=2
    )
    bucket_cell = jnp.max(
        jnp.where(chosen, sounding_cell[:, :, None] + 1, 0), axis=1
    ).astype(jnp.float32) - 1.0
    packed = jnp.concatenate([bucket_values, bucket_cell[:, None, :]], axis=1)
    packed = packed.reshape(step_count, lev_dev + 1, owner_count, cap)
    packed = jnp.transpose(packed, (2, 0, 1, 3))
    row_width = step_count * (lev_dev + 1) * cap
    rows = jnp.pad(packed.reshape(owner_count, row_width), ((0, 0), (0, 128 - row_width)))
    early_part = jnp.concatenate(
        [jnp.sum(detrain_share[None] * adjoint_field, axis=1), detrain_part[None]], axis=0
    )
    arrived, early = exchange(rows, early_part, 0)
    arrived = arrived[:, :row_width].reshape(owner_count, step_count, lev_dev + 1, cap)
    arrived = jnp.transpose(arrived, (1, 2, 0, 3)).reshape(
        step_count, lev_dev + 1, owner_count * cap
    )
    cells = arrived[:, lev_dev, :].astype(jnp.int32)
    row_hit = (cells // lon_cols)[:, :, None] == jnp.arange(lat_rows, dtype=jnp.int32)
    col_hit = (cells % lon_cols)[:, :, None] == jnp.arange(lon_cols, dtype=jnp.int32)
    spread = jnp.where(row_hit[:, None, :, :], arrived[:, :lev_dev, :, None], 0.0)
    forcing_grid = jnp.einsum(
        "tker,tec->tkrc", spread, col_hit.astype(jnp.float32), precision=lax.Precision.HIGHEST
    )
    row_index = jnp.arange(lat_rows, dtype=jnp.int32)[None, :, None]
    at_top = jnp.logical_and(lat_place == lat_count - 1, row_index == lat_rows - 1)
    at_bottom = jnp.logical_and(lat_place == 0, row_index == 0)
    upwind_east = jnp.maximum(east_courant, 0.0)
    forcing_part = jnp.sum(detrain_share * forcing_grid[step_count - 1], axis=0)
    forcing_sum = lev_sum(forcing_part[None], 4)[0]
    adjoint = adjoint_field
    for position in range(step_count):
        step_now = step_count - 1 - position
        adjoint = adjoint + forcing_grid[step_now][None]
        if position == 0:
            column_sum = early[:tracers] + forcing_sum[None]
            total_detrain = early[tracers]
        else:
            partial_sum = jnp.sum(detrain_share[None] * adjoint, axis=1)
            column_sum = lev_sum(partial_sum, 1)
        adjoint = (1.0 - mix_fraction)[None] * adjoint + mix_fraction[None] * (
            column_sum / total_detrain
        )[:, None]
        planes = tracers * lev_dev
        col_last = adjoint[:, :, :, -1].reshape(planes, lat_rows)
        col_first = adjoint[:, :, :, 0].reshape(planes, lat_rows)
        row_last = adjoint[:, :, -1, :].reshape(planes, lon_cols)
        row_first = adjoint[:, :, 0, :].reshape(planes, lon_cols)
        if position == 0:
            col_last = jnp.concatenate([col_last, east_courant[:, :, -1]], axis=0)
            col_first = jnp.concatenate([col_first, east_courant[:, :, 0]], axis=0)
            row_last = jnp.concatenate([row_last, north_courant[:, -1, :]], axis=0)
            row_first = jnp.concatenate([row_first, pole_courant], axis=0)
        west_halo, east_halo, north_halo, south_halo = halo_swap(
            col_last, col_first, row_last, row_first, 2 + position
        )
        if position == 0:
            west_wind = jnp.concatenate(
                [west_halo[planes:, :, None], east_courant[:, :, :-1]], axis=2
            )
            partner_top = north_halo[planes:]
            south_wind = jnp.concatenate(
                [south_halo[planes:, None, :], north_courant[:, :-1, :]], axis=1
            )
            partner_pole = south_halo[planes:]
            upwind_west = -jnp.minimum(west_wind, 0.0)
            upwind_north = jnp.maximum(north_courant, 0.0) + jnp.where(
                at_top, -jnp.minimum(partner_top, 0.0)[:, None, :], 0.0
            )
            upwind_south = jnp.where(
                at_bottom,
                (jnp.maximum(pole_courant, 0.0) - jnp.minimum(partner_pole, 0.0))[:, None, :],
                -jnp.minimum(south_wind, 0.0),
            )
            west_halo, east_halo = west_halo[:planes], east_halo[:planes]
            north_halo, south_halo = north_halo[:planes], south_halo[:planes]
        east_side = jnp.concatenate(
            [adjoint[:, :, :, 1:], east_halo.reshape(tracers, lev_dev, lat_rows, 1)], axis=3
        )
        west_side = jnp.concatenate(
            [west_halo.reshape(tracers, lev_dev, lat_rows, 1), adjoint[:, :, :, :-1]], axis=3
        )
        north_side = jnp.concatenate(
            [adjoint[:, :, 1:, :], north_halo.reshape(tracers, lev_dev, 1, lon_cols)], axis=2
        )
        south_side = jnp.concatenate(
            [south_halo.reshape(tracers, lev_dev, 1, lon_cols), adjoint[:, :, :-1, :]], axis=2
        )
        adjoint = (
            adjoint
            + upwind_east * (east_side - adjoint)
            + upwind_west * (west_side - adjoint)
            + upwind_north * (north_side - adjoint)
            + upwind_south * (south_side - adjoint)
        )
    return adjoint


def solution(mesh):
    return jax.shard_map(
        on_device,
        mesh=mesh,
        in_specs=(
            P(None, "lev", "lat", "lon"),
            P("lev", "lat", "lon"),
            P("lev", "lat", "lon"),
            P("lev", "lon"),
            P("lev", "lat", "lon"),
            P("lev", "lat", "lon"),
            P(None, ("lon", "lat"), None),
            P(None, ("lon", "lat")),
            P(None, ("lon", "lat")),
            P(None, "lev", ("lon", "lat")),
        ),
        out_specs=P(None, "lev", "lat", "lon"),
        check_vma=False,
    )
```

```python
import functools

import jax
import jax.numpy as jnp
from jax import lax
from jax.experimental import pallas as pl
from jax.experimental.pallas import tpu as pltpu
from jax.sharding import PartitionSpec as P

MESH = pl.DeviceIdType.MESH


def lev_sum_body(n, part_ref, out_ref, pieces, reduced, sends, recvs, gsends, grecvs):
    lev = lax.axis_index("lev")
    barrier = pltpu.get_barrier_semaphore()
    for d in range(1, n):
        pl.semaphore_signal(
            barrier, inc=1, device_id={"lev": lax.rem(lev + d, n)}, device_id_type=MESH
        )
    pl.semaphore_wait(barrier, n - 1)
    scatter_start(n, part_ref, pieces, sends, recvs)
    scatter_finish_gather_start(n, part_ref, pieces, reduced, sends, recvs, gsends, grecvs)
    gather_finish(n, out_ref, reduced, gsends, grecvs)


def halo_body(lon_n, lat_n, col_last, col_first, row_last, row_first,
              west_out, east_out, north_out, south_out, cols, rows, send_sem, col_sem, row_sem):
    lon = lax.axis_index("lon")
    lat = lax.axis_index("lat")
    half = lon_n // 2
    top = lat // (lat_n - 1)
    inner = (lat + lat_n - 1) // lat_n
    east = {"lon": lax.rem(lon + 1, lon_n)}
    west = {"lon": lax.rem(lon + lon_n - 1, lon_n)}
    up = {"lon": lax.rem(lon + half * top, lon_n), "lat": lat + 1 - top}
    down = {"lon": lax.rem(lon + half * (1 - inner), lon_n), "lat": lat - inner}
    up_slot = 1 - top
    down_slot = 1 - inner
    barrier = pltpu.get_barrier_semaphore()
    for peer in (east, west, up, down):
        pl.semaphore_signal(barrier, inc=1, device_id=peer, device_id_type=MESH)
    pl.semaphore_wait(barrier, 4)
    plan = (
        (col_last, cols.at[0], col_sem.at[0], east),
        (col_first, cols.at[1], col_sem.at[1], west),
        (row_last, rows.at[up_slot], row_sem.at[up_slot], up),
        (row_first, rows.at[down_slot], row_sem.at[down_slot], down),
    )
    sends = []
    for i, (src, dst, sem, peer) in enumerate(plan):
        copy = pltpu.make_async_remote_copy(
            src_ref=src, dst_ref=dst, send_sem=send_sem.at[i], recv_sem=sem,
            device_id=peer, device_id_type=MESH,
        )
        copy.start()
        sends.append(copy)
    arrivals = (
        (col_last, cols.at[0], col_sem.at[0]),
        (col_first, cols.at[1], col_sem.at[1]),
        (row_last, rows.at[0], row_sem.at[0]),
        (row_first, rows.at[1], row_sem.at[1]),
    )
    for src, dst, sem in arrivals:
        pltpu.make_async_remote_copy(
            src_ref=src, dst_ref=dst, send_sem=send_sem.at[0], recv_sem=sem,
            device_id=east, device_id_type=MESH,
        ).wait_recv()
    for copy in sends:
        copy.wait_send()
    west_out[...] = cols[0]
    east_out[...] = cols[1]
    north_out[...] = rows[0]
    south_out[...] = rows[1]


def halo_swap(col_last, col_first, row_last, row_first, collective_id):
    lon_n, lat_n = lax.axis_size("lon"), lax.axis_size("lat")
    vmem = pl.BlockSpec(memory_space=pltpu.VMEM)
    return pl.pallas_call(
        functools.partial(halo_body, lon_n, lat_n),
        out_shape=(
            jax.ShapeDtypeStruct(col_last.shape, col_last.dtype),
            jax.ShapeDtypeStruct(col_last.shape, col_last.dtype),
            jax.ShapeDtypeStruct(row_last.shape, row_last.dtype),
            jax.ShapeDtypeStruct(row_last.shape, row_last.dtype),
        ),
        in_specs=[vmem] * 4,
        out_specs=(vmem,) * 4,
        scratch_shapes=[
            pltpu.VMEM((2,) + col_last.shape, col_last.dtype),
            pltpu.VMEM((2,) + row_last.shape, row_last.dtype),
            pltpu.SemaphoreType.DMA((4,)),
            pltpu.SemaphoreType.DMA((2,)),
            pltpu.SemaphoreType.DMA((2,)),
        ],
        compiler_params=pltpu.CompilerParams(
            collective_id=collective_id, has_side_effects=True
        ),
    )(col_last, col_first, row_last, row_first)


def lev_copy(src, dst, send, recv, peer):
    return pltpu.make_async_remote_copy(
        src_ref=src, dst_ref=dst, send_sem=send, recv_sem=recv,
        device_id={"lev": peer}, device_id_type=MESH,
    )


def scatter_start(n, part_ref, pieces, sends, recvs):
    lev = lax.axis_index("lev")
    rows = part_ref.shape[1] // n
    for d in range(1, n):
        peer = lax.rem(lev + d, n)
        lev_copy(
            part_ref.at[:, pl.ds(pl.multiple_of(peer * rows, rows), rows), :],
            pieces.at[lev], sends.at[d - 1], recvs.at[lev], peer,
        ).start()
    pieces[lev] = part_ref[:, pl.ds(pl.multiple_of(lev * rows, rows), rows), :]


def scatter_finish_gather_start(n, part_ref, pieces, reduced, sends, recvs, gsends, grecvs):
    lev = lax.axis_index("lev")
    rows = part_ref.shape[1] // n
    for d in range(1, n):
        sender = lax.rem(lev + n - d, n)
        peer = lax.rem(lev + d, n)
        lev_copy(
            part_ref.at[:, pl.ds(0, rows), :], pieces.at[sender],
            sends.at[d - 1], recvs.at[sender], sender,
        ).wait_recv()
        lev_copy(
            part_ref.at[:, pl.ds(0, rows), :], pieces.at[sender],
            sends.at[d - 1], recvs.at[sender], peer,
        ).wait_send()
    total = pieces[0]
    for s in range(1, n):
        total = total + pieces[s]
    reduced[lev] = total
    for d in range(1, n):
        peer = lax.rem(lev + d, n)
        lev_copy(reduced.at[lev], reduced.at[lev], gsends.at[d - 1], grecvs.at[lev], peer).start()


def gather_finish(n, out_ref, reduced, gsends, grecvs):
    lev = lax.axis_index("lev")
    rows = out_ref.shape[1] // n
    for d in range(1, n):
        sender = lax.rem(lev + n - d, n)
        lev_copy(reduced.at[sender], reduced.at[sender], gsends.at[d - 1], grecvs.at[sender], sender).wait_recv()
        lev_copy(reduced.at[lev], reduced.at[lev], gsends.at[d - 1], grecvs.at[lev], lax.rem(lev + d, n)).wait_send()
    for q in range(n):
        out_ref[:, q * rows:(q + 1) * rows, :] = reduced[q]


def lev_scratch(n, shape, dtype):
    piece = (shape[0], shape[1] // n, shape[2])
    return [
        pltpu.VMEM((n,) + piece, dtype),
        pltpu.VMEM((n,) + piece, dtype),
        pltpu.SemaphoreType.DMA((n - 1,)),
        pltpu.SemaphoreType.DMA((n,)),
        pltpu.SemaphoreType.DMA((n - 1,)),
        pltpu.SemaphoreType.DMA((n,)),
    ]


def exchange_body(lev_n, owners, lat_n, rows_ref, part_ref, rows_out, sum_out,
                  got, row_send, row_recv, pieces, reduced, sends, recvs, gsends, grecvs):
    lat = lax.axis_index("lat")
    lev = lax.axis_index("lev")
    me = lax.axis_index("lon") * lat_n + lat

    def place(peer):
        return {"lon": peer // lat_n, "lat": lax.rem(peer, lat_n)}

    barrier = pltpu.get_barrier_semaphore()

    def greet(d, carry):
        peer = lax.rem(me + d, owners)
        pl.semaphore_signal(barrier, inc=1, device_id=place(peer), device_id_type=MESH)
        return carry

    lax.fori_loop(1, owners, greet, 0)
    for d in range(1, lev_n):
        pl.semaphore_signal(
            barrier, inc=1, device_id={"lev": lax.rem(lev + d, lev_n)}, device_id_type=MESH
        )
    pl.semaphore_wait(barrier, owners - 1 + lev_n - 1)
    scatter_start(lev_n, part_ref, pieces, sends, recvs)

    def row_copy(peer, target):
        return pltpu.make_async_remote_copy(
            src_ref=rows_ref.at[pl.ds(peer, 1)],
            dst_ref=got.at[pl.ds(target, 1)],
            send_sem=row_send.at[peer],
            recv_sem=row_recv.at[target],
            device_id=place(peer),
            device_id_type=MESH,
        )

    def send(d, carry):
        row_copy(lax.rem(me + d, owners), me).start()
        return carry

    lax.fori_loop(1, owners, send, 0)
    got[pl.ds(me, 1), :] = rows_ref[pl.ds(me, 1), :]
    scatter_finish_gather_start(lev_n, part_ref, pieces, reduced, sends, recvs, gsends, grecvs)

    def finish(d, carry):
        source = lax.rem(me + owners - d, owners)
        row_copy(lax.rem(me + d, owners), me).wait_send()
        row_copy(source, source).wait_recv()
        return carry

    lax.fori_loop(1, owners, finish, 0)
    gather_finish(lev_n, sum_out, reduced, gsends, grecvs)
    rows_out[...] = got[...]


def exchange(rows, part, collective_id):
    lev_n = lax.axis_size("lev")
    lat_n = lax.axis_size("lat")
    owners = lax.axis_size("lon") * lat_n
    vmem = pl.BlockSpec(memory_space=pltpu.VMEM)
    return pl.pallas_call(
        functools.partial(exchange_body, lev_n, owners, lat_n),
        out_shape=(
            jax.ShapeDtypeStruct(rows.shape, rows.dtype),
            jax.ShapeDtypeStruct(part.shape, part.dtype),
        ),
        in_specs=[vmem, vmem],
        out_specs=(vmem, vmem),
        scratch_shapes=[
            pltpu.VMEM(rows.shape, rows.dtype),
            pltpu.SemaphoreType.DMA((owners,)),
            pltpu.SemaphoreType.DMA((owners,)),
        ] + lev_scratch(lev_n, part.shape, part.dtype),
        compiler_params=pltpu.CompilerParams(
            collective_id=collective_id, has_side_effects=True
        ),
    )(rows, part)


def lev_direct_body(n, part_ref, out_ref, slots, send_sem, recv_sem):
    me = lax.axis_index("lev")
    barrier = pltpu.get_barrier_semaphore()
    for d in range(1, n):
        pl.semaphore_signal(
            barrier, inc=1, device_id={"lev": lax.rem(me + d, n)}, device_id_type=MESH
        )
    pl.semaphore_wait(barrier, n - 1)
    for d in range(1, n):
        lev_copy(part_ref, slots.at[me], send_sem.at[d - 1], recv_sem.at[me], lax.rem(me + d, n)).start()
    slots[me] = part_ref[...]
    for d in range(1, n):
        sender = lax.rem(me + n - d, n)
        lev_copy(part_ref, slots.at[sender], send_sem.at[d - 1], recv_sem.at[sender], sender).wait_recv()
        lev_copy(part_ref, slots.at[sender], send_sem.at[d - 1], recv_sem.at[sender], lax.rem(me + d, n)).wait_send()
    total = slots[0]
    for s in range(1, n):
        total = total + slots[s]
    out_ref[...] = total


def lev_direct(x, collective_id):
    n = lax.axis_size("lev")
    return pl.pallas_call(
        functools.partial(lev_direct_body, n),
        out_shape=jax.ShapeDtypeStruct(x.shape, x.dtype),
        in_specs=[pl.BlockSpec(memory_space=pltpu.VMEM)],
        out_specs=pl.BlockSpec(memory_space=pltpu.VMEM),
        scratch_shapes=[
            pltpu.VMEM((n,) + x.shape, x.dtype),
            pltpu.SemaphoreType.DMA((n - 1,)),
            pltpu.SemaphoreType.DMA((n,)),
        ],
        compiler_params=pltpu.CompilerParams(
            collective_id=collective_id, has_side_effects=True
        ),
    )(x)


def lev_sum(x, collective_id):
    n = lax.axis_size("lev")
    return pl.pallas_call(
        functools.partial(lev_sum_body, n),
        out_shape=jax.ShapeDtypeStruct(x.shape, x.dtype),
        in_specs=[pl.BlockSpec(memory_space=pltpu.VMEM)],
        out_specs=pl.BlockSpec(memory_space=pltpu.VMEM),
        scratch_shapes=lev_scratch(n, x.shape, x.dtype),
        compiler_params=pltpu.CompilerParams(
            collective_id=collective_id, has_side_effects=True
        ),
        cost_estimate=pl.CostEstimate(
            flops=n * x.size, bytes_accessed=(2 * n + 2) * x.size * 4, transcendentals=0
        ),
    )(x)


def from_behind(value, axis, steps):
    count = lax.axis_size(axis)
    pairs = [(source, (source + steps) % count) for source in range(count)]
    return lax.ppermute(value, axis, pairs)


def from_behind_2(block, axis, distance):
    devices = range(lax.axis_size(axis))
    route = [(i - distance, i) for i in devices if i - distance in devices]
    return lax.ppermute(block, axis, route)


def extended(x, sides, width, wrap):
    for axis, dim in sides:
        size, length = (lax.axis_size(axis), x.shape[dim])
        up = [(i, (i + 1) % size) for i in range(size if wrap else size - 1)]
        down = [(j, i) for i, j in up]
        last = lax.slice_in_dim(x, length - width, length, axis=dim)
        initial = lax.slice_in_dim(x, 0, width, axis=dim)
        before = lax.ppermute(last, axis, up)
        after = lax.ppermute(initial, axis, down)
        x = jnp.concatenate([before, x, after], axis=dim)
    return x


def mix_sum(partial_sum):
    return lax.psum(partial_sum, "lev")


def on_device(
    adjoint_field,
    east_courant,
    north_courant,
    pole_courant,
    mix_fraction,
    detrain_share,
    sounding_owner,
    sounding_cell,
    sounding_count,
    sounding_forcing,
):
    lon_count = lax.axis_size("lon")
    lat_count = lax.axis_size("lat")
    lat_place = lax.axis_index("lat")
    owner_self = lax.axis_index("lon") * lat_count + lat_place
    tracers, lev_dev, lat_rows, lon_cols = adjoint_field.shape
    step_count = sounding_forcing.shape[0]
    slot_count = sounding_forcing.shape[2]
    grid_cells = lat_rows * lon_cols
    detrain_part = jnp.sum(detrain_share, axis=0)
    owner_count = lon_count * lat_count
    cap = 4
    live_slots = jnp.arange(slot_count, dtype=jnp.int32)[None, :] < sounding_count
    values = jnp.where(live_slots[:, None, :], sounding_forcing, 0.0)
    owner_ids = sounding_owner[:, :, 0]
    slot_iota = jnp.arange(slot_count, dtype=jnp.int32)
    earlier = slot_iota[None, :, None] < slot_iota[None, None, :]
    same_owner = owner_ids[:, :, None] == owner_ids[:, None, :]
    rank = jnp.sum(jnp.logical_and(earlier, same_owner), axis=1, dtype=jnp.int32)
    position = owner_ids * cap + rank
    bucket_iota = jnp.arange(owner_count * cap, dtype=jnp.int32)
    chosen = position[:, :, None] == bucket_iota[None, None, :]
    bucket_values = jnp.sum(
        jnp.where(chosen[:, None, :, :], values[:, :, :, None], 0.0), axis=2
    )
    bucket_cell = jnp.max(
        jnp.where(chosen, sounding_cell[:, :, None] + 1, 0), axis=1
    ).astype(jnp.float32) - 1.0
    packed = jnp.concatenate([bucket_values, bucket_cell[:, None, :]], axis=1)
    packed = packed.reshape(step_count, lev_dev + 1, owner_count, cap)
    packed = jnp.transpose(packed, (2, 0, 1, 3))
    row_width = step_count * (lev_dev + 1) * cap
    rows = jnp.pad(packed.reshape(owner_count, row_width), ((0, 0), (0, 128 - row_width)))
    early_part = jnp.concatenate(
        [jnp.sum(detrain_share[None] * adjoint_field, axis=1), detrain_part[None]], axis=0
    )
    arrived, early = exchange(rows, early_part, 0)
    arrived = arrived[:, :row_width].reshape(owner_count, step_count, lev_dev + 1, cap)
    arrived = jnp.transpose(arrived, (1, 2, 0, 3)).reshape(
        step_count, lev_dev + 1, owner_count * cap
    )
    cells = arrived[:, lev_dev, :].astype(jnp.int32)
    row_hit = (cells // lon_cols)[:, :, None] == jnp.arange(lat_rows, dtype=jnp.int32)
    col_hit = (cells % lon_cols)[:, :, None] == jnp.arange(lon_cols, dtype=jnp.int32)
    spread = jnp.where(row_hit[:, None, :, :], arrived[:, :lev_dev, :, None], 0.0)
    forcing_grid = jnp.einsum(
        "tker,tec->tkrc", spread, col_hit.astype(jnp.float32), precision=lax.Precision.HIGHEST
    )
    row_index = jnp.arange(lat_rows, dtype=jnp.int32)[None, :, None]
    at_top = jnp.logical_and(lat_place == lat_count - 1, row_index == lat_rows - 1)
    at_bottom = jnp.logical_and(lat_place == 0, row_index == 0)
    upwind_east = jnp.maximum(east_courant, 0.0)
    forcing_part = jnp.sum(detrain_share * forcing_grid[step_count - 1], axis=0)
    forcing_sum = lev_direct(forcing_part[None], 4)[0]
    adjoint = adjoint_field
    for position in range(step_count):
        step_now = step_count - 1 - position
        adjoint = adjoint + forcing_grid[step_now][None]
        if position == 0:
            column_sum = early[:tracers] + forcing_sum[None]
            total_detrain = early[tracers]
        else:
            partial_sum = jnp.sum(detrain_share[None] * adjoint, axis=1)
            column_sum = lev_sum(partial_sum, 1)
        adjoint = (1.0 - mix_fraction)[None] * adjoint + mix_fraction[None] * (
            column_sum / total_detrain
        )[:, None]
        planes = tracers * lev_dev
        col_last = adjoint[:, :, :, -1].reshape(planes, lat_rows)
        col_first = adjoint[:, :, :, 0].reshape(planes, lat_rows)
        row_last = adjoint[:, :, -1, :].reshape(planes, lon_cols)
        row_first = adjoint[:, :, 0, :].reshape(planes, lon_cols)
        if position == 0:
            col_last = jnp.concatenate([col_last, east_courant[:, :, -1]], axis=0)
            col_first = jnp.concatenate([col_first, east_courant[:, :, 0]], axis=0)
            row_last = jnp.concatenate([row_last, north_courant[:, -1, :]], axis=0)
            row_first = jnp.concatenate([row_first, pole_courant], axis=0)
        west_halo, east_halo, north_halo, south_halo = halo_swap(
            col_last, col_first, row_last, row_first, 2 + position
        )
        if position == 0:
            west_wind = jnp.concatenate(
                [west_halo[planes:, :, None], east_courant[:, :, :-1]], axis=2
            )
            partner_top = north_halo[planes:]
            south_wind = jnp.concatenate(
                [south_halo[planes:, None, :], north_courant[:, :-1, :]], axis=1
            )
            partner_pole = south_halo[planes:]
            upwind_west = -jnp.minimum(west_wind, 0.0)
            upwind_north = jnp.maximum(north_courant, 0.0) + jnp.where(
                at_top, -jnp.minimum(partner_top, 0.0)[:, None, :], 0.0
            )
            upwind_south = jnp.where(
                at_bottom,
                (jnp.maximum(pole_courant, 0.0) - jnp.minimum(partner_pole, 0.0))[:, None, :],
                -jnp.minimum(south_wind, 0.0),
            )
            west_halo, east_halo = west_halo[:planes], east_halo[:planes]
            north_halo, south_halo = north_halo[:planes], south_halo[:planes]
        east_side = jnp.concatenate(
            [adjoint[:, :, :, 1:], east_halo.reshape(tracers, lev_dev, lat_rows, 1)], axis=3
        )
        west_side = jnp.concatenate(
            [west_halo.reshape(tracers, lev_dev, lat_rows, 1), adjoint[:, :, :, :-1]], axis=3
        )
        north_side = jnp.concatenate(
            [adjoint[:, :, 1:, :], north_halo.reshape(tracers, lev_dev, 1, lon_cols)], axis=2
        )
        south_side = jnp.concatenate(
            [south_halo.reshape(tracers, lev_dev, 1, lon_cols), adjoint[:, :, :-1, :]], axis=2
        )
        adjoint = (
            adjoint
            + upwind_east * (east_side - adjoint)
            + upwind_west * (west_side - adjoint)
            + upwind_north * (north_side - adjoint)
            + upwind_south * (south_side - adjoint)
        )
    return adjoint


def solution(mesh):
    return jax.shard_map(
        on_device,
        mesh=mesh,
        in_specs=(
            P(None, "lev", "lat", "lon"),
            P("lev", "lat", "lon"),
            P("lev", "lat", "lon"),
            P("lev", "lon"),
            P("lev", "lat", "lon"),
            P("lev", "lat", "lon"),
            P(None, ("lon", "lat"), None),
            P(None, ("lon", "lat")),
            P(None, ("lon", "lat")),
            P(None, "lev", ("lon", "lat")),
        ),
        out_specs=P(None, "lev", "lat", "lon"),
        check_vma=False,
    )
```

```python
import functools

import jax
import jax.numpy as jnp
from jax import lax
from jax.experimental import pallas as pl
from jax.experimental.pallas import tpu as pltpu
from jax.sharding import PartitionSpec as P

MESH = pl.DeviceIdType.MESH


def lev_sum_body(n, part_ref, out_ref, pieces, reduced, sends, recvs, gsends, grecvs):
    lev = lax.axis_index("lev")
    barrier = pltpu.get_barrier_semaphore()
    for d in range(1, n):
        pl.semaphore_signal(
            barrier, inc=1, device_id={"lev": lax.rem(lev + d, n)}, device_id_type=MESH
        )
    pl.semaphore_wait(barrier, n - 1)
    scatter_start(n, part_ref, pieces, sends, recvs)
    scatter_finish_gather_start(n, part_ref, pieces, reduced, sends, recvs, gsends, grecvs)
    gather_finish(n, out_ref, reduced, gsends, grecvs)


def halo_body(lon_n, lat_n, col_last, col_first, row_last, row_first,
              west_out, east_out, north_out, south_out, cols, rows, send_sem, col_sem, row_sem):
    lon = lax.axis_index("lon")
    lat = lax.axis_index("lat")
    half = lon_n // 2
    top = lat // (lat_n - 1)
    inner = (lat + lat_n - 1) // lat_n
    east = {"lon": lax.rem(lon + 1, lon_n)}
    west = {"lon": lax.rem(lon + lon_n - 1, lon_n)}
    up = {"lon": lax.rem(lon + half * top, lon_n), "lat": lat + 1 - top}
    down = {"lon": lax.rem(lon + half * (1 - inner), lon_n), "lat": lat - inner}
    up_slot = 1 - top
    down_slot = 1 - inner
    barrier = pltpu.get_barrier_semaphore()
    for peer in (east, west, up, down):
        pl.semaphore_signal(barrier, inc=1, device_id=peer, device_id_type=MESH)
    pl.semaphore_wait(barrier, 4)
    plan = (
        (col_last, cols.at[0], col_sem.at[0], east),
        (col_first, cols.at[1], col_sem.at[1], west),
        (row_last, rows.at[up_slot], row_sem.at[up_slot], up),
        (row_first, rows.at[down_slot], row_sem.at[down_slot], down),
    )
    sends = []
    for i, (src, dst, sem, peer) in enumerate(plan):
        copy = pltpu.make_async_remote_copy(
            src_ref=src, dst_ref=dst, send_sem=send_sem.at[i], recv_sem=sem,
            device_id=peer, device_id_type=MESH,
        )
        copy.start()
        sends.append(copy)
    arrivals = (
        (col_last, cols.at[0], col_sem.at[0]),
        (col_first, cols.at[1], col_sem.at[1]),
        (row_last, rows.at[0], row_sem.at[0]),
        (row_first, rows.at[1], row_sem.at[1]),
    )
    for src, dst, sem in arrivals:
        pltpu.make_async_remote_copy(
            src_ref=src, dst_ref=dst, send_sem=send_sem.at[0], recv_sem=sem,
            device_id=east, device_id_type=MESH,
        ).wait_recv()
    for copy in sends:
        copy.wait_send()
    west_out[...] = cols[0]
    east_out[...] = cols[1]
    north_out[...] = rows[0]
    south_out[...] = rows[1]


def halo_swap(col_last, col_first, row_last, row_first, collective_id):
    lon_n, lat_n = lax.axis_size("lon"), lax.axis_size("lat")
    vmem = pl.BlockSpec(memory_space=pltpu.VMEM)
    return pl.pallas_call(
        functools.partial(halo_body, lon_n, lat_n),
        out_shape=(
            jax.ShapeDtypeStruct(col_last.shape, col_last.dtype),
            jax.ShapeDtypeStruct(col_last.shape, col_last.dtype),
            jax.ShapeDtypeStruct(row_last.shape, row_last.dtype),
            jax.ShapeDtypeStruct(row_last.shape, row_last.dtype),
        ),
        in_specs=[vmem] * 4,
        out_specs=(vmem,) * 4,
        scratch_shapes=[
            pltpu.VMEM((2,) + col_last.shape, col_last.dtype),
            pltpu.VMEM((2,) + row_last.shape, row_last.dtype),
            pltpu.SemaphoreType.DMA((4,)),
            pltpu.SemaphoreType.DMA((2,)),
            pltpu.SemaphoreType.DMA((2,)),
        ],
        compiler_params=pltpu.CompilerParams(
            collective_id=collective_id, has_side_effects=True
        ),
    )(col_last, col_first, row_last, row_first)


def lev_copy(src, dst, send, recv, peer):
    return pltpu.make_async_remote_copy(
        src_ref=src, dst_ref=dst, send_sem=send, recv_sem=recv,
        device_id={"lev": peer}, device_id_type=MESH,
    )


def scatter_start(n, part_ref, pieces, sends, recvs):
    lev = lax.axis_index("lev")
    rows = part_ref.shape[1] // n
    for d in range(1, n):
        peer = lax.rem(lev + d, n)
        lev_copy(
            part_ref.at[:, pl.ds(pl.multiple_of(peer * rows, rows), rows), :],
            pieces.at[lev], sends.at[d - 1], recvs.at[lev], peer,
        ).start()
    pieces[lev] = part_ref[:, pl.ds(pl.multiple_of(lev * rows, rows), rows), :]


def scatter_finish_gather_start(n, part_ref, pieces, reduced, sends, recvs, gsends, grecvs):
    lev = lax.axis_index("lev")
    rows = part_ref.shape[1] // n
    for d in range(1, n):
        sender = lax.rem(lev + n - d, n)
        peer = lax.rem(lev + d, n)
        lev_copy(
            part_ref.at[:, pl.ds(0, rows), :], pieces.at[sender],
            sends.at[d - 1], recvs.at[sender], sender,
        ).wait_recv()
        lev_copy(
            part_ref.at[:, pl.ds(0, rows), :], pieces.at[sender],
            sends.at[d - 1], recvs.at[sender], peer,
        ).wait_send()
    total = pieces[0]
    for s in range(1, n):
        total = total + pieces[s]
    reduced[lev] = total
    for d in range(1, n):
        peer = lax.rem(lev + d, n)
        lev_copy(reduced.at[lev], reduced.at[lev], gsends.at[d - 1], grecvs.at[lev], peer).start()


def gather_finish(n, out_ref, reduced, gsends, grecvs):
    lev = lax.axis_index("lev")
    rows = out_ref.shape[1] // n
    for d in range(1, n):
        sender = lax.rem(lev + n - d, n)
        lev_copy(reduced.at[sender], reduced.at[sender], gsends.at[d - 1], grecvs.at[sender], sender).wait_recv()
        lev_copy(reduced.at[lev], reduced.at[lev], gsends.at[d - 1], grecvs.at[lev], lax.rem(lev + d, n)).wait_send()
    for q in range(n):
        out_ref[:, q * rows:(q + 1) * rows, :] = reduced[q]


def lev_scratch(n, shape, dtype):
    piece = (shape[0], shape[1] // n, shape[2])
    return [
        pltpu.VMEM((n,) + piece, dtype),
        pltpu.VMEM((n,) + piece, dtype),
        pltpu.SemaphoreType.DMA((n - 1,)),
        pltpu.SemaphoreType.DMA((n,)),
        pltpu.SemaphoreType.DMA((n - 1,)),
        pltpu.SemaphoreType.DMA((n,)),
    ]


def exchange_body(lev_n, owners, lat_n, rows_ref, part_ref, rows_out, sum_out,
                  got, row_send, row_recv, pieces, reduced, sends, recvs, gsends, grecvs):
    lat = lax.axis_index("lat")
    lev = lax.axis_index("lev")
    me = lax.axis_index("lon") * lat_n + lat

    def place(peer):
        return {"lon": peer // lat_n, "lat": lax.rem(peer, lat_n)}

    barrier = pltpu.get_barrier_semaphore()

    def greet(d, carry):
        peer = lax.rem(me + d, owners)
        pl.semaphore_signal(barrier, inc=1, device_id=place(peer), device_id_type=MESH)
        return carry

    lax.fori_loop(1, owners, greet, 0)
    for d in range(1, lev_n):
        pl.semaphore_signal(
            barrier, inc=1, device_id={"lev": lax.rem(lev + d, lev_n)}, device_id_type=MESH
        )
    pl.semaphore_wait(barrier, owners - 1 + lev_n - 1)
    scatter_start(lev_n, part_ref, pieces, sends, recvs)

    def row_copy(peer, target):
        return pltpu.make_async_remote_copy(
            src_ref=rows_ref.at[pl.ds(peer, 1)],
            dst_ref=got.at[pl.ds(target, 1)],
            send_sem=row_send.at[peer],
            recv_sem=row_recv.at[target],
            device_id=place(peer),
            device_id_type=MESH,
        )

    def send(d, carry):
        row_copy(lax.rem(me + d, owners), me).start()
        return carry

    lax.fori_loop(1, owners, send, 0)
    got[pl.ds(me, 1), :] = rows_ref[pl.ds(me, 1), :]
    scatter_finish_gather_start(lev_n, part_ref, pieces, reduced, sends, recvs, gsends, grecvs)

    def finish(d, carry):
        source = lax.rem(me + owners - d, owners)
        row_copy(lax.rem(me + d, owners), me).wait_send()
        row_copy(source, source).wait_recv()
        return carry

    lax.fori_loop(1, owners, finish, 0)
    gather_finish(lev_n, sum_out, reduced, gsends, grecvs)
    rows_out[...] = got[...]


def exchange(rows, part, collective_id):
    lev_n = lax.axis_size("lev")
    lat_n = lax.axis_size("lat")
    owners = lax.axis_size("lon") * lat_n
    vmem = pl.BlockSpec(memory_space=pltpu.VMEM)
    return pl.pallas_call(
        functools.partial(exchange_body, lev_n, owners, lat_n),
        out_shape=(
            jax.ShapeDtypeStruct(rows.shape, rows.dtype),
            jax.ShapeDtypeStruct(part.shape, part.dtype),
        ),
        in_specs=[vmem, vmem],
        out_specs=(vmem, vmem),
        scratch_shapes=[
            pltpu.VMEM(rows.shape, rows.dtype),
            pltpu.SemaphoreType.DMA((owners,)),
            pltpu.SemaphoreType.DMA((owners,)),
        ] + lev_scratch(lev_n, part.shape, part.dtype),
        compiler_params=pltpu.CompilerParams(
            collective_id=collective_id, has_side_effects=True
        ),
    )(rows, part)


def lev_direct_body(n, part_ref, out_ref, slots, send_sem, recv_sem):
    me = lax.axis_index("lev")
    barrier = pltpu.get_barrier_semaphore()
    for d in range(1, n):
        pl.semaphore_signal(
            barrier, inc=1, device_id={"lev": lax.rem(me + d, n)}, device_id_type=MESH
        )
    pl.semaphore_wait(barrier, n - 1)
    for d in range(1, n):
        lev_copy(part_ref, slots.at[me], send_sem.at[d - 1], recv_sem.at[me], lax.rem(me + d, n)).start()
    slots[me] = part_ref[...]
    for d in range(1, n):
        sender = lax.rem(me + n - d, n)
        lev_copy(part_ref, slots.at[sender], send_sem.at[d - 1], recv_sem.at[sender], sender).wait_recv()
        lev_copy(part_ref, slots.at[sender], send_sem.at[d - 1], recv_sem.at[sender], lax.rem(me + d, n)).wait_send()
    total = slots[0]
    for s in range(1, n):
        total = total + slots[s]
    out_ref[...] = total


def lev_direct(x, collective_id):
    n = lax.axis_size("lev")
    return pl.pallas_call(
        functools.partial(lev_direct_body, n),
        out_shape=jax.ShapeDtypeStruct(x.shape, x.dtype),
        in_specs=[pl.BlockSpec(memory_space=pltpu.VMEM)],
        out_specs=pl.BlockSpec(memory_space=pltpu.VMEM),
        scratch_shapes=[
            pltpu.VMEM((n,) + x.shape, x.dtype),
            pltpu.SemaphoreType.DMA((n - 1,)),
            pltpu.SemaphoreType.DMA((n,)),
        ],
        compiler_params=pltpu.CompilerParams(
            collective_id=collective_id, has_side_effects=True
        ),
    )(x)


def lev_sum(x, collective_id):
    n = lax.axis_size("lev")
    return pl.pallas_call(
        functools.partial(lev_sum_body, n),
        out_shape=jax.ShapeDtypeStruct(x.shape, x.dtype),
        in_specs=[pl.BlockSpec(memory_space=pltpu.VMEM)],
        out_specs=pl.BlockSpec(memory_space=pltpu.VMEM),
        scratch_shapes=lev_scratch(n, x.shape, x.dtype),
        compiler_params=pltpu.CompilerParams(
            collective_id=collective_id, has_side_effects=True
        ),
        cost_estimate=pl.CostEstimate(
            flops=n * x.size, bytes_accessed=(2 * n + 2) * x.size * 4, transcendentals=0
        ),
    )(x)


def from_behind(value, axis, steps):
    count = lax.axis_size(axis)
    pairs = [(source, (source + steps) % count) for source in range(count)]
    return lax.ppermute(value, axis, pairs)


def from_behind_2(block, axis, distance):
    devices = range(lax.axis_size(axis))
    route = [(i - distance, i) for i in devices if i - distance in devices]
    return lax.ppermute(block, axis, route)


def extended(x, sides, width, wrap):
    for axis, dim in sides:
        size, length = (lax.axis_size(axis), x.shape[dim])
        up = [(i, (i + 1) % size) for i in range(size if wrap else size - 1)]
        down = [(j, i) for i, j in up]
        last = lax.slice_in_dim(x, length - width, length, axis=dim)
        initial = lax.slice_in_dim(x, 0, width, axis=dim)
        before = lax.ppermute(last, axis, up)
        after = lax.ppermute(initial, axis, down)
        x = jnp.concatenate([before, x, after], axis=dim)
    return x


def mix_sum(partial_sum):
    return lax.psum(partial_sum, "lev")


def on_device(
    adjoint_field,
    east_courant,
    north_courant,
    pole_courant,
    mix_fraction,
    detrain_share,
    sounding_owner,
    sounding_cell,
    sounding_count,
    sounding_forcing,
):
    lon_count = lax.axis_size("lon")
    lat_count = lax.axis_size("lat")
    lat_place = lax.axis_index("lat")
    owner_self = lax.axis_index("lon") * lat_count + lat_place
    tracers, lev_dev, lat_rows, lon_cols = adjoint_field.shape
    step_count = sounding_forcing.shape[0]
    slot_count = sounding_forcing.shape[2]
    grid_cells = lat_rows * lon_cols
    detrain_part = jnp.sum(detrain_share, axis=0)
    owner_count = lon_count * lat_count
    cap = 4
    live_slots = jnp.arange(slot_count, dtype=jnp.int32)[None, :] < sounding_count
    values = jnp.where(live_slots[:, None, :], sounding_forcing, 0.0)
    owner_ids = sounding_owner[:, :, 0]
    slot_iota = jnp.arange(slot_count, dtype=jnp.int32)
    earlier = slot_iota[None, :, None] < slot_iota[None, None, :]
    same_owner = owner_ids[:, :, None] == owner_ids[:, None, :]
    rank = jnp.sum(jnp.logical_and(earlier, same_owner), axis=1, dtype=jnp.int32)
    position = owner_ids * cap + rank
    bucket_iota = jnp.arange(owner_count * cap, dtype=jnp.int32)
    chosen = position[:, :, None] == bucket_iota[None, None, :]
    bucket_values = jnp.sum(
        jnp.where(chosen[:, None, :, :], values[:, :, :, None], 0.0), axis=2
    )
    bucket_cell = jnp.max(
        jnp.where(chosen, sounding_cell[:, :, None] + 1, 0), axis=1
    ).astype(jnp.float32) - 1.0
    packed = jnp.concatenate([bucket_values, bucket_cell[:, None, :]], axis=1)
    packed = packed.reshape(step_count, lev_dev + 1, owner_count, cap)
    packed = jnp.transpose(packed, (2, 0, 1, 3))
    row_width = step_count * (lev_dev + 1) * cap
    rows = jnp.pad(packed.reshape(owner_count, row_width), ((0, 0), (0, 128 - row_width)))
    early_part = jnp.concatenate(
        [jnp.sum(detrain_share[None] * adjoint_field, axis=1), detrain_part[None]], axis=0
    )
    arrived, early = exchange(rows, early_part, 0)
    arrived = arrived[:, :row_width].reshape(owner_count, step_count, lev_dev + 1, cap)
    arrived = jnp.transpose(arrived, (1, 2, 0, 3)).reshape(
        step_count, lev_dev + 1, owner_count * cap
    )
    cells = arrived[:, lev_dev, :].astype(jnp.int32)
    row_hit = (cells // lon_cols)[:, :, None] == jnp.arange(lat_rows, dtype=jnp.int32)
    col_hit = (cells % lon_cols)[:, :, None] == jnp.arange(lon_cols, dtype=jnp.int32)
    spread = jnp.where(row_hit[:, None, :, :], arrived[:, :lev_dev, :, None], 0.0)
    forcing_grid = jnp.einsum(
        "tker,tec->tkrc", spread, col_hit.astype(jnp.float32), precision=lax.Precision.HIGHEST
    )
    row_index = jnp.arange(lat_rows, dtype=jnp.int32)[None, :, None]
    at_top = jnp.logical_and(lat_place == lat_count - 1, row_index == lat_rows - 1)
    at_bottom = jnp.logical_and(lat_place == 0, row_index == 0)
    upwind_east = jnp.maximum(east_courant, 0.0)
    forcing_part = jnp.sum(detrain_share * forcing_grid[step_count - 1], axis=0)
    forcing_sum = lev_direct(forcing_part[None], 4)[0]
    adjoint = adjoint_field
    for position in range(step_count):
        step_now = step_count - 1 - position
        adjoint = adjoint + forcing_grid[step_now][None]
        if position == 0:
            column_sum = early[:tracers] + forcing_sum[None]
            total_detrain = early[tracers]
        else:
            partial_sum = jnp.sum(detrain_share[None] * adjoint, axis=1)
            column_sum = lev_sum(partial_sum, 1)
        adjoint = (1.0 - mix_fraction)[None] * adjoint + mix_fraction[None] * (
            column_sum / total_detrain
        )[:, None]
        planes = tracers * lev_dev
        col_last = adjoint[:, :, :, -1].reshape(planes, lat_rows)
        col_first = adjoint[:, :, :, 0].reshape(planes, lat_rows)
        row_last = adjoint[:, :, -1, :].reshape(planes, lon_cols)
        row_first = adjoint[:, :, 0, :].reshape(planes, lon_cols)
        if position == 0:
            col_last = jnp.concatenate([col_last, east_courant[:, :, -1]], axis=0)
            col_first = jnp.concatenate([col_first, east_courant[:, :, 0]], axis=0)
            row_last = jnp.concatenate([row_last, north_courant[:, -1, :]], axis=0)
            row_first = jnp.concatenate([row_first, pole_courant], axis=0)
        west_halo, east_halo, north_halo, south_halo = halo_swap(
            col_last, col_first, row_last, row_first, 2 + position
        )
        if position == 0:
            west_wind = jnp.concatenate(
                [west_halo[planes:, :, None], east_courant[:, :, :-1]], axis=2
            )
            partner_top = north_halo[planes:]
            south_wind = jnp.concatenate(
                [south_halo[planes:, None, :], north_courant[:, :-1, :]], axis=1
            )
            partner_pole = south_halo[planes:]
            upwind_west = -jnp.minimum(west_wind, 0.0)
            upwind_north = jnp.maximum(north_courant, 0.0) + jnp.where(
                at_top, -jnp.minimum(partner_top, 0.0)[:, None, :], 0.0
            )
            upwind_south = jnp.where(
                at_bottom,
                (jnp.maximum(pole_courant, 0.0) - jnp.minimum(partner_pole, 0.0))[:, None, :],
                -jnp.minimum(south_wind, 0.0),
            )
            west_halo, east_halo = west_halo[:planes], east_halo[:planes]
            north_halo, south_halo = north_halo[:planes], south_halo[:planes]
        lane = jnp.arange(lon_cols, dtype=jnp.int32)
        sub = jnp.arange(lat_rows, dtype=jnp.int32)[:, None]
        east_side = jnp.where(
            lane == lon_cols - 1,
            east_halo.reshape(tracers, lev_dev, lat_rows)[..., None],
            jnp.roll(adjoint, -1, axis=3),
        )
        west_side = jnp.where(
            lane == 0,
            west_halo.reshape(tracers, lev_dev, lat_rows)[..., None],
            jnp.roll(adjoint, 1, axis=3),
        )
        north_side = jnp.where(
            sub == lat_rows - 1,
            north_halo.reshape(tracers, lev_dev, 1, lon_cols),
            jnp.roll(adjoint, -1, axis=2),
        )
        south_side = jnp.where(
            sub == 0,
            south_halo.reshape(tracers, lev_dev, 1, lon_cols),
            jnp.roll(adjoint, 1, axis=2),
        )
        adjoint = (
            adjoint
            + upwind_east * (east_side - adjoint)
            + upwind_west * (west_side - adjoint)
            + upwind_north * (north_side - adjoint)
            + upwind_south * (south_side - adjoint)
        )
    return adjoint


def solution(mesh):
    return jax.shard_map(
        on_device,
        mesh=mesh,
        in_specs=(
            P(None, "lev", "lat", "lon"),
            P("lev", "lat", "lon"),
            P("lev", "lat", "lon"),
            P("lev", "lon"),
            P("lev", "lat", "lon"),
            P("lev", "lat", "lon"),
            P(None, ("lon", "lat"), None),
            P(None, ("lon", "lat")),
            P(None, ("lon", "lat")),
            P(None, "lev", ("lon", "lat")),
        ),
        out_specs=P(None, "lev", "lat", "lon"),
        check_vma=False,
    )
```

```python
import functools

import jax
import jax.numpy as jnp
from jax import lax
from jax.experimental import pallas as pl
from jax.experimental.pallas import tpu as pltpu
from jax.sharding import PartitionSpec as P

MESH = pl.DeviceIdType.MESH


def lev_sum_body(n, part_ref, out_ref, pieces, reduced, sends, recvs, gsends, grecvs):
    lev = lax.axis_index("lev")
    barrier = pltpu.get_barrier_semaphore()
    for d in range(1, n):
        pl.semaphore_signal(
            barrier, inc=1, device_id={"lev": lax.rem(lev + d, n)}, device_id_type=MESH
        )
    pl.semaphore_wait(barrier, n - 1)
    scatter_start(n, part_ref, pieces, sends, recvs)
    scatter_finish_gather_start(n, part_ref, pieces, reduced, sends, recvs, gsends, grecvs)
    gather_finish(n, out_ref, reduced, gsends, grecvs)


def halo_body(lon_n, lat_n, col_last, col_first, row_last, row_first,
              west_out, east_out, north_out, south_out, cols, rows, send_sem, col_sem, row_sem):
    lon = lax.axis_index("lon")
    lat = lax.axis_index("lat")
    half = lon_n // 2
    top = lat // (lat_n - 1)
    inner = (lat + lat_n - 1) // lat_n
    east = {"lon": lax.rem(lon + 1, lon_n)}
    west = {"lon": lax.rem(lon + lon_n - 1, lon_n)}
    up = {"lon": lax.rem(lon + half * top, lon_n), "lat": lat + 1 - top}
    down = {"lon": lax.rem(lon + half * (1 - inner), lon_n), "lat": lat - inner}
    up_slot = 1 - top
    down_slot = 1 - inner
    barrier = pltpu.get_barrier_semaphore()
    for peer in (east, west, up, down):
        pl.semaphore_signal(barrier, inc=1, device_id=peer, device_id_type=MESH)
    pl.semaphore_wait(barrier, 4)
    plan = (
        (col_last, cols.at[0], col_sem.at[0], east),
        (col_first, cols.at[1], col_sem.at[1], west),
        (row_last, rows.at[up_slot], row_sem.at[up_slot], up),
        (row_first, rows.at[down_slot], row_sem.at[down_slot], down),
    )
    sends = []
    for i, (src, dst, sem, peer) in enumerate(plan):
        copy = pltpu.make_async_remote_copy(
            src_ref=src, dst_ref=dst, send_sem=send_sem.at[i], recv_sem=sem,
            device_id=peer, device_id_type=MESH,
        )
        copy.start()
        sends.append(copy)
    arrivals = (
        (col_last, cols.at[0], col_sem.at[0]),
        (col_first, cols.at[1], col_sem.at[1]),
        (row_last, rows.at[0], row_sem.at[0]),
        (row_first, rows.at[1], row_sem.at[1]),
    )
    for src, dst, sem in arrivals:
        pltpu.make_async_remote_copy(
            src_ref=src, dst_ref=dst, send_sem=send_sem.at[0], recv_sem=sem,
            device_id=east, device_id_type=MESH,
        ).wait_recv()
    for copy in sends:
        copy.wait_send()
    west_out[...] = cols[0]
    east_out[...] = cols[1]
    north_out[...] = rows[0]
    south_out[...] = rows[1]


def halo_swap(col_last, col_first, row_last, row_first, collective_id):
    lon_n, lat_n = lax.axis_size("lon"), lax.axis_size("lat")
    vmem = pl.BlockSpec(memory_space=pltpu.VMEM)
    return pl.pallas_call(
        functools.partial(halo_body, lon_n, lat_n),
        out_shape=(
            jax.ShapeDtypeStruct(col_last.shape, col_last.dtype),
            jax.ShapeDtypeStruct(col_last.shape, col_last.dtype),
            jax.ShapeDtypeStruct(row_last.shape, row_last.dtype),
            jax.ShapeDtypeStruct(row_last.shape, row_last.dtype),
        ),
        in_specs=[vmem] * 4,
        out_specs=(vmem,) * 4,
        scratch_shapes=[
            pltpu.VMEM((2,) + col_last.shape, col_last.dtype),
            pltpu.VMEM((2,) + row_last.shape, row_last.dtype),
            pltpu.SemaphoreType.DMA((4,)),
            pltpu.SemaphoreType.DMA((2,)),
            pltpu.SemaphoreType.DMA((2,)),
        ],
        compiler_params=pltpu.CompilerParams(
            collective_id=collective_id, has_side_effects=True
        ),
    )(col_last, col_first, row_last, row_first)


def lev_copy(src, dst, send, recv, peer):
    return pltpu.make_async_remote_copy(
        src_ref=src, dst_ref=dst, send_sem=send, recv_sem=recv,
        device_id={"lev": peer}, device_id_type=MESH,
    )


def scatter_start(n, part_ref, pieces, sends, recvs):
    lev = lax.axis_index("lev")
    rows = part_ref.shape[1] // n
    for d in range(1, n):
        peer = lax.rem(lev + d, n)
        lev_copy(
            part_ref.at[:, pl.ds(pl.multiple_of(peer * rows, rows), rows), :],
            pieces.at[lev], sends.at[d - 1], recvs.at[lev], peer,
        ).start()
    pieces[lev] = part_ref[:, pl.ds(pl.multiple_of(lev * rows, rows), rows), :]


def scatter_finish_gather_start(n, part_ref, pieces, reduced, sends, recvs, gsends, grecvs):
    lev = lax.axis_index("lev")
    rows = part_ref.shape[1] // n
    for d in range(1, n):
        sender = lax.rem(lev + n - d, n)
        peer = lax.rem(lev + d, n)
        lev_copy(
            part_ref.at[:, pl.ds(0, rows), :], pieces.at[sender],
            sends.at[d - 1], recvs.at[sender], sender,
        ).wait_recv()
        lev_copy(
            part_ref.at[:, pl.ds(0, rows), :], pieces.at[sender],
            sends.at[d - 1], recvs.at[sender], peer,
        ).wait_send()
    total = pieces[0]
    for s in range(1, n):
        total = total + pieces[s]
    reduced[lev] = total
    for d in range(1, n):
        peer = lax.rem(lev + d, n)
        lev_copy(reduced.at[lev], reduced.at[lev], gsends.at[d - 1], grecvs.at[lev], peer).start()


def gather_finish(n, out_ref, reduced, gsends, grecvs):
    lev = lax.axis_index("lev")
    rows = out_ref.shape[1] // n
    for d in range(1, n):
        sender = lax.rem(lev + n - d, n)
        lev_copy(reduced.at[sender], reduced.at[sender], gsends.at[d - 1], grecvs.at[sender], sender).wait_recv()
        lev_copy(reduced.at[lev], reduced.at[lev], gsends.at[d - 1], grecvs.at[lev], lax.rem(lev + d, n)).wait_send()
    for q in range(n):
        out_ref[:, q * rows:(q + 1) * rows, :] = reduced[q]


def lev_scratch(n, shape, dtype):
    piece = (shape[0], shape[1] // n, shape[2])
    return [
        pltpu.VMEM((n,) + piece, dtype),
        pltpu.VMEM((n,) + piece, dtype),
        pltpu.SemaphoreType.DMA((n - 1,)),
        pltpu.SemaphoreType.DMA((n,)),
        pltpu.SemaphoreType.DMA((n - 1,)),
        pltpu.SemaphoreType.DMA((n,)),
    ]


def exchange_body(lev_n, owners, lat_n, rows_ref, part_ref, rows_out, sum_out,
                  got, row_send, row_recv, pieces, reduced, sends, recvs, gsends, grecvs):
    lat = lax.axis_index("lat")
    lev = lax.axis_index("lev")
    me = lax.axis_index("lon") * lat_n + lat

    def place(peer):
        return {"lon": peer // lat_n, "lat": lax.rem(peer, lat_n)}

    barrier = pltpu.get_barrier_semaphore()

    def greet(d, carry):
        peer = lax.rem(me + d, owners)
        pl.semaphore_signal(barrier, inc=1, device_id=place(peer), device_id_type=MESH)
        return carry

    lax.fori_loop(1, owners, greet, 0)
    for d in range(1, lev_n):
        pl.semaphore_signal(
            barrier, inc=1, device_id={"lev": lax.rem(lev + d, lev_n)}, device_id_type=MESH
        )
    pl.semaphore_wait(barrier, owners - 1 + lev_n - 1)
    scatter_start(lev_n, part_ref, pieces, sends, recvs)

    def row_copy(peer, target):
        return pltpu.make_async_remote_copy(
            src_ref=rows_ref.at[pl.ds(peer, 1)],
            dst_ref=got.at[pl.ds(target, 1)],
            send_sem=row_send.at[peer],
            recv_sem=row_recv.at[target],
            device_id=place(peer),
            device_id_type=MESH,
        )

    def send(d, carry):
        row_copy(lax.rem(me + d, owners), me).start()
        return carry

    lax.fori_loop(1, owners, send, 0)
    got[pl.ds(me, 1), :] = rows_ref[pl.ds(me, 1), :]
    scatter_finish_gather_start(lev_n, part_ref, pieces, reduced, sends, recvs, gsends, grecvs)

    def finish(d, carry):
        source = lax.rem(me + owners - d, owners)
        row_copy(lax.rem(me + d, owners), me).wait_send()
        row_copy(source, source).wait_recv()
        return carry

    lax.fori_loop(1, owners, finish, 0)
    gather_finish(lev_n, sum_out, reduced, gsends, grecvs)
    rows_out[...] = got[...]


def exchange(rows, part, collective_id):
    lev_n = lax.axis_size("lev")
    lat_n = lax.axis_size("lat")
    owners = lax.axis_size("lon") * lat_n
    vmem = pl.BlockSpec(memory_space=pltpu.VMEM)
    return pl.pallas_call(
        functools.partial(exchange_body, lev_n, owners, lat_n),
        out_shape=(
            jax.ShapeDtypeStruct(rows.shape, rows.dtype),
            jax.ShapeDtypeStruct(part.shape, part.dtype),
        ),
        in_specs=[vmem, vmem],
        out_specs=(vmem, vmem),
        scratch_shapes=[
            pltpu.VMEM(rows.shape, rows.dtype),
            pltpu.SemaphoreType.DMA((owners,)),
            pltpu.SemaphoreType.DMA((owners,)),
        ] + lev_scratch(lev_n, part.shape, part.dtype),
        compiler_params=pltpu.CompilerParams(
            collective_id=collective_id, has_side_effects=True
        ),
    )(rows, part)


def lev_direct_body(n, part_ref, out_ref, slots, send_sem, recv_sem):
    me = lax.axis_index("lev")
    barrier = pltpu.get_barrier_semaphore()
    for d in range(1, n):
        pl.semaphore_signal(
            barrier, inc=1, device_id={"lev": lax.rem(me + d, n)}, device_id_type=MESH
        )
    pl.semaphore_wait(barrier, n - 1)
    for d in range(1, n):
        lev_copy(part_ref, slots.at[me], send_sem.at[d - 1], recv_sem.at[me], lax.rem(me + d, n)).start()
    slots[me] = part_ref[...]
    for d in range(1, n):
        sender = lax.rem(me + n - d, n)
        lev_copy(part_ref, slots.at[sender], send_sem.at[d - 1], recv_sem.at[sender], sender).wait_recv()
        lev_copy(part_ref, slots.at[sender], send_sem.at[d - 1], recv_sem.at[sender], lax.rem(me + d, n)).wait_send()
    total = slots[0]
    for s in range(1, n):
        total = total + slots[s]
    out_ref[...] = total


def lev_direct(x, collective_id):
    n = lax.axis_size("lev")
    return pl.pallas_call(
        functools.partial(lev_direct_body, n),
        out_shape=jax.ShapeDtypeStruct(x.shape, x.dtype),
        in_specs=[pl.BlockSpec(memory_space=pltpu.VMEM)],
        out_specs=pl.BlockSpec(memory_space=pltpu.VMEM),
        scratch_shapes=[
            pltpu.VMEM((n,) + x.shape, x.dtype),
            pltpu.SemaphoreType.DMA((n - 1,)),
            pltpu.SemaphoreType.DMA((n,)),
        ],
        compiler_params=pltpu.CompilerParams(
            collective_id=collective_id, has_side_effects=True
        ),
    )(x)


def halo_places(lon_n, lat_n):
    lon = lax.axis_index("lon")
    lat = lax.axis_index("lat")
    half = lon_n // 2
    top = lat // (lat_n - 1)
    inner = (lat + lat_n - 1) // lat_n
    east = {"lon": lax.rem(lon + 1, lon_n)}
    west = {"lon": lax.rem(lon + lon_n - 1, lon_n)}
    up = {"lon": lax.rem(lon + half * top, lon_n), "lat": lat + 1 - top}
    down = {"lon": lax.rem(lon + half * (1 - inner), lon_n), "lat": lat - inner}
    return east, west, up, down, 1 - top, 1 - inner


def mix_halo_body(lev_n, lon_n, lat_n, p_ref, pc_ref, ar_ref, ac_ref, mr_ref, mc_ref, tr_ref, tc_ref,
                  cs_out, west_out, east_out, north_out, south_out,
                  pieces, reduced, sends, recvs, gsends, grecvs,
                  pc_slots, pc_send, pc_recv, colbuf, rowbuf, cols, rows, h_send, col_sem, row_sem):
    lev = lax.axis_index("lev")
    east, west, up, down, up_slot, down_slot = halo_places(lon_n, lat_n)
    barrier = pltpu.get_barrier_semaphore()
    for d in range(1, lev_n):
        pl.semaphore_signal(
            barrier, inc=1, device_id={"lev": lax.rem(lev + d, lev_n)}, device_id_type=MESH
        )
    for peer in (east, west, up, down):
        pl.semaphore_signal(barrier, inc=1, device_id=peer, device_id_type=MESH)
    pl.semaphore_wait(barrier, lev_n - 1 + 4)
    scatter_start(lev_n, p_ref, pieces, sends, recvs)
    for d in range(1, lev_n):
        lev_copy(pc_ref, pc_slots.at[lev], pc_send.at[d - 1], pc_recv.at[lev], lax.rem(lev + d, lev_n)).start()
    pc_slots[lev] = pc_ref[...]
    scatter_finish_gather_start(lev_n, p_ref, pieces, reduced, sends, recvs, gsends, grecvs)
    for d in range(1, lev_n):
        sender = lax.rem(lev + lev_n - d, lev_n)
        lev_copy(pc_ref, pc_slots.at[sender], pc_send.at[d - 1], pc_recv.at[sender], sender).wait_recv()
        lev_copy(pc_ref, pc_slots.at[sender], pc_send.at[d - 1], pc_recv.at[sender], lax.rem(lev + d, lev_n)).wait_send()
    pc_sum = pc_slots[0]
    for s in range(1, lev_n):
        pc_sum = pc_sum + pc_slots[s]
    gather_finish(lev_n, cs_out, reduced, gsends, grecvs)
    last_row = cs_out.shape[1] - 1
    for e, r in ((0, last_row), (1, 0)):
        cs_row = cs_out[:, r, :]
        m = mr_ref[e]
        rowbuf[e] = (1.0 - m) * ar_ref[e] + m * (cs_row[None] / tr_ref[e][None])
        mc = mc_ref[e]
        colbuf[e] = (1.0 - mc) * ac_ref[e] + mc * (pc_sum[e][None] / tc_ref[e][None])
    plan = (
        (colbuf.at[0], cols.at[0], col_sem.at[0], east),
        (colbuf.at[1], cols.at[1], col_sem.at[1], west),
        (rowbuf.at[0], rows.at[up_slot], row_sem.at[up_slot], up),
        (rowbuf.at[1], rows.at[down_slot], row_sem.at[down_slot], down),
    )
    copies = []
    for i, (src, dst, sem, peer) in enumerate(plan):
        copy = pltpu.make_async_remote_copy(
            src_ref=src, dst_ref=dst, send_sem=h_send.at[i], recv_sem=sem,
            device_id=peer, device_id_type=MESH,
        )
        copy.start()
        copies.append(copy)
    for src, dst, sem in (
        (colbuf.at[0], cols.at[0], col_sem.at[0]),
        (colbuf.at[1], cols.at[1], col_sem.at[1]),
        (rowbuf.at[0], rows.at[0], row_sem.at[0]),
        (rowbuf.at[1], rows.at[1], row_sem.at[1]),
    ):
        pltpu.make_async_remote_copy(
            src_ref=src, dst_ref=dst, send_sem=h_send.at[0], recv_sem=sem,
            device_id=east, device_id_type=MESH,
        ).wait_recv()
    for copy in copies:
        copy.wait_send()
    west_out[...] = cols[0]
    east_out[...] = cols[1]
    north_out[...] = rows[0]
    south_out[...] = rows[1]


def mix_halo(p, pc, ar, ac, mr, mc, tr, tc, collective_id):
    lev_n, lon_n, lat_n = lax.axis_size("lev"), lax.axis_size("lon"), lax.axis_size("lat")
    vmem = pl.BlockSpec(memory_space=pltpu.VMEM)
    col_shape, row_shape = ac.shape[1:], ar.shape[1:]
    return pl.pallas_call(
        functools.partial(mix_halo_body, lev_n, lon_n, lat_n),
        out_shape=(
            jax.ShapeDtypeStruct(p.shape, p.dtype),
            jax.ShapeDtypeStruct(col_shape, p.dtype),
            jax.ShapeDtypeStruct(col_shape, p.dtype),
            jax.ShapeDtypeStruct(row_shape, p.dtype),
            jax.ShapeDtypeStruct(row_shape, p.dtype),
        ),
        in_specs=[vmem] * 8,
        out_specs=(vmem,) * 5,
        scratch_shapes=lev_scratch(lev_n, p.shape, p.dtype) + [
            pltpu.VMEM((lev_n,) + pc.shape, p.dtype),
            pltpu.SemaphoreType.DMA((lev_n - 1,)),
            pltpu.SemaphoreType.DMA((lev_n,)),
            pltpu.VMEM(ac.shape, p.dtype),
            pltpu.VMEM(ar.shape, p.dtype),
            pltpu.VMEM(ac.shape, p.dtype),
            pltpu.VMEM(ar.shape, p.dtype),
            pltpu.SemaphoreType.DMA((4,)),
            pltpu.SemaphoreType.DMA((2,)),
            pltpu.SemaphoreType.DMA((2,)),
        ],
        compiler_params=pltpu.CompilerParams(
            collective_id=collective_id, has_side_effects=True
        ),
    )(p, pc, ar, ac, mr, mc, tr, tc)


def lev_sum(x, collective_id):
    n = lax.axis_size("lev")
    return pl.pallas_call(
        functools.partial(lev_sum_body, n),
        out_shape=jax.ShapeDtypeStruct(x.shape, x.dtype),
        in_specs=[pl.BlockSpec(memory_space=pltpu.VMEM)],
        out_specs=pl.BlockSpec(memory_space=pltpu.VMEM),
        scratch_shapes=lev_scratch(n, x.shape, x.dtype),
        compiler_params=pltpu.CompilerParams(
            collective_id=collective_id, has_side_effects=True
        ),
        cost_estimate=pl.CostEstimate(
            flops=n * x.size, bytes_accessed=(2 * n + 2) * x.size * 4, transcendentals=0
        ),
    )(x)


def from_behind(value, axis, steps):
    count = lax.axis_size(axis)
    pairs = [(source, (source + steps) % count) for source in range(count)]
    return lax.ppermute(value, axis, pairs)


def from_behind_2(block, axis, distance):
    devices = range(lax.axis_size(axis))
    route = [(i - distance, i) for i in devices if i - distance in devices]
    return lax.ppermute(block, axis, route)


def extended(x, sides, width, wrap):
    for axis, dim in sides:
        size, length = (lax.axis_size(axis), x.shape[dim])
        up = [(i, (i + 1) % size) for i in range(size if wrap else size - 1)]
        down = [(j, i) for i, j in up]
        last = lax.slice_in_dim(x, length - width, length, axis=dim)
        initial = lax.slice_in_dim(x, 0, width, axis=dim)
        before = lax.ppermute(last, axis, up)
        after = lax.ppermute(initial, axis, down)
        x = jnp.concatenate([before, x, after], axis=dim)
    return x


def mix_sum(partial_sum):
    return lax.psum(partial_sum, "lev")


def on_device(
    adjoint_field,
    east_courant,
    north_courant,
    pole_courant,
    mix_fraction,
    detrain_share,
    sounding_owner,
    sounding_cell,
    sounding_count,
    sounding_forcing,
):
    lon_count = lax.axis_size("lon")
    lat_count = lax.axis_size("lat")
    lat_place = lax.axis_index("lat")
    owner_self = lax.axis_index("lon") * lat_count + lat_place
    tracers, lev_dev, lat_rows, lon_cols = adjoint_field.shape
    step_count = sounding_forcing.shape[0]
    slot_count = sounding_forcing.shape[2]
    grid_cells = lat_rows * lon_cols
    detrain_part = jnp.sum(detrain_share, axis=0)
    owner_count = lon_count * lat_count
    cap = 4
    live_slots = jnp.arange(slot_count, dtype=jnp.int32)[None, :] < sounding_count
    values = jnp.where(live_slots[:, None, :], sounding_forcing, 0.0)
    owner_ids = sounding_owner[:, :, 0]
    slot_iota = jnp.arange(slot_count, dtype=jnp.int32)
    earlier = slot_iota[None, :, None] < slot_iota[None, None, :]
    same_owner = owner_ids[:, :, None] == owner_ids[:, None, :]
    rank = jnp.sum(jnp.logical_and(earlier, same_owner), axis=1, dtype=jnp.int32)
    position = owner_ids * cap + rank
    bucket_iota = jnp.arange(owner_count * cap, dtype=jnp.int32)
    chosen = position[:, :, None] == bucket_iota[None, None, :]
    bucket_values = jnp.sum(
        jnp.where(chosen[:, None, :, :], values[:, :, :, None], 0.0), axis=2
    )
    bucket_cell = jnp.max(
        jnp.where(chosen, sounding_cell[:, :, None] + 1, 0), axis=1
    ).astype(jnp.float32) - 1.0
    packed = jnp.concatenate([bucket_values, bucket_cell[:, None, :]], axis=1)
    packed = packed.reshape(step_count, lev_dev + 1, owner_count, cap)
    packed = jnp.transpose(packed, (2, 0, 1, 3))
    row_width = step_count * (lev_dev + 1) * cap
    rows = jnp.pad(packed.reshape(owner_count, row_width), ((0, 0), (0, 128 - row_width)))
    early_part = jnp.concatenate(
        [jnp.sum(detrain_share[None] * adjoint_field, axis=1), detrain_part[None]], axis=0
    )
    arrived, early = exchange(rows, early_part, 0)
    arrived = arrived[:, :row_width].reshape(owner_count, step_count, lev_dev + 1, cap)
    arrived = jnp.transpose(arrived, (1, 2, 0, 3)).reshape(
        step_count, lev_dev + 1, owner_count * cap
    )
    cells = arrived[:, lev_dev, :].astype(jnp.int32)
    row_hit = (cells // lon_cols)[:, :, None] == jnp.arange(lat_rows, dtype=jnp.int32)
    col_hit = (cells % lon_cols)[:, :, None] == jnp.arange(lon_cols, dtype=jnp.int32)
    spread = jnp.where(row_hit[:, None, :, :], arrived[:, :lev_dev, :, None], 0.0)
    forcing_grid = jnp.einsum(
        "tker,tec->tkrc", spread, col_hit.astype(jnp.float32), precision=lax.Precision.HIGHEST
    )
    row_index = jnp.arange(lat_rows, dtype=jnp.int32)[None, :, None]
    at_top = jnp.logical_and(lat_place == lat_count - 1, row_index == lat_rows - 1)
    at_bottom = jnp.logical_and(lat_place == 0, row_index == 0)
    upwind_east = jnp.maximum(east_courant, 0.0)
    forcing_part = jnp.sum(detrain_share * forcing_grid[step_count - 1], axis=0)
    forcing_sum = lev_direct(forcing_part[None], 4)[0]
    adjoint = adjoint_field
    for position in range(step_count):
        step_now = step_count - 1 - position
        adjoint = adjoint + forcing_grid[step_now][None]
        if position == 0:
            column_sum = early[:tracers] + forcing_sum[None]
            total_detrain = early[tracers]
        else:
            partial_sum = jnp.sum(detrain_share[None] * adjoint, axis=1)
            edge_cols = jnp.stack([partial_sum[:, :, -1], partial_sum[:, :, 0]])
            edge_a_rows = jnp.stack([adjoint[:, :, -1, :], adjoint[:, :, 0, :]]).transpose(0, 2, 1, 3)
            edge_a_cols = jnp.stack([adjoint[:, :, :, -1], adjoint[:, :, :, 0]]).transpose(0, 2, 1, 3)
            edge_m_rows = jnp.stack([mix_fraction[:, -1:, :], mix_fraction[:, :1, :]])
            edge_m_cols = jnp.stack([mix_fraction[:, :, -1], mix_fraction[:, :, 0]])[:, :, None, :]
            edge_t_rows = jnp.stack([total_detrain[-1:, :], total_detrain[:1, :]])
            edge_t_cols = jnp.stack([total_detrain[:, -1], total_detrain[:, 0]])[:, None, :]
            column_sum, west_k, east_k, north_k, south_k = mix_halo(
                partial_sum, edge_cols, edge_a_rows, edge_a_cols,
                edge_m_rows, edge_m_cols, edge_t_rows, edge_t_cols, 5,
            )
        adjoint = (1.0 - mix_fraction)[None] * adjoint + mix_fraction[None] * (
            column_sum / total_detrain
        )[:, None]
        if position == 1:
            west_halo = jnp.swapaxes(west_k, 0, 1).reshape(tracers * lev_dev, lat_rows)
            east_halo = jnp.swapaxes(east_k, 0, 1).reshape(tracers * lev_dev, lat_rows)
            north_halo = jnp.swapaxes(north_k, 0, 1).reshape(tracers * lev_dev, lon_cols)
            south_halo = jnp.swapaxes(south_k, 0, 1).reshape(tracers * lev_dev, lon_cols)
        planes = tracers * lev_dev
        if position == 0:
            col_last = adjoint[:, :, :, -1].reshape(planes, lat_rows)
            col_first = adjoint[:, :, :, 0].reshape(planes, lat_rows)
            row_last = adjoint[:, :, -1, :].reshape(planes, lon_cols)
            row_first = adjoint[:, :, 0, :].reshape(planes, lon_cols)
            if position == 0:
                col_last = jnp.concatenate([col_last, east_courant[:, :, -1]], axis=0)
                col_first = jnp.concatenate([col_first, east_courant[:, :, 0]], axis=0)
                row_last = jnp.concatenate([row_last, north_courant[:, -1, :]], axis=0)
                row_first = jnp.concatenate([row_first, pole_courant], axis=0)
            west_halo, east_halo, north_halo, south_halo = halo_swap(
                col_last, col_first, row_last, row_first, 2 + position
            )
            if position == 0:
                west_wind = jnp.concatenate(
                    [west_halo[planes:, :, None], east_courant[:, :, :-1]], axis=2
                )
                partner_top = north_halo[planes:]
                south_wind = jnp.concatenate(
                    [south_halo[planes:, None, :], north_courant[:, :-1, :]], axis=1
                )
                partner_pole = south_halo[planes:]
                upwind_west = -jnp.minimum(west_wind, 0.0)
                upwind_north = jnp.maximum(north_courant, 0.0) + jnp.where(
                    at_top, -jnp.minimum(partner_top, 0.0)[:, None, :], 0.0
                )
                upwind_south = jnp.where(
                    at_bottom,
                    (jnp.maximum(pole_courant, 0.0) - jnp.minimum(partner_pole, 0.0))[:, None, :],
                    -jnp.minimum(south_wind, 0.0),
                )
                west_halo, east_halo = west_halo[:planes], east_halo[:planes]
                north_halo, south_halo = north_halo[:planes], south_halo[:planes]
        east_side = jnp.concatenate(
            [adjoint[:, :, :, 1:], east_halo.reshape(tracers, lev_dev, lat_rows, 1)], axis=3
        )
        west_side = jnp.concatenate(
            [west_halo.reshape(tracers, lev_dev, lat_rows, 1), adjoint[:, :, :, :-1]], axis=3
        )
        north_side = jnp.concatenate(
            [adjoint[:, :, 1:, :], north_halo.reshape(tracers, lev_dev, 1, lon_cols)], axis=2
        )
        south_side = jnp.concatenate(
            [south_halo.reshape(tracers, lev_dev, 1, lon_cols), adjoint[:, :, :-1, :]], axis=2
        )
        adjoint = (
            adjoint
            + upwind_east * (east_side - adjoint)
            + upwind_west * (west_side - adjoint)
            + upwind_north * (north_side - adjoint)
            + upwind_south * (south_side - adjoint)
        )
    return adjoint


def solution(mesh):
    return jax.shard_map(
        on_device,
        mesh=mesh,
        in_specs=(
            P(None, "lev", "lat", "lon"),
            P("lev", "lat", "lon"),
            P("lev", "lat", "lon"),
            P("lev", "lon"),
            P("lev", "lat", "lon"),
            P("lev", "lat", "lon"),
            P(None, ("lon", "lat"), None),
            P(None, ("lon", "lat")),
            P(None, ("lon", "lat")),
            P(None, "lev", ("lon", "lat")),
        ),
        out_specs=P(None, "lev", "lat", "lon"),
        check_vma=False,
    )
```

```python
import functools

import jax
import jax.numpy as jnp
from jax import lax
from jax.experimental import pallas as pl
from jax.experimental.pallas import tpu as pltpu
from jax.sharding import PartitionSpec as P

MESH = pl.DeviceIdType.MESH


def lev_sum_body(n, part_ref, out_ref, pieces, reduced, sends, recvs, gsends, grecvs):
    lev = lax.axis_index("lev")
    barrier = pltpu.get_barrier_semaphore()
    for d in range(1, n):
        pl.semaphore_signal(
            barrier, inc=1, device_id={"lev": lax.rem(lev + d, n)}, device_id_type=MESH
        )
    pl.semaphore_wait(barrier, n - 1)
    scatter_start(n, part_ref, pieces, sends, recvs)
    scatter_finish_gather_start(n, part_ref, pieces, reduced, sends, recvs, gsends, grecvs)
    gather_finish(n, out_ref, reduced, gsends, grecvs)


def halo_body(lon_n, lat_n, col_last, col_first, row_last, row_first,
              west_out, east_out, north_out, south_out, cols, rows, send_sem, col_sem, row_sem):
    lon = lax.axis_index("lon")
    lat = lax.axis_index("lat")
    half = lon_n // 2
    top = lat // (lat_n - 1)
    inner = (lat + lat_n - 1) // lat_n
    east = {"lon": lax.rem(lon + 1, lon_n)}
    west = {"lon": lax.rem(lon + lon_n - 1, lon_n)}
    up = {"lon": lax.rem(lon + half * top, lon_n), "lat": lat + 1 - top}
    down = {"lon": lax.rem(lon + half * (1 - inner), lon_n), "lat": lat - inner}
    up_slot = 1 - top
    down_slot = 1 - inner
    barrier = pltpu.get_barrier_semaphore()
    for peer in (east, west, up, down):
        pl.semaphore_signal(barrier, inc=1, device_id=peer, device_id_type=MESH)
    pl.semaphore_wait(barrier, 4)
    plan = (
        (col_last, cols.at[0], col_sem.at[0], east),
        (col_first, cols.at[1], col_sem.at[1], west),
        (row_last, rows.at[up_slot], row_sem.at[up_slot], up),
        (row_first, rows.at[down_slot], row_sem.at[down_slot], down),
    )
    sends = []
    for i, (src, dst, sem, peer) in enumerate(plan):
        copy = pltpu.make_async_remote_copy(
            src_ref=src, dst_ref=dst, send_sem=send_sem.at[i], recv_sem=sem,
            device_id=peer, device_id_type=MESH,
        )
        copy.start()
        sends.append(copy)
    arrivals = (
        (col_last, cols.at[0], col_sem.at[0]),
        (col_first, cols.at[1], col_sem.at[1]),
        (row_last, rows.at[0], row_sem.at[0]),
        (row_first, rows.at[1], row_sem.at[1]),
    )
    for src, dst, sem in arrivals:
        pltpu.make_async_remote_copy(
            src_ref=src, dst_ref=dst, send_sem=send_sem.at[0], recv_sem=sem,
            device_id=east, device_id_type=MESH,
        ).wait_recv()
    for copy in sends:
        copy.wait_send()
    west_out[...] = cols[0]
    east_out[...] = cols[1]
    north_out[...] = rows[0]
    south_out[...] = rows[1]


def halo_swap(col_last, col_first, row_last, row_first, collective_id):
    lon_n, lat_n = lax.axis_size("lon"), lax.axis_size("lat")
    vmem = pl.BlockSpec(memory_space=pltpu.VMEM)
    return pl.pallas_call(
        functools.partial(halo_body, lon_n, lat_n),
        out_shape=(
            jax.ShapeDtypeStruct(col_last.shape, col_last.dtype),
            jax.ShapeDtypeStruct(col_last.shape, col_last.dtype),
            jax.ShapeDtypeStruct(row_last.shape, row_last.dtype),
            jax.ShapeDtypeStruct(row_last.shape, row_last.dtype),
        ),
        in_specs=[vmem] * 4,
        out_specs=(vmem,) * 4,
        scratch_shapes=[
            pltpu.VMEM((2,) + col_last.shape, col_last.dtype),
            pltpu.VMEM((2,) + row_last.shape, row_last.dtype),
            pltpu.SemaphoreType.DMA((4,)),
            pltpu.SemaphoreType.DMA((2,)),
            pltpu.SemaphoreType.DMA((2,)),
        ],
        compiler_params=pltpu.CompilerParams(
            collective_id=collective_id, has_side_effects=True
        ),
    )(col_last, col_first, row_last, row_first)


def lev_copy(src, dst, send, recv, peer):
    return pltpu.make_async_remote_copy(
        src_ref=src, dst_ref=dst, send_sem=send, recv_sem=recv,
        device_id={"lev": peer}, device_id_type=MESH,
    )


def scatter_start(n, part_ref, pieces, sends, recvs):
    lev = lax.axis_index("lev")
    rows = part_ref.shape[1] // n
    for d in range(1, n):
        peer = lax.rem(lev + d, n)
        lev_copy(
            part_ref.at[:, pl.ds(pl.multiple_of(peer * rows, rows), rows), :],
            pieces.at[lev], sends.at[d - 1], recvs.at[lev], peer,
        ).start()
    pieces[lev] = part_ref[:, pl.ds(pl.multiple_of(lev * rows, rows), rows), :]


def scatter_finish_gather_start(n, part_ref, pieces, reduced, sends, recvs, gsends, grecvs):
    lev = lax.axis_index("lev")
    rows = part_ref.shape[1] // n
    for d in range(1, n):
        sender = lax.rem(lev + n - d, n)
        peer = lax.rem(lev + d, n)
        lev_copy(
            part_ref.at[:, pl.ds(0, rows), :], pieces.at[sender],
            sends.at[d - 1], recvs.at[sender], sender,
        ).wait_recv()
        lev_copy(
            part_ref.at[:, pl.ds(0, rows), :], pieces.at[sender],
            sends.at[d - 1], recvs.at[sender], peer,
        ).wait_send()
    total = pieces[0]
    for s in range(1, n):
        total = total + pieces[s]
    reduced[lev] = total
    for d in range(1, n):
        peer = lax.rem(lev + d, n)
        lev_copy(reduced.at[lev], reduced.at[lev], gsends.at[d - 1], grecvs.at[lev], peer).start()


def gather_finish(n, out_ref, reduced, gsends, grecvs):
    lev = lax.axis_index("lev")
    rows = out_ref.shape[1] // n
    for d in range(1, n):
        sender = lax.rem(lev + n - d, n)
        lev_copy(reduced.at[sender], reduced.at[sender], gsends.at[d - 1], grecvs.at[sender], sender).wait_recv()
        lev_copy(reduced.at[lev], reduced.at[lev], gsends.at[d - 1], grecvs.at[lev], lax.rem(lev + d, n)).wait_send()
    for q in range(n):
        out_ref[:, q * rows:(q + 1) * rows, :] = reduced[q]


def lev_scratch(n, shape, dtype):
    piece = (shape[0], shape[1] // n, shape[2])
    return [
        pltpu.VMEM((n,) + piece, dtype),
        pltpu.VMEM((n,) + piece, dtype),
        pltpu.SemaphoreType.DMA((n - 1,)),
        pltpu.SemaphoreType.DMA((n,)),
        pltpu.SemaphoreType.DMA((n - 1,)),
        pltpu.SemaphoreType.DMA((n,)),
    ]


def exchange_body(lev_n, owners, lat_n, rows_ref, part_ref, rows_out, sum_out,
                  got, row_send, row_recv, pieces, reduced, sends, recvs, gsends, grecvs):
    lat = lax.axis_index("lat")
    lev = lax.axis_index("lev")
    me = lax.axis_index("lon") * lat_n + lat

    def place(peer):
        return {"lon": peer // lat_n, "lat": lax.rem(peer, lat_n)}

    barrier = pltpu.get_barrier_semaphore()

    def greet(d, carry):
        peer = lax.rem(me + d, owners)
        pl.semaphore_signal(barrier, inc=1, device_id=place(peer), device_id_type=MESH)
        return carry

    lax.fori_loop(1, owners, greet, 0)
    for d in range(1, lev_n):
        pl.semaphore_signal(
            barrier, inc=1, device_id={"lev": lax.rem(lev + d, lev_n)}, device_id_type=MESH
        )
    pl.semaphore_wait(barrier, owners - 1 + lev_n - 1)
    scatter_start(lev_n, part_ref, pieces, sends, recvs)

    def row_copy(peer, target):
        return pltpu.make_async_remote_copy(
            src_ref=rows_ref.at[pl.ds(peer, 1)],
            dst_ref=got.at[pl.ds(target, 1)],
            send_sem=row_send.at[peer],
            recv_sem=row_recv.at[target],
            device_id=place(peer),
            device_id_type=MESH,
        )

    def send(d, carry):
        row_copy(lax.rem(me + d, owners), me).start()
        return carry

    lax.fori_loop(1, owners, send, 0)
    got[pl.ds(me, 1), :] = rows_ref[pl.ds(me, 1), :]
    scatter_finish_gather_start(lev_n, part_ref, pieces, reduced, sends, recvs, gsends, grecvs)

    def finish(d, carry):
        source = lax.rem(me + owners - d, owners)
        row_copy(lax.rem(me + d, owners), me).wait_send()
        row_copy(source, source).wait_recv()
        return carry

    lax.fori_loop(1, owners, finish, 0)
    gather_finish(lev_n, sum_out, reduced, gsends, grecvs)
    rows_out[...] = got[...]


def exchange(rows, part, collective_id):
    lev_n = lax.axis_size("lev")
    lat_n = lax.axis_size("lat")
    owners = lax.axis_size("lon") * lat_n
    vmem = pl.BlockSpec(memory_space=pltpu.VMEM)
    return pl.pallas_call(
        functools.partial(exchange_body, lev_n, owners, lat_n),
        out_shape=(
            jax.ShapeDtypeStruct(rows.shape, rows.dtype),
            jax.ShapeDtypeStruct(part.shape, part.dtype),
        ),
        in_specs=[vmem, vmem],
        out_specs=(vmem, vmem),
        scratch_shapes=[
            pltpu.VMEM(rows.shape, rows.dtype),
            pltpu.SemaphoreType.DMA((owners,)),
            pltpu.SemaphoreType.DMA((owners,)),
        ] + lev_scratch(lev_n, part.shape, part.dtype),
        compiler_params=pltpu.CompilerParams(
            collective_id=collective_id, has_side_effects=True
        ),
    )(rows, part)


def lev_direct_body(n, part_ref, out_ref, slots, send_sem, recv_sem):
    me = lax.axis_index("lev")
    barrier = pltpu.get_barrier_semaphore()
    for d in range(1, n):
        pl.semaphore_signal(
            barrier, inc=1, device_id={"lev": lax.rem(me + d, n)}, device_id_type=MESH
        )
    pl.semaphore_wait(barrier, n - 1)
    for d in range(1, n):
        lev_copy(part_ref, slots.at[me], send_sem.at[d - 1], recv_sem.at[me], lax.rem(me + d, n)).start()
    slots[me] = part_ref[...]
    for d in range(1, n):
        sender = lax.rem(me + n - d, n)
        lev_copy(part_ref, slots.at[sender], send_sem.at[d - 1], recv_sem.at[sender], sender).wait_recv()
        lev_copy(part_ref, slots.at[sender], send_sem.at[d - 1], recv_sem.at[sender], lax.rem(me + d, n)).wait_send()
    total = slots[0]
    for s in range(1, n):
        total = total + slots[s]
    out_ref[...] = total


def lev_direct(x, collective_id):
    n = lax.axis_size("lev")
    return pl.pallas_call(
        functools.partial(lev_direct_body, n),
        out_shape=jax.ShapeDtypeStruct(x.shape, x.dtype),
        in_specs=[pl.BlockSpec(memory_space=pltpu.VMEM)],
        out_specs=pl.BlockSpec(memory_space=pltpu.VMEM),
        scratch_shapes=[
            pltpu.VMEM((n,) + x.shape, x.dtype),
            pltpu.SemaphoreType.DMA((n - 1,)),
            pltpu.SemaphoreType.DMA((n,)),
        ],
        compiler_params=pltpu.CompilerParams(
            collective_id=collective_id, has_side_effects=True
        ),
    )(x)


def halo_places(lon_n, lat_n):
    lon = lax.axis_index("lon")
    lat = lax.axis_index("lat")
    half = lon_n // 2
    top = lat // (lat_n - 1)
    inner = (lat + lat_n - 1) // lat_n
    east = {"lon": lax.rem(lon + 1, lon_n)}
    west = {"lon": lax.rem(lon + lon_n - 1, lon_n)}
    up = {"lon": lax.rem(lon + half * top, lon_n), "lat": lat + 1 - top}
    down = {"lon": lax.rem(lon + half * (1 - inner), lon_n), "lat": lat - inner}
    return east, west, up, down, 1 - top, 1 - inner


def mix_halo_body(lev_n, lon_n, lat_n, p_ref, pe_ref, ae_ref, me_ref, te_ref, cs_out, halo_out,
                  pieces, reduced, sends, recvs, gsends, grecvs,
                  pe_slots, pe_send, pe_recv, mixed, got, h_send, h_recv):
    lev = lax.axis_index("lev")
    east, west, up, down, up_slot, down_slot = halo_places(lon_n, lat_n)
    barrier = pltpu.get_barrier_semaphore()
    for d in range(1, lev_n):
        pl.semaphore_signal(
            barrier, inc=1, device_id={"lev": lax.rem(lev + d, lev_n)}, device_id_type=MESH
        )
    for peer in (east, west, up, down):
        pl.semaphore_signal(barrier, inc=1, device_id=peer, device_id_type=MESH)
    pl.semaphore_wait(barrier, lev_n - 1 + 4)
    scatter_start(lev_n, p_ref, pieces, sends, recvs)
    for d in range(1, lev_n):
        lev_copy(pe_ref, pe_slots.at[lev], pe_send.at[d - 1], pe_recv.at[lev], lax.rem(lev + d, lev_n)).start()
    pe_slots[lev] = pe_ref[...]
    scatter_finish_gather_start(lev_n, p_ref, pieces, reduced, sends, recvs, gsends, grecvs)
    for d in range(1, lev_n):
        sender = lax.rem(lev + lev_n - d, lev_n)
        lev_copy(pe_ref, pe_slots.at[sender], pe_send.at[d - 1], pe_recv.at[sender], sender).wait_recv()
        lev_copy(pe_ref, pe_slots.at[sender], pe_send.at[d - 1], pe_recv.at[sender], lax.rem(lev + d, lev_n)).wait_send()
    pe_sum = pe_slots[0]
    for s in range(1, lev_n):
        pe_sum = pe_sum + pe_slots[s]
    share = me_ref[...]
    mixed[...] = (1.0 - share) * ae_ref[...] + share * (pe_sum / te_ref[...])
    plan = (
        (mixed.at[0], got.at[0], h_recv.at[0], east),
        (mixed.at[1], got.at[1], h_recv.at[1], west),
        (mixed.at[2], got.at[2 + up_slot], h_recv.at[2 + up_slot], up),
        (mixed.at[3], got.at[2 + down_slot], h_recv.at[2 + down_slot], down),
    )
    copies = []
    for i, (src, dst, sem, peer) in enumerate(plan):
        copy = pltpu.make_async_remote_copy(
            src_ref=src, dst_ref=dst, send_sem=h_send.at[i], recv_sem=sem,
            device_id=peer, device_id_type=MESH,
        )
        copy.start()
        copies.append(copy)
    gather_finish(lev_n, cs_out, reduced, gsends, grecvs)
    for i in range(4):
        pltpu.make_async_remote_copy(
            src_ref=mixed.at[i], dst_ref=got.at[i], send_sem=h_send.at[i], recv_sem=h_recv.at[i],
            device_id=east, device_id_type=MESH,
        ).wait_recv()
    for copy in copies:
        copy.wait_send()
    halo_out[...] = got[...]


def mix_halo(p, pe, ae, me, te, collective_id):
    lev_n, lon_n, lat_n = lax.axis_size("lev"), lax.axis_size("lon"), lax.axis_size("lat")
    vmem = pl.BlockSpec(memory_space=pltpu.VMEM)
    return pl.pallas_call(
        functools.partial(mix_halo_body, lev_n, lon_n, lat_n),
        out_shape=(
            jax.ShapeDtypeStruct(p.shape, p.dtype),
            jax.ShapeDtypeStruct(pe.shape, p.dtype),
        ),
        in_specs=[vmem] * 5,
        out_specs=(vmem, vmem),
        scratch_shapes=lev_scratch(lev_n, p.shape, p.dtype) + [
            pltpu.VMEM((lev_n,) + pe.shape, p.dtype),
            pltpu.SemaphoreType.DMA((lev_n - 1,)),
            pltpu.SemaphoreType.DMA((lev_n,)),
            pltpu.VMEM(pe.shape, p.dtype),
            pltpu.VMEM(pe.shape, p.dtype),
            pltpu.SemaphoreType.DMA((4,)),
            pltpu.SemaphoreType.DMA((4,)),
        ],
        compiler_params=pltpu.CompilerParams(
            collective_id=collective_id, has_side_effects=True
        ),
    )(p, pe, ae, me, te)


def lev_sum(x, collective_id):
    n = lax.axis_size("lev")
    return pl.pallas_call(
        functools.partial(lev_sum_body, n),
        out_shape=jax.ShapeDtypeStruct(x.shape, x.dtype),
        in_specs=[pl.BlockSpec(memory_space=pltpu.VMEM)],
        out_specs=pl.BlockSpec(memory_space=pltpu.VMEM),
        scratch_shapes=lev_scratch(n, x.shape, x.dtype),
        compiler_params=pltpu.CompilerParams(
            collective_id=collective_id, has_side_effects=True
        ),
        cost_estimate=pl.CostEstimate(
            flops=n * x.size, bytes_accessed=(2 * n + 2) * x.size * 4, transcendentals=0
        ),
    )(x)


def from_behind(value, axis, steps):
    count = lax.axis_size(axis)
    pairs = [(source, (source + steps) % count) for source in range(count)]
    return lax.ppermute(value, axis, pairs)


def from_behind_2(block, axis, distance):
    devices = range(lax.axis_size(axis))
    route = [(i - distance, i) for i in devices if i - distance in devices]
    return lax.ppermute(block, axis, route)


def extended(x, sides, width, wrap):
    for axis, dim in sides:
        size, length = (lax.axis_size(axis), x.shape[dim])
        up = [(i, (i + 1) % size) for i in range(size if wrap else size - 1)]
        down = [(j, i) for i, j in up]
        last = lax.slice_in_dim(x, length - width, length, axis=dim)
        initial = lax.slice_in_dim(x, 0, width, axis=dim)
        before = lax.ppermute(last, axis, up)
        after = lax.ppermute(initial, axis, down)
        x = jnp.concatenate([before, x, after], axis=dim)
    return x


def mix_sum(partial_sum):
    return lax.psum(partial_sum, "lev")


def on_device(
    adjoint_field,
    east_courant,
    north_courant,
    pole_courant,
    mix_fraction,
    detrain_share,
    sounding_owner,
    sounding_cell,
    sounding_count,
    sounding_forcing,
):
    lon_count = lax.axis_size("lon")
    lat_count = lax.axis_size("lat")
    lat_place = lax.axis_index("lat")
    owner_self = lax.axis_index("lon") * lat_count + lat_place
    tracers, lev_dev, lat_rows, lon_cols = adjoint_field.shape
    step_count = sounding_forcing.shape[0]
    slot_count = sounding_forcing.shape[2]
    grid_cells = lat_rows * lon_cols
    detrain_part = jnp.sum(detrain_share, axis=0)
    owner_count = lon_count * lat_count
    cap = 4
    live_slots = jnp.arange(slot_count, dtype=jnp.int32)[None, :] < sounding_count
    values = jnp.where(live_slots[:, None, :], sounding_forcing, 0.0)
    owner_ids = sounding_owner[:, :, 0]
    slot_iota = jnp.arange(slot_count, dtype=jnp.int32)
    earlier = slot_iota[None, :, None] < slot_iota[None, None, :]
    same_owner = owner_ids[:, :, None] == owner_ids[:, None, :]
    rank = jnp.sum(jnp.logical_and(earlier, same_owner), axis=1, dtype=jnp.int32)
    position = owner_ids * cap + rank
    bucket_iota = jnp.arange(owner_count * cap, dtype=jnp.int32)
    chosen = position[:, :, None] == bucket_iota[None, None, :]
    bucket_values = jnp.sum(
        jnp.where(chosen[:, None, :, :], values[:, :, :, None], 0.0), axis=2
    )
    bucket_cell = jnp.max(
        jnp.where(chosen, sounding_cell[:, :, None] + 1, 0), axis=1
    ).astype(jnp.float32) - 1.0
    packed = jnp.concatenate([bucket_values, bucket_cell[:, None, :]], axis=1)
    packed = packed.reshape(step_count, lev_dev + 1, owner_count, cap)
    packed = jnp.transpose(packed, (2, 0, 1, 3))
    row_width = step_count * (lev_dev + 1) * cap
    rows = jnp.pad(packed.reshape(owner_count, row_width), ((0, 0), (0, 128 - row_width)))
    early_part = jnp.concatenate(
        [jnp.sum(detrain_share[None] * adjoint_field, axis=1), detrain_part[None]], axis=0
    )
    arrived, early = exchange(rows, early_part, 0)
    arrived = arrived[:, :row_width].reshape(owner_count, step_count, lev_dev + 1, cap)
    arrived = jnp.transpose(arrived, (1, 2, 0, 3)).reshape(
        step_count, lev_dev + 1, owner_count * cap
    )
    cells = arrived[:, lev_dev, :].astype(jnp.int32)
    row_hit = (cells // lon_cols)[:, :, None] == jnp.arange(lat_rows, dtype=jnp.int32)
    col_hit = (cells % lon_cols)[:, :, None] == jnp.arange(lon_cols, dtype=jnp.int32)
    spread = jnp.where(row_hit[:, None, :, :], arrived[:, :lev_dev, :, None], 0.0)
    forcing_grid = jnp.einsum(
        "tker,tec->tkrc", spread, col_hit.astype(jnp.float32), precision=lax.Precision.HIGHEST
    )
    row_index = jnp.arange(lat_rows, dtype=jnp.int32)[None, :, None]
    at_top = jnp.logical_and(lat_place == lat_count - 1, row_index == lat_rows - 1)
    at_bottom = jnp.logical_and(lat_place == 0, row_index == 0)
    upwind_east = jnp.maximum(east_courant, 0.0)
    forcing_part = jnp.sum(detrain_share * forcing_grid[step_count - 1], axis=0)
    forcing_sum = lev_direct(forcing_part[None], 4)[0]
    adjoint = adjoint_field
    for position in range(step_count):
        step_now = step_count - 1 - position
        adjoint = adjoint + forcing_grid[step_now][None]
        if position == 0:
            column_sum = early[:tracers] + forcing_sum[None]
            total_detrain = early[tracers]
        else:
            partial_sum = jnp.sum(detrain_share[None] * adjoint, axis=1)
            planes = tracers * lev_dev

            def spread(x, width, fill=0.0):
                x = jnp.broadcast_to(x, (tracers, lev_dev, width)).reshape(planes, width)
                return jnp.pad(x, ((0, 0), (0, lon_cols - width)), constant_values=fill)

            def edges(x, fill=0.0):
                return jnp.stack([
                    spread(x[..., :, -1], lat_rows, fill), spread(x[..., :, 0], lat_rows, fill),
                    spread(x[..., -1, :], lon_cols), spread(x[..., 0, :], lon_cols),
                ])

            column_sum, halos = mix_halo(
                partial_sum,
                edges(partial_sum[:, None]),
                edges(adjoint),
                edges(mix_fraction[None]),
                edges(total_detrain[None, None], 1.0),
                5,
            )
        adjoint = (1.0 - mix_fraction)[None] * adjoint + mix_fraction[None] * (
            column_sum / total_detrain
        )[:, None]
        if position == 1:
            west_halo = halos[0, :, :lat_rows]
            east_halo = halos[1, :, :lat_rows]
            north_halo = halos[2]
            south_halo = halos[3]
        planes = tracers * lev_dev
        if position == 0:
            col_last = adjoint[:, :, :, -1].reshape(planes, lat_rows)
            col_first = adjoint[:, :, :, 0].reshape(planes, lat_rows)
            row_last = adjoint[:, :, -1, :].reshape(planes, lon_cols)
            row_first = adjoint[:, :, 0, :].reshape(planes, lon_cols)
            if position == 0:
                col_last = jnp.concatenate([col_last, east_courant[:, :, -1]], axis=0)
                col_first = jnp.concatenate([col_first, east_courant[:, :, 0]], axis=0)
                row_last = jnp.concatenate([row_last, north_courant[:, -1, :]], axis=0)
                row_first = jnp.concatenate([row_first, pole_courant], axis=0)
            west_halo, east_halo, north_halo, south_halo = halo_swap(
                col_last, col_first, row_last, row_first, 2 + position
            )
            if position == 0:
                west_wind = jnp.concatenate(
                    [west_halo[planes:, :, None], east_courant[:, :, :-1]], axis=2
                )
                partner_top = north_halo[planes:]
                south_wind = jnp.concatenate(
                    [south_halo[planes:, None, :], north_courant[:, :-1, :]], axis=1
                )
                partner_pole = south_halo[planes:]
                upwind_west = -jnp.minimum(west_wind, 0.0)
                upwind_north = jnp.maximum(north_courant, 0.0) + jnp.where(
                    at_top, -jnp.minimum(partner_top, 0.0)[:, None, :], 0.0
                )
                upwind_south = jnp.where(
                    at_bottom,
                    (jnp.maximum(pole_courant, 0.0) - jnp.minimum(partner_pole, 0.0))[:, None, :],
                    -jnp.minimum(south_wind, 0.0),
                )
                west_halo, east_halo = west_halo[:planes], east_halo[:planes]
                north_halo, south_halo = north_halo[:planes], south_halo[:planes]
        east_side = jnp.concatenate(
            [adjoint[:, :, :, 1:], east_halo.reshape(tracers, lev_dev, lat_rows, 1)], axis=3
        )
        west_side = jnp.concatenate(
            [west_halo.reshape(tracers, lev_dev, lat_rows, 1), adjoint[:, :, :, :-1]], axis=3
        )
        north_side = jnp.concatenate(
            [adjoint[:, :, 1:, :], north_halo.reshape(tracers, lev_dev, 1, lon_cols)], axis=2
        )
        south_side = jnp.concatenate(
            [south_halo.reshape(tracers, lev_dev, 1, lon_cols), adjoint[:, :, :-1, :]], axis=2
        )
        adjoint = (
            adjoint
            + upwind_east * (east_side - adjoint)
            + upwind_west * (west_side - adjoint)
            + upwind_north * (north_side - adjoint)
            + upwind_south * (south_side - adjoint)
        )
    return adjoint


def solution(mesh):
    return jax.shard_map(
        on_device,
        mesh=mesh,
        in_specs=(
            P(None, "lev", "lat", "lon"),
            P("lev", "lat", "lon"),
            P("lev", "lat", "lon"),
            P("lev", "lon"),
            P("lev", "lat", "lon"),
            P("lev", "lat", "lon"),
            P(None, ("lon", "lat"), None),
            P(None, ("lon", "lat")),
            P(None, ("lon", "lat")),
            P(None, "lev", ("lon", "lat")),
        ),
        out_specs=P(None, "lev", "lat", "lon"),
        check_vma=False,
    )
```

```python
import functools

import jax
import jax.numpy as jnp
from jax import lax
from jax.experimental import pallas as pl
from jax.experimental.pallas import tpu as pltpu
from jax.sharding import PartitionSpec as P

MESH = pl.DeviceIdType.MESH


def lev_sum_body(n, part_ref, out_ref, pieces, reduced, sends, recvs, gsends, grecvs):
    lev = lax.axis_index("lev")
    barrier = pltpu.get_barrier_semaphore()
    for d in range(1, n):
        pl.semaphore_signal(
            barrier, inc=1, device_id={"lev": lax.rem(lev + d, n)}, device_id_type=MESH
        )
    pl.semaphore_wait(barrier, n - 1)
    scatter_start(n, part_ref, pieces, sends, recvs)
    scatter_finish_gather_start(n, part_ref, pieces, reduced, sends, recvs, gsends, grecvs)
    gather_finish(n, out_ref, reduced, gsends, grecvs)


def halo_body(lon_n, lat_n, col_last, col_first, row_last, row_first,
              west_out, east_out, north_out, south_out, cols, rows, send_sem, col_sem, row_sem):
    lon = lax.axis_index("lon")
    lat = lax.axis_index("lat")
    half = lon_n // 2
    top = lat // (lat_n - 1)
    inner = (lat + lat_n - 1) // lat_n
    east = {"lon": lax.rem(lon + 1, lon_n)}
    west = {"lon": lax.rem(lon + lon_n - 1, lon_n)}
    up = {"lon": lax.rem(lon + half * top, lon_n), "lat": lat + 1 - top}
    down = {"lon": lax.rem(lon + half * (1 - inner), lon_n), "lat": lat - inner}
    up_slot = 1 - top
    down_slot = 1 - inner
    barrier = pltpu.get_barrier_semaphore()
    for peer in (east, west, up, down):
        pl.semaphore_signal(barrier, inc=1, device_id=peer, device_id_type=MESH)
    pl.semaphore_wait(barrier, 4)
    plan = (
        (col_last, cols.at[0], col_sem.at[0], east),
        (col_first, cols.at[1], col_sem.at[1], west),
        (row_last, rows.at[up_slot], row_sem.at[up_slot], up),
        (row_first, rows.at[down_slot], row_sem.at[down_slot], down),
    )
    sends = []
    for i, (src, dst, sem, peer) in enumerate(plan):
        copy = pltpu.make_async_remote_copy(
            src_ref=src, dst_ref=dst, send_sem=send_sem.at[i], recv_sem=sem,
            device_id=peer, device_id_type=MESH,
        )
        copy.start()
        sends.append(copy)
    arrivals = (
        (col_last, cols.at[0], col_sem.at[0]),
        (col_first, cols.at[1], col_sem.at[1]),
        (row_last, rows.at[0], row_sem.at[0]),
        (row_first, rows.at[1], row_sem.at[1]),
    )
    for src, dst, sem in arrivals:
        pltpu.make_async_remote_copy(
            src_ref=src, dst_ref=dst, send_sem=send_sem.at[0], recv_sem=sem,
            device_id=east, device_id_type=MESH,
        ).wait_recv()
    for copy in sends:
        copy.wait_send()
    west_out[...] = cols[0]
    east_out[...] = cols[1]
    north_out[...] = rows[0]
    south_out[...] = rows[1]


def halo_swap(col_last, col_first, row_last, row_first, collective_id):
    lon_n, lat_n = lax.axis_size("lon"), lax.axis_size("lat")
    vmem = pl.BlockSpec(memory_space=pltpu.VMEM)
    return pl.pallas_call(
        functools.partial(halo_body, lon_n, lat_n),
        out_shape=(
            jax.ShapeDtypeStruct(col_last.shape, col_last.dtype),
            jax.ShapeDtypeStruct(col_last.shape, col_last.dtype),
            jax.ShapeDtypeStruct(row_last.shape, row_last.dtype),
            jax.ShapeDtypeStruct(row_last.shape, row_last.dtype),
        ),
        in_specs=[vmem] * 4,
        out_specs=(vmem,) * 4,
        scratch_shapes=[
            pltpu.VMEM((2,) + col_last.shape, col_last.dtype),
            pltpu.VMEM((2,) + row_last.shape, row_last.dtype),
            pltpu.SemaphoreType.DMA((4,)),
            pltpu.SemaphoreType.DMA((2,)),
            pltpu.SemaphoreType.DMA((2,)),
        ],
        compiler_params=pltpu.CompilerParams(
            collective_id=collective_id, has_side_effects=True
        ),
    )(col_last, col_first, row_last, row_first)


def lev_copy(src, dst, send, recv, peer):
    return pltpu.make_async_remote_copy(
        src_ref=src, dst_ref=dst, send_sem=send, recv_sem=recv,
        device_id={"lev": peer}, device_id_type=MESH,
    )


def scatter_start(n, part_ref, pieces, sends, recvs):
    lev = lax.axis_index("lev")
    rows = part_ref.shape[1] // n
    for d in range(1, n):
        peer = lax.rem(lev + d, n)
        lev_copy(
            part_ref.at[:, pl.ds(pl.multiple_of(peer * rows, rows), rows), :],
            pieces.at[lev], sends.at[d - 1], recvs.at[lev], peer,
        ).start()
    pieces[lev] = part_ref[:, pl.ds(pl.multiple_of(lev * rows, rows), rows), :]


def scatter_finish_gather_start(n, part_ref, pieces, reduced, sends, recvs, gsends, grecvs):
    lev = lax.axis_index("lev")
    rows = part_ref.shape[1] // n
    for d in range(1, n):
        sender = lax.rem(lev + n - d, n)
        peer = lax.rem(lev + d, n)
        lev_copy(
            part_ref.at[:, pl.ds(0, rows), :], pieces.at[sender],
            sends.at[d - 1], recvs.at[sender], sender,
        ).wait_recv()
        lev_copy(
            part_ref.at[:, pl.ds(0, rows), :], pieces.at[sender],
            sends.at[d - 1], recvs.at[sender], peer,
        ).wait_send()
    total = pieces[0]
    for s in range(1, n):
        total = total + pieces[s]
    reduced[lev] = total
    for d in range(1, n):
        peer = lax.rem(lev + d, n)
        lev_copy(reduced.at[lev], reduced.at[lev], gsends.at[d - 1], grecvs.at[lev], peer).start()


def gather_finish(n, out_ref, reduced, gsends, grecvs):
    lev = lax.axis_index("lev")
    rows = out_ref.shape[1] // n
    for d in range(1, n):
        sender = lax.rem(lev + n - d, n)
        lev_copy(reduced.at[sender], reduced.at[sender], gsends.at[d - 1], grecvs.at[sender], sender).wait_recv()
        lev_copy(reduced.at[lev], reduced.at[lev], gsends.at[d - 1], grecvs.at[lev], lax.rem(lev + d, n)).wait_send()
    for q in range(n):
        out_ref[:, q * rows:(q + 1) * rows, :] = reduced[q]


def lev_scratch(n, shape, dtype):
    piece = (shape[0], shape[1] // n, shape[2])
    return [
        pltpu.VMEM((n,) + piece, dtype),
        pltpu.VMEM((n,) + piece, dtype),
        pltpu.SemaphoreType.DMA((n - 1,)),
        pltpu.SemaphoreType.DMA((n,)),
        pltpu.SemaphoreType.DMA((n - 1,)),
        pltpu.SemaphoreType.DMA((n,)),
    ]


def exchange_body(lev_n, owners, lat_n, rows_ref, part_ref, rows_out, sum_out,
                  got, row_send, row_recv, pieces, reduced, sends, recvs, gsends, grecvs):
    lat = lax.axis_index("lat")
    lev = lax.axis_index("lev")
    me = lax.axis_index("lon") * lat_n + lat

    def place(peer):
        return {"lon": peer // lat_n, "lat": lax.rem(peer, lat_n)}

    barrier = pltpu.get_barrier_semaphore()

    def greet(d, carry):
        peer = lax.rem(me + d, owners)
        pl.semaphore_signal(barrier, inc=1, device_id=place(peer), device_id_type=MESH)
        return carry

    lax.fori_loop(1, owners, greet, 0)
    for d in range(1, lev_n):
        pl.semaphore_signal(
            barrier, inc=1, device_id={"lev": lax.rem(lev + d, lev_n)}, device_id_type=MESH
        )
    pl.semaphore_wait(barrier, owners - 1 + lev_n - 1)
    scatter_start(lev_n, part_ref, pieces, sends, recvs)

    def row_copy(peer, target):
        return pltpu.make_async_remote_copy(
            src_ref=rows_ref.at[pl.ds(peer, 1)],
            dst_ref=got.at[pl.ds(target, 1)],
            send_sem=row_send.at[peer],
            recv_sem=row_recv.at[target],
            device_id=place(peer),
            device_id_type=MESH,
        )

    def send(d, carry):
        row_copy(lax.rem(me + d, owners), me).start()
        return carry

    lax.fori_loop(1, owners, send, 0)
    got[pl.ds(me, 1), :] = rows_ref[pl.ds(me, 1), :]
    scatter_finish_gather_start(lev_n, part_ref, pieces, reduced, sends, recvs, gsends, grecvs)

    def finish(d, carry):
        source = lax.rem(me + owners - d, owners)
        row_copy(lax.rem(me + d, owners), me).wait_send()
        row_copy(source, source).wait_recv()
        return carry

    lax.fori_loop(1, owners, finish, 0)
    gather_finish(lev_n, sum_out, reduced, gsends, grecvs)
    rows_out[...] = got[...]


def exchange(rows, part, collective_id):
    lev_n = lax.axis_size("lev")
    lat_n = lax.axis_size("lat")
    owners = lax.axis_size("lon") * lat_n
    vmem = pl.BlockSpec(memory_space=pltpu.VMEM)
    return pl.pallas_call(
        functools.partial(exchange_body, lev_n, owners, lat_n),
        out_shape=(
            jax.ShapeDtypeStruct(rows.shape, rows.dtype),
            jax.ShapeDtypeStruct(part.shape, part.dtype),
        ),
        in_specs=[vmem, vmem],
        out_specs=(vmem, vmem),
        scratch_shapes=[
            pltpu.VMEM(rows.shape, rows.dtype),
            pltpu.SemaphoreType.DMA((owners,)),
            pltpu.SemaphoreType.DMA((owners,)),
        ] + lev_scratch(lev_n, part.shape, part.dtype),
        compiler_params=pltpu.CompilerParams(
            collective_id=collective_id, has_side_effects=True
        ),
    )(rows, part)


def lev_direct_body(n, part_ref, out_ref, slots, send_sem, recv_sem):
    me = lax.axis_index("lev")
    barrier = pltpu.get_barrier_semaphore()
    for d in range(1, n):
        pl.semaphore_signal(
            barrier, inc=1, device_id={"lev": lax.rem(me + d, n)}, device_id_type=MESH
        )
    pl.semaphore_wait(barrier, n - 1)
    for d in range(1, n):
        lev_copy(part_ref, slots.at[me], send_sem.at[d - 1], recv_sem.at[me], lax.rem(me + d, n)).start()
    slots[me] = part_ref[...]
    for d in range(1, n):
        sender = lax.rem(me + n - d, n)
        lev_copy(part_ref, slots.at[sender], send_sem.at[d - 1], recv_sem.at[sender], sender).wait_recv()
        lev_copy(part_ref, slots.at[sender], send_sem.at[d - 1], recv_sem.at[sender], lax.rem(me + d, n)).wait_send()
    total = slots[0]
    for s in range(1, n):
        total = total + slots[s]
    out_ref[...] = total


def lev_direct(x, collective_id):
    n = lax.axis_size("lev")
    return pl.pallas_call(
        functools.partial(lev_direct_body, n),
        out_shape=jax.ShapeDtypeStruct(x.shape, x.dtype),
        in_specs=[pl.BlockSpec(memory_space=pltpu.VMEM)],
        out_specs=pl.BlockSpec(memory_space=pltpu.VMEM),
        scratch_shapes=[
            pltpu.VMEM((n,) + x.shape, x.dtype),
            pltpu.SemaphoreType.DMA((n - 1,)),
            pltpu.SemaphoreType.DMA((n,)),
        ],
        compiler_params=pltpu.CompilerParams(
            collective_id=collective_id, has_side_effects=True
        ),
    )(x)


def halo_places(lon_n, lat_n):
    lon = lax.axis_index("lon")
    lat = lax.axis_index("lat")
    half = lon_n // 2
    top = lat // (lat_n - 1)
    inner = (lat + lat_n - 1) // lat_n
    east = {"lon": lax.rem(lon + 1, lon_n)}
    west = {"lon": lax.rem(lon + lon_n - 1, lon_n)}
    up = {"lon": lax.rem(lon + half * top, lon_n), "lat": lat + 1 - top}
    down = {"lon": lax.rem(lon + half * (1 - inner), lon_n), "lat": lat - inner}
    return east, west, up, down, 1 - top, 1 - inner


def mix_halo_body(lev_n, lon_n, lat_n, with_base, p_ref, pe_ref, ae_ref, me_ref, te_ref, be_ref, cs_out, halo_out,
                  pieces, reduced, sends, recvs, gsends, grecvs,
                  pe_slots, pe_send, pe_recv, mixed, got, h_send, h_recv):
    lev = lax.axis_index("lev")
    east, west, up, down, up_slot, down_slot = halo_places(lon_n, lat_n)
    barrier = pltpu.get_barrier_semaphore()
    for d in range(1, lev_n):
        pl.semaphore_signal(
            barrier, inc=1, device_id={"lev": lax.rem(lev + d, lev_n)}, device_id_type=MESH
        )
    for peer in (east, west, up, down):
        pl.semaphore_signal(barrier, inc=1, device_id=peer, device_id_type=MESH)
    pl.semaphore_wait(barrier, lev_n - 1 + 4)
    scatter_start(lev_n, p_ref, pieces, sends, recvs)
    for d in range(1, lev_n):
        lev_copy(pe_ref, pe_slots.at[lev], pe_send.at[d - 1], pe_recv.at[lev], lax.rem(lev + d, lev_n)).start()
    pe_slots[lev] = pe_ref[...]
    scatter_finish_gather_start(lev_n, p_ref, pieces, reduced, sends, recvs, gsends, grecvs)
    for d in range(1, lev_n):
        sender = lax.rem(lev + lev_n - d, lev_n)
        lev_copy(pe_ref, pe_slots.at[sender], pe_send.at[d - 1], pe_recv.at[sender], sender).wait_recv()
        lev_copy(pe_ref, pe_slots.at[sender], pe_send.at[d - 1], pe_recv.at[sender], lax.rem(lev + d, lev_n)).wait_send()
    pe_sum = pe_slots[0]
    for s in range(1, lev_n):
        pe_sum = pe_sum + pe_slots[s]
    share = me_ref[...]
    if with_base:
        pe_sum = be_ref[...] + pe_sum
    mixed[...] = (1.0 - share) * ae_ref[...] + share * (pe_sum / te_ref[...])
    plan = (
        (mixed.at[0], got.at[0], h_recv.at[0], east),
        (mixed.at[1], got.at[1], h_recv.at[1], west),
        (mixed.at[2], got.at[2 + up_slot], h_recv.at[2 + up_slot], up),
        (mixed.at[3], got.at[2 + down_slot], h_recv.at[2 + down_slot], down),
    )
    copies = []
    for i, (src, dst, sem, peer) in enumerate(plan):
        copy = pltpu.make_async_remote_copy(
            src_ref=src, dst_ref=dst, send_sem=h_send.at[i], recv_sem=sem,
            device_id=peer, device_id_type=MESH,
        )
        copy.start()
        copies.append(copy)
    gather_finish(lev_n, cs_out, reduced, gsends, grecvs)
    for i in range(4):
        pltpu.make_async_remote_copy(
            src_ref=mixed.at[i], dst_ref=got.at[i], send_sem=h_send.at[i], recv_sem=h_recv.at[i],
            device_id=east, device_id_type=MESH,
        ).wait_recv()
    for copy in copies:
        copy.wait_send()
    halo_out[...] = got[...]


def mix_halo(p, pe, ae, me, te, be, collective_id):
    lev_n, lon_n, lat_n = lax.axis_size("lev"), lax.axis_size("lon"), lax.axis_size("lat")
    vmem = pl.BlockSpec(memory_space=pltpu.VMEM)
    return pl.pallas_call(
        functools.partial(mix_halo_body, lev_n, lon_n, lat_n, be is not None),
        out_shape=(
            jax.ShapeDtypeStruct(p.shape, p.dtype),
            jax.ShapeDtypeStruct(pe.shape, p.dtype),
        ),
        in_specs=[vmem] * 6,
        out_specs=(vmem, vmem),
        scratch_shapes=lev_scratch(lev_n, p.shape, p.dtype) + [
            pltpu.VMEM((lev_n,) + pe.shape, p.dtype),
            pltpu.SemaphoreType.DMA((lev_n - 1,)),
            pltpu.SemaphoreType.DMA((lev_n,)),
            pltpu.VMEM(pe.shape, p.dtype),
            pltpu.VMEM(pe.shape, p.dtype),
            pltpu.SemaphoreType.DMA((4,)),
            pltpu.SemaphoreType.DMA((4,)),
        ],
        compiler_params=pltpu.CompilerParams(
            collective_id=collective_id, has_side_effects=True
        ),
    )(p, pe, ae, me, te, pe if be is None else be)


def lev_sum(x, collective_id):
    n = lax.axis_size("lev")
    return pl.pallas_call(
        functools.partial(lev_sum_body, n),
        out_shape=jax.ShapeDtypeStruct(x.shape, x.dtype),
        in_specs=[pl.BlockSpec(memory_space=pltpu.VMEM)],
        out_specs=pl.BlockSpec(memory_space=pltpu.VMEM),
        scratch_shapes=lev_scratch(n, x.shape, x.dtype),
        compiler_params=pltpu.CompilerParams(
            collective_id=collective_id, has_side_effects=True
        ),
        cost_estimate=pl.CostEstimate(
            flops=n * x.size, bytes_accessed=(2 * n + 2) * x.size * 4, transcendentals=0
        ),
    )(x)


def from_behind(value, axis, steps):
    count = lax.axis_size(axis)
    pairs = [(source, (source + steps) % count) for source in range(count)]
    return lax.ppermute(value, axis, pairs)


def from_behind_2(block, axis, distance):
    devices = range(lax.axis_size(axis))
    route = [(i - distance, i) for i in devices if i - distance in devices]
    return lax.ppermute(block, axis, route)


def extended(x, sides, width, wrap):
    for axis, dim in sides:
        size, length = (lax.axis_size(axis), x.shape[dim])
        up = [(i, (i + 1) % size) for i in range(size if wrap else size - 1)]
        down = [(j, i) for i, j in up]
        last = lax.slice_in_dim(x, length - width, length, axis=dim)
        initial = lax.slice_in_dim(x, 0, width, axis=dim)
        before = lax.ppermute(last, axis, up)
        after = lax.ppermute(initial, axis, down)
        x = jnp.concatenate([before, x, after], axis=dim)
    return x


def mix_sum(partial_sum):
    return lax.psum(partial_sum, "lev")


def on_device(
    adjoint_field,
    east_courant,
    north_courant,
    pole_courant,
    mix_fraction,
    detrain_share,
    sounding_owner,
    sounding_cell,
    sounding_count,
    sounding_forcing,
):
    lon_count = lax.axis_size("lon")
    lat_count = lax.axis_size("lat")
    lat_place = lax.axis_index("lat")
    owner_self = lax.axis_index("lon") * lat_count + lat_place
    tracers, lev_dev, lat_rows, lon_cols = adjoint_field.shape
    step_count = sounding_forcing.shape[0]
    slot_count = sounding_forcing.shape[2]
    grid_cells = lat_rows * lon_cols
    detrain_part = jnp.sum(detrain_share, axis=0)
    owner_count = lon_count * lat_count
    cap = 4
    live_slots = jnp.arange(slot_count, dtype=jnp.int32)[None, :] < sounding_count
    values = jnp.where(live_slots[:, None, :], sounding_forcing, 0.0)
    owner_ids = sounding_owner[:, :, 0]
    slot_iota = jnp.arange(slot_count, dtype=jnp.int32)
    earlier = slot_iota[None, :, None] < slot_iota[None, None, :]
    same_owner = owner_ids[:, :, None] == owner_ids[:, None, :]
    rank = jnp.sum(jnp.logical_and(earlier, same_owner), axis=1, dtype=jnp.int32)
    position = owner_ids * cap + rank
    bucket_iota = jnp.arange(owner_count * cap, dtype=jnp.int32)
    chosen = position[:, :, None] == bucket_iota[None, None, :]
    bucket_values = jnp.sum(
        jnp.where(chosen[:, None, :, :], values[:, :, :, None], 0.0), axis=2
    )
    bucket_cell = jnp.max(
        jnp.where(chosen, sounding_cell[:, :, None] + 1, 0), axis=1
    ).astype(jnp.float32) - 1.0
    packed = jnp.concatenate([bucket_values, bucket_cell[:, None, :]], axis=1)
    packed = packed.reshape(step_count, lev_dev + 1, owner_count, cap)
    packed = jnp.transpose(packed, (2, 0, 1, 3))
    row_width = step_count * (lev_dev + 1) * cap
    rows = jnp.pad(packed.reshape(owner_count, row_width), ((0, 0), (0, 128 - row_width)))
    early_part = jnp.concatenate(
        [jnp.sum(detrain_share[None] * adjoint_field, axis=1), detrain_part[None]], axis=0
    )
    arrived, early = exchange(rows, early_part, 0)
    arrived = arrived[:, :row_width].reshape(owner_count, step_count, lev_dev + 1, cap)
    arrived = jnp.transpose(arrived, (1, 2, 0, 3)).reshape(
        step_count, lev_dev + 1, owner_count * cap
    )
    cells = arrived[:, lev_dev, :].astype(jnp.int32)
    row_hit = (cells // lon_cols)[:, :, None] == jnp.arange(lat_rows, dtype=jnp.int32)
    col_hit = (cells % lon_cols)[:, :, None] == jnp.arange(lon_cols, dtype=jnp.int32)
    spread = jnp.where(row_hit[:, None, :, :], arrived[:, :lev_dev, :, None], 0.0)
    forcing_grid = jnp.einsum(
        "tker,tec->tkrc", spread, col_hit.astype(jnp.float32), precision=lax.Precision.HIGHEST
    )
    row_index = jnp.arange(lat_rows, dtype=jnp.int32)[None, :, None]
    at_top = jnp.logical_and(lat_place == lat_count - 1, row_index == lat_rows - 1)
    at_bottom = jnp.logical_and(lat_place == 0, row_index == 0)
    upwind_east = jnp.maximum(east_courant, 0.0)
    total_detrain = early[tracers]
    planes = tracers * lev_dev

    def spread(x, width, fill=0.0):
        x = jnp.broadcast_to(x, (tracers, lev_dev, width)).reshape(planes, width)
        return jnp.pad(x, ((0, 0), (0, lon_cols - width)), constant_values=fill)

    def edges(x, fill=0.0):
        return jnp.stack([
            spread(x[..., :, -1], lat_rows, fill), spread(x[..., :, 0], lat_rows, fill),
            spread(x[..., -1, :], lon_cols), spread(x[..., 0, :], lon_cols),
        ])

    def widen(x):
        return jnp.pad(x, ((0, 0), (0, lon_cols - x.shape[1])))

    extra_winds = jnp.stack([
        widen(east_courant[:, :, -1]), widen(east_courant[:, :, 0]),
        north_courant[:, -1, :], pole_courant,
    ])
    no_extra = jnp.zeros_like(extra_winds)
    adjoint = adjoint_field
    for position in range(step_count):
        step_now = step_count - 1 - position
        adjoint = adjoint + forcing_grid[step_now][None]
        if position == 0:
            forcing_part = jnp.sum(detrain_share * forcing_grid[step_now], axis=0)
            fsum, halos = mix_halo(
                forcing_part[None],
                jnp.concatenate([edges(forcing_part[None, None]), no_extra], axis=1),
                jnp.concatenate([edges(adjoint), extra_winds], axis=1),
                jnp.concatenate([edges(mix_fraction[None]), no_extra], axis=1),
                jnp.concatenate([edges(total_detrain[None, None], 1.0), no_extra + 1.0], axis=1),
                jnp.concatenate([edges(early[:tracers][:, None]), no_extra], axis=1),
                6,
            )
            column_sum = early[:tracers] + fsum
        else:
            partial_sum = jnp.sum(detrain_share[None] * adjoint, axis=1)
            column_sum, halos = mix_halo(
                partial_sum,
                edges(partial_sum[:, None]),
                edges(adjoint),
                edges(mix_fraction[None]),
                edges(total_detrain[None, None], 1.0),
                None,
                5,
            )
        adjoint = (1.0 - mix_fraction)[None] * adjoint + mix_fraction[None] * (
            column_sum / total_detrain
        )[:, None]
        west_halo = halos[0, :planes, :lat_rows]
        east_halo = halos[1, :planes, :lat_rows]
        north_halo = halos[2, :planes]
        south_halo = halos[3, :planes]
        if position == 0:
            west_wind = jnp.concatenate(
                [halos[0, planes:, :lat_rows, None], east_courant[:, :, :-1]], axis=2
            )
            partner_top = halos[2, planes:]
            south_wind = jnp.concatenate(
                [halos[3, planes:, None, :], north_courant[:, :-1, :]], axis=1
            )
            partner_pole = halos[3, planes:]
            upwind_west = -jnp.minimum(west_wind, 0.0)
            upwind_north = jnp.maximum(north_courant, 0.0) + jnp.where(
                at_top, -jnp.minimum(partner_top, 0.0)[:, None, :], 0.0
            )
            upwind_south = jnp.where(
                at_bottom,
                (jnp.maximum(pole_courant, 0.0) - jnp.minimum(partner_pole, 0.0))[:, None, :],
                -jnp.minimum(south_wind, 0.0),
            )
        east_side = jnp.concatenate(
            [adjoint[:, :, :, 1:], east_halo.reshape(tracers, lev_dev, lat_rows, 1)], axis=3
        )
        west_side = jnp.concatenate(
            [west_halo.reshape(tracers, lev_dev, lat_rows, 1), adjoint[:, :, :, :-1]], axis=3
        )
        north_side = jnp.concatenate(
            [adjoint[:, :, 1:, :], north_halo.reshape(tracers, lev_dev, 1, lon_cols)], axis=2
        )
        south_side = jnp.concatenate(
            [south_halo.reshape(tracers, lev_dev, 1, lon_cols), adjoint[:, :, :-1, :]], axis=2
        )
        adjoint = (
            adjoint
            + upwind_east * (east_side - adjoint)
            + upwind_west * (west_side - adjoint)
            + upwind_north * (north_side - adjoint)
            + upwind_south * (south_side - adjoint)
        )
    return adjoint


def solution(mesh):
    return jax.shard_map(
        on_device,
        mesh=mesh,
        in_specs=(
            P(None, "lev", "lat", "lon"),
            P("lev", "lat", "lon"),
            P("lev", "lat", "lon"),
            P("lev", "lon"),
            P("lev", "lat", "lon"),
            P("lev", "lat", "lon"),
            P(None, ("lon", "lat"), None),
            P(None, ("lon", "lat")),
            P(None, ("lon", "lat")),
            P(None, "lev", ("lon", "lat")),
        ),
        out_specs=P(None, "lev", "lat", "lon"),
        check_vma=False,
    )
```

```python
import functools

import jax
import jax.numpy as jnp
from jax import lax
from jax.experimental import pallas as pl
from jax.experimental.pallas import tpu as pltpu
from jax.sharding import PartitionSpec as P

MESH = pl.DeviceIdType.MESH


def lev_sum_body(n, part_ref, out_ref, pieces, reduced, sends, recvs, gsends, grecvs):
    lev = lax.axis_index("lev")
    barrier = pltpu.get_barrier_semaphore()
    for d in range(1, n):
        pl.semaphore_signal(
            barrier, inc=1, device_id={"lev": lax.rem(lev + d, n)}, device_id_type=MESH
        )
    pl.semaphore_wait(barrier, n - 1)
    scatter_start(n, part_ref, pieces, sends, recvs)
    scatter_finish_gather_start(n, part_ref, pieces, reduced, sends, recvs, gsends, grecvs)
    gather_finish(n, out_ref, reduced, gsends, grecvs)


def halo_body(lon_n, lat_n, col_last, col_first, row_last, row_first,
              west_out, east_out, north_out, south_out, cols, rows, send_sem, col_sem, row_sem):
    lon = lax.axis_index("lon")
    lat = lax.axis_index("lat")
    half = lon_n // 2
    top = lat // (lat_n - 1)
    inner = (lat + lat_n - 1) // lat_n
    east = {"lon": lax.rem(lon + 1, lon_n)}
    west = {"lon": lax.rem(lon + lon_n - 1, lon_n)}
    up = {"lon": lax.rem(lon + half * top, lon_n), "lat": lat + 1 - top}
    down = {"lon": lax.rem(lon + half * (1 - inner), lon_n), "lat": lat - inner}
    up_slot = 1 - top
    down_slot = 1 - inner
    barrier = pltpu.get_barrier_semaphore()
    for peer in (east, west, up, down):
        pl.semaphore_signal(barrier, inc=1, device_id=peer, device_id_type=MESH)
    pl.semaphore_wait(barrier, 4)
    plan = (
        (col_last, cols.at[0], col_sem.at[0], east),
        (col_first, cols.at[1], col_sem.at[1], west),
        (row_last, rows.at[up_slot], row_sem.at[up_slot], up),
        (row_first, rows.at[down_slot], row_sem.at[down_slot], down),
    )
    sends = []
    for i, (src, dst, sem, peer) in enumerate(plan):
        copy = pltpu.make_async_remote_copy(
            src_ref=src, dst_ref=dst, send_sem=send_sem.at[i], recv_sem=sem,
            device_id=peer, device_id_type=MESH,
        )
        copy.start()
        sends.append(copy)
    arrivals = (
        (col_last, cols.at[0], col_sem.at[0]),
        (col_first, cols.at[1], col_sem.at[1]),
        (row_last, rows.at[0], row_sem.at[0]),
        (row_first, rows.at[1], row_sem.at[1]),
    )
    for src, dst, sem in arrivals:
        pltpu.make_async_remote_copy(
            src_ref=src, dst_ref=dst, send_sem=send_sem.at[0], recv_sem=sem,
            device_id=east, device_id_type=MESH,
        ).wait_recv()
    for copy in sends:
        copy.wait_send()
    west_out[...] = cols[0]
    east_out[...] = cols[1]
    north_out[...] = rows[0]
    south_out[...] = rows[1]


def halo_swap(col_last, col_first, row_last, row_first, collective_id):
    lon_n, lat_n = lax.axis_size("lon"), lax.axis_size("lat")
    vmem = pl.BlockSpec(memory_space=pltpu.VMEM)
    return pl.pallas_call(
        functools.partial(halo_body, lon_n, lat_n),
        out_shape=(
            jax.ShapeDtypeStruct(col_last.shape, col_last.dtype),
            jax.ShapeDtypeStruct(col_last.shape, col_last.dtype),
            jax.ShapeDtypeStruct(row_last.shape, row_last.dtype),
            jax.ShapeDtypeStruct(row_last.shape, row_last.dtype),
        ),
        in_specs=[vmem] * 4,
        out_specs=(vmem,) * 4,
        scratch_shapes=[
            pltpu.VMEM((2,) + col_last.shape, col_last.dtype),
            pltpu.VMEM((2,) + row_last.shape, row_last.dtype),
            pltpu.SemaphoreType.DMA((4,)),
            pltpu.SemaphoreType.DMA((2,)),
            pltpu.SemaphoreType.DMA((2,)),
        ],
        compiler_params=pltpu.CompilerParams(
            collective_id=collective_id, has_side_effects=True
        ),
    )(col_last, col_first, row_last, row_first)


def lev_copy(src, dst, send, recv, peer):
    return pltpu.make_async_remote_copy(
        src_ref=src, dst_ref=dst, send_sem=send, recv_sem=recv,
        device_id={"lev": peer}, device_id_type=MESH,
    )


def scatter_start(n, part_ref, pieces, sends, recvs):
    lev = lax.axis_index("lev")
    rows = part_ref.shape[1] // n
    for d in range(1, n):
        peer = lax.rem(lev + d, n)
        lev_copy(
            part_ref.at[:, pl.ds(pl.multiple_of(peer * rows, rows), rows), :],
            pieces.at[lev], sends.at[d - 1], recvs.at[lev], peer,
        ).start()
    pieces[lev] = part_ref[:, pl.ds(pl.multiple_of(lev * rows, rows), rows), :]


def scatter_finish_gather_start(n, part_ref, pieces, reduced, sends, recvs, gsends, grecvs):
    lev = lax.axis_index("lev")
    rows = part_ref.shape[1] // n
    for d in range(1, n):
        sender = lax.rem(lev + n - d, n)
        peer = lax.rem(lev + d, n)
        lev_copy(
            part_ref.at[:, pl.ds(0, rows), :], pieces.at[sender],
            sends.at[d - 1], recvs.at[sender], sender,
        ).wait_recv()
        lev_copy(
            part_ref.at[:, pl.ds(0, rows), :], pieces.at[sender],
            sends.at[d - 1], recvs.at[sender], peer,
        ).wait_send()
    total = pieces[0]
    for s in range(1, n):
        total = total + pieces[s]
    reduced[lev] = total
    for d in range(1, n):
        peer = lax.rem(lev + d, n)
        lev_copy(reduced.at[lev], reduced.at[lev], gsends.at[d - 1], grecvs.at[lev], peer).start()


def gather_finish(n, out_ref, reduced, gsends, grecvs):
    lev = lax.axis_index("lev")
    rows = out_ref.shape[1] // n
    for d in range(1, n):
        sender = lax.rem(lev + n - d, n)
        lev_copy(reduced.at[sender], reduced.at[sender], gsends.at[d - 1], grecvs.at[sender], sender).wait_recv()
        lev_copy(reduced.at[lev], reduced.at[lev], gsends.at[d - 1], grecvs.at[lev], lax.rem(lev + d, n)).wait_send()
    for q in range(n):
        out_ref[:, q * rows:(q + 1) * rows, :] = reduced[q]


def lev_scratch(n, shape, dtype):
    piece = (shape[0], shape[1] // n, shape[2])
    return [
        pltpu.VMEM((n,) + piece, dtype),
        pltpu.VMEM((n,) + piece, dtype),
        pltpu.SemaphoreType.DMA((n - 1,)),
        pltpu.SemaphoreType.DMA((n,)),
        pltpu.SemaphoreType.DMA((n - 1,)),
        pltpu.SemaphoreType.DMA((n,)),
    ]


def exchange_body(lev_n, owners, lat_n, rows_ref, part_ref, rows_out, sum_out,
                  got, row_send, row_recv, pieces, reduced, sends, recvs, gsends, grecvs):
    lat = lax.axis_index("lat")
    lev = lax.axis_index("lev")
    me = lax.axis_index("lon") * lat_n + lat

    def place(peer):
        return {"lon": peer // lat_n, "lat": lax.rem(peer, lat_n)}

    barrier = pltpu.get_barrier_semaphore()

    def greet(d, carry):
        peer = lax.rem(me + d, owners)
        pl.semaphore_signal(barrier, inc=1, device_id=place(peer), device_id_type=MESH)
        return carry

    lax.fori_loop(1, owners, greet, 0)
    for d in range(1, lev_n):
        pl.semaphore_signal(
            barrier, inc=1, device_id={"lev": lax.rem(lev + d, lev_n)}, device_id_type=MESH
        )
    pl.semaphore_wait(barrier, owners - 1 + lev_n - 1)
    scatter_start(lev_n, part_ref, pieces, sends, recvs)

    def row_copy(peer, target):
        return pltpu.make_async_remote_copy(
            src_ref=rows_ref.at[pl.ds(peer, 1)],
            dst_ref=got.at[pl.ds(target, 1)],
            send_sem=row_send.at[peer],
            recv_sem=row_recv.at[target],
            device_id=place(peer),
            device_id_type=MESH,
        )

    def send(d, carry):
        row_copy(lax.rem(me + d, owners), me).start()
        return carry

    lax.fori_loop(1, owners, send, 0)
    got[pl.ds(me, 1), :] = rows_ref[pl.ds(me, 1), :]
    scatter_finish_gather_start(lev_n, part_ref, pieces, reduced, sends, recvs, gsends, grecvs)

    def finish(d, carry):
        source = lax.rem(me + owners - d, owners)
        row_copy(lax.rem(me + d, owners), me).wait_send()
        row_copy(source, source).wait_recv()
        return carry

    lax.fori_loop(1, owners, finish, 0)
    gather_finish(lev_n, sum_out, reduced, gsends, grecvs)
    rows_out[...] = got[...]


def exchange(rows, part, collective_id):
    lev_n = lax.axis_size("lev")
    lat_n = lax.axis_size("lat")
    owners = lax.axis_size("lon") * lat_n
    vmem = pl.BlockSpec(memory_space=pltpu.VMEM)
    return pl.pallas_call(
        functools.partial(exchange_body, lev_n, owners, lat_n),
        out_shape=(
            jax.ShapeDtypeStruct(rows.shape, rows.dtype),
            jax.ShapeDtypeStruct(part.shape, part.dtype),
        ),
        in_specs=[vmem, vmem],
        out_specs=(vmem, vmem),
        scratch_shapes=[
            pltpu.VMEM(rows.shape, rows.dtype),
            pltpu.SemaphoreType.DMA((owners,)),
            pltpu.SemaphoreType.DMA((owners,)),
        ] + lev_scratch(lev_n, part.shape, part.dtype),
        compiler_params=pltpu.CompilerParams(
            collective_id=collective_id, has_side_effects=True
        ),
    )(rows, part)


def lev_direct_body(n, part_ref, out_ref, slots, send_sem, recv_sem):
    me = lax.axis_index("lev")
    barrier = pltpu.get_barrier_semaphore()
    for d in range(1, n):
        pl.semaphore_signal(
            barrier, inc=1, device_id={"lev": lax.rem(me + d, n)}, device_id_type=MESH
        )
    pl.semaphore_wait(barrier, n - 1)
    for d in range(1, n):
        lev_copy(part_ref, slots.at[me], send_sem.at[d - 1], recv_sem.at[me], lax.rem(me + d, n)).start()
    slots[me] = part_ref[...]
    for d in range(1, n):
        sender = lax.rem(me + n - d, n)
        lev_copy(part_ref, slots.at[sender], send_sem.at[d - 1], recv_sem.at[sender], sender).wait_recv()
        lev_copy(part_ref, slots.at[sender], send_sem.at[d - 1], recv_sem.at[sender], lax.rem(me + d, n)).wait_send()
    total = slots[0]
    for s in range(1, n):
        total = total + slots[s]
    out_ref[...] = total


def lev_direct(x, collective_id):
    n = lax.axis_size("lev")
    return pl.pallas_call(
        functools.partial(lev_direct_body, n),
        out_shape=jax.ShapeDtypeStruct(x.shape, x.dtype),
        in_specs=[pl.BlockSpec(memory_space=pltpu.VMEM)],
        out_specs=pl.BlockSpec(memory_space=pltpu.VMEM),
        scratch_shapes=[
            pltpu.VMEM((n,) + x.shape, x.dtype),
            pltpu.SemaphoreType.DMA((n - 1,)),
            pltpu.SemaphoreType.DMA((n,)),
        ],
        compiler_params=pltpu.CompilerParams(
            collective_id=collective_id, has_side_effects=True
        ),
    )(x)


def halo_places(lon_n, lat_n):
    lon = lax.axis_index("lon")
    lat = lax.axis_index("lat")
    half = lon_n // 2
    top = lat // (lat_n - 1)
    inner = (lat + lat_n - 1) // lat_n
    east = {"lon": lax.rem(lon + 1, lon_n)}
    west = {"lon": lax.rem(lon + lon_n - 1, lon_n)}
    up = {"lon": lax.rem(lon + half * top, lon_n), "lat": lat + 1 - top}
    down = {"lon": lax.rem(lon + half * (1 - inner), lon_n), "lat": lat - inner}
    return east, west, up, down, 1 - top, 1 - inner


def mix_halo_body(lev_n, lon_n, lat_n, with_base, p_ref, st_ref, cs_out, halo_out,
                  pieces, reduced, sends, recvs, gsends, grecvs,
                  pe_slots, pe_send, pe_recv, mixed, got, h_send, h_recv):
    lev = lax.axis_index("lev")
    pe_ref = st_ref.at[0]
    east, west, up, down, up_slot, down_slot = halo_places(lon_n, lat_n)
    barrier = pltpu.get_barrier_semaphore()
    for d in range(1, lev_n):
        pl.semaphore_signal(
            barrier, inc=1, device_id={"lev": lax.rem(lev + d, lev_n)}, device_id_type=MESH
        )
    for peer in (east, west, up, down):
        pl.semaphore_signal(barrier, inc=1, device_id=peer, device_id_type=MESH)
    pl.semaphore_wait(barrier, lev_n - 1 + 4)
    scatter_start(lev_n, p_ref, pieces, sends, recvs)
    for d in range(1, lev_n):
        lev_copy(pe_ref, pe_slots.at[lev], pe_send.at[d - 1], pe_recv.at[lev], lax.rem(lev + d, lev_n)).start()
    pe_slots[lev] = pe_ref[...]
    scatter_finish_gather_start(lev_n, p_ref, pieces, reduced, sends, recvs, gsends, grecvs)
    for d in range(1, lev_n):
        sender = lax.rem(lev + lev_n - d, lev_n)
        lev_copy(pe_ref, pe_slots.at[sender], pe_send.at[d - 1], pe_recv.at[sender], sender).wait_recv()
        lev_copy(pe_ref, pe_slots.at[sender], pe_send.at[d - 1], pe_recv.at[sender], lax.rem(lev + d, lev_n)).wait_send()
    pe_sum = pe_slots[0]
    for s in range(1, lev_n):
        pe_sum = pe_sum + pe_slots[s]
    if with_base:
        pe_sum = st_ref[4] + pe_sum
    share = st_ref[2]
    mixed[...] = (1.0 - share) * st_ref[1] + share * (pe_sum / st_ref[3])
    plan = (
        (mixed.at[0], got.at[0], h_recv.at[0], east),
        (mixed.at[1], got.at[1], h_recv.at[1], west),
        (mixed.at[2], got.at[2 + up_slot], h_recv.at[2 + up_slot], up),
        (mixed.at[3], got.at[2 + down_slot], h_recv.at[2 + down_slot], down),
    )
    copies = []
    for i, (src, dst, sem, peer) in enumerate(plan):
        copy = pltpu.make_async_remote_copy(
            src_ref=src, dst_ref=dst, send_sem=h_send.at[i], recv_sem=sem,
            device_id=peer, device_id_type=MESH,
        )
        copy.start()
        copies.append(copy)
    gather_finish(lev_n, cs_out, reduced, gsends, grecvs)
    for i in range(4):
        pltpu.make_async_remote_copy(
            src_ref=mixed.at[i], dst_ref=got.at[i], send_sem=h_send.at[i], recv_sem=h_recv.at[i],
            device_id=east, device_id_type=MESH,
        ).wait_recv()
    for copy in copies:
        copy.wait_send()
    halo_out[...] = got[...]


def mix_halo(p, st, with_base, collective_id):
    lev_n, lon_n, lat_n = lax.axis_size("lev"), lax.axis_size("lon"), lax.axis_size("lat")
    vmem = pl.BlockSpec(memory_space=pltpu.VMEM)
    return pl.pallas_call(
        functools.partial(mix_halo_body, lev_n, lon_n, lat_n, with_base),
        out_shape=(
            jax.ShapeDtypeStruct(p.shape, p.dtype),
            jax.ShapeDtypeStruct(st.shape[1:], p.dtype),
        ),
        in_specs=[vmem] * 2,
        out_specs=(vmem, vmem),
        scratch_shapes=lev_scratch(lev_n, p.shape, p.dtype) + [
            pltpu.VMEM((lev_n,) + st.shape[1:], p.dtype),
            pltpu.SemaphoreType.DMA((lev_n - 1,)),
            pltpu.SemaphoreType.DMA((lev_n,)),
            pltpu.VMEM(st.shape[1:], p.dtype),
            pltpu.VMEM(st.shape[1:], p.dtype),
            pltpu.SemaphoreType.DMA((4,)),
            pltpu.SemaphoreType.DMA((4,)),
        ],
        compiler_params=pltpu.CompilerParams(
            collective_id=collective_id, has_side_effects=True
        ),
    )(p, st)


def lev_sum(x, collective_id):
    n = lax.axis_size("lev")
    return pl.pallas_call(
        functools.partial(lev_sum_body, n),
        out_shape=jax.ShapeDtypeStruct(x.shape, x.dtype),
        in_specs=[pl.BlockSpec(memory_space=pltpu.VMEM)],
        out_specs=pl.BlockSpec(memory_space=pltpu.VMEM),
        scratch_shapes=lev_scratch(n, x.shape, x.dtype),
        compiler_params=pltpu.CompilerParams(
            collective_id=collective_id, has_side_effects=True
        ),
        cost_estimate=pl.CostEstimate(
            flops=n * x.size, bytes_accessed=(2 * n + 2) * x.size * 4, transcendentals=0
        ),
    )(x)


def from_behind(value, axis, steps):
    count = lax.axis_size(axis)
    pairs = [(source, (source + steps) % count) for source in range(count)]
    return lax.ppermute(value, axis, pairs)


def from_behind_2(block, axis, distance):
    devices = range(lax.axis_size(axis))
    route = [(i - distance, i) for i in devices if i - distance in devices]
    return lax.ppermute(block, axis, route)


def extended(x, sides, width, wrap):
    for axis, dim in sides:
        size, length = (lax.axis_size(axis), x.shape[dim])
        up = [(i, (i + 1) % size) for i in range(size if wrap else size - 1)]
        down = [(j, i) for i, j in up]
        last = lax.slice_in_dim(x, length - width, length, axis=dim)
        initial = lax.slice_in_dim(x, 0, width, axis=dim)
        before = lax.ppermute(last, axis, up)
        after = lax.ppermute(initial, axis, down)
        x = jnp.concatenate([before, x, after], axis=dim)
    return x


def mix_sum(partial_sum):
    return lax.psum(partial_sum, "lev")


def on_device(
    adjoint_field,
    east_courant,
    north_courant,
    pole_courant,
    mix_fraction,
    detrain_share,
    sounding_owner,
    sounding_cell,
    sounding_count,
    sounding_forcing,
):
    lon_count = lax.axis_size("lon")
    lat_count = lax.axis_size("lat")
    lat_place = lax.axis_index("lat")
    owner_self = lax.axis_index("lon") * lat_count + lat_place
    tracers, lev_dev, lat_rows, lon_cols = adjoint_field.shape
    step_count = sounding_forcing.shape[0]
    slot_count = sounding_forcing.shape[2]
    grid_cells = lat_rows * lon_cols
    detrain_part = jnp.sum(detrain_share, axis=0)
    owner_count = lon_count * lat_count
    cap = 4
    live_slots = jnp.arange(slot_count, dtype=jnp.int32)[None, :] < sounding_count
    values = jnp.where(live_slots[:, None, :], sounding_forcing, 0.0)
    owner_ids = sounding_owner[:, :, 0]
    slot_iota = jnp.arange(slot_count, dtype=jnp.int32)
    earlier = slot_iota[None, :, None] < slot_iota[None, None, :]
    same_owner = owner_ids[:, :, None] == owner_ids[:, None, :]
    rank = jnp.sum(jnp.logical_and(earlier, same_owner), axis=1, dtype=jnp.int32)
    position = owner_ids * cap + rank
    bucket_iota = jnp.arange(owner_count * cap, dtype=jnp.int32)
    chosen = position[:, :, None] == bucket_iota[None, None, :]
    bucket_values = jnp.sum(
        jnp.where(chosen[:, None, :, :], values[:, :, :, None], 0.0), axis=2
    )
    bucket_cell = jnp.max(
        jnp.where(chosen, sounding_cell[:, :, None] + 1, 0), axis=1
    ).astype(jnp.float32) - 1.0
    packed = jnp.concatenate([bucket_values, bucket_cell[:, None, :]], axis=1)
    packed = packed.reshape(step_count, lev_dev + 1, owner_count, cap)
    packed = jnp.transpose(packed, (2, 0, 1, 3))
    row_width = step_count * (lev_dev + 1) * cap
    rows = jnp.pad(packed.reshape(owner_count, row_width), ((0, 0), (0, 128 - row_width)))
    early_part = jnp.concatenate(
        [jnp.sum(detrain_share[None] * adjoint_field, axis=1), detrain_part[None]], axis=0
    )
    arrived, early = exchange(rows, early_part, 0)
    arrived = arrived[:, :row_width].reshape(owner_count, step_count, lev_dev + 1, cap)
    arrived = jnp.transpose(arrived, (1, 2, 0, 3)).reshape(
        step_count, lev_dev + 1, owner_count * cap
    )
    cells = arrived[:, lev_dev, :].astype(jnp.int32)
    row_hit = (cells // lon_cols)[:, :, None] == jnp.arange(lat_rows, dtype=jnp.int32)
    col_hit = (cells % lon_cols)[:, :, None] == jnp.arange(lon_cols, dtype=jnp.int32)
    spread = jnp.where(row_hit[:, None, :, :], arrived[:, :lev_dev, :, None], 0.0)
    forcing_grid = jnp.einsum(
        "tker,tec->tkrc", spread, col_hit.astype(jnp.float32), precision=lax.Precision.HIGHEST
    )
    row_index = jnp.arange(lat_rows, dtype=jnp.int32)[None, :, None]
    at_top = jnp.logical_and(lat_place == lat_count - 1, row_index == lat_rows - 1)
    at_bottom = jnp.logical_and(lat_place == 0, row_index == 0)
    upwind_east = jnp.maximum(east_courant, 0.0)
    total_detrain = early[tracers]
    planes = tracers * lev_dev

    def spread(x, width, fill=0.0):
        x = jnp.broadcast_to(x, (tracers, lev_dev, width)).reshape(planes, width)
        return jnp.pad(x, ((0, 0), (0, lon_cols - width)), constant_values=fill)

    def edges(x, fill=0.0):
        return jnp.stack([
            spread(x[..., :, -1], lat_rows, fill), spread(x[..., :, 0], lat_rows, fill),
            spread(x[..., -1, :], lon_cols), spread(x[..., 0, :], lon_cols),
        ])

    def widen(x):
        return jnp.pad(x, ((0, 0), (0, lon_cols - x.shape[1])))

    extra_winds = jnp.stack([
        widen(east_courant[:, :, -1]), widen(east_courant[:, :, 0]),
        north_courant[:, -1, :], pole_courant,
    ])
    no_extra = jnp.zeros_like(extra_winds)
    adjoint = adjoint_field
    for position in range(step_count):
        step_now = step_count - 1 - position
        adjoint = adjoint + forcing_grid[step_now][None]
        if position == 0:
            forcing_part = jnp.sum(detrain_share * forcing_grid[step_now], axis=0)
            fsum, halos = mix_halo(
                forcing_part[None],
                jnp.stack([
                    jnp.concatenate([edges(forcing_part[None, None]), no_extra], axis=1),
                    jnp.concatenate([edges(adjoint), extra_winds], axis=1),
                    jnp.concatenate([edges(mix_fraction[None]), no_extra], axis=1),
                    jnp.concatenate([edges(total_detrain[None, None], 1.0), no_extra + 1.0], axis=1),
                    jnp.concatenate([edges(early[:tracers][:, None]), no_extra], axis=1),
                ]),
                True,
                6,
            )
            column_sum = early[:tracers] + fsum
        else:
            partial_sum = jnp.sum(detrain_share[None] * adjoint, axis=1)
            column_sum, halos = mix_halo(
                partial_sum,
                jnp.stack([
                    edges(partial_sum[:, None]),
                    edges(adjoint),
                    edges(mix_fraction[None]),
                    edges(total_detrain[None, None], 1.0),
                ]),
                False,
                5,
            )
        adjoint = (1.0 - mix_fraction)[None] * adjoint + mix_fraction[None] * (
            column_sum / total_detrain
        )[:, None]
        west_halo = halos[0, :planes, :lat_rows]
        east_halo = halos[1, :planes, :lat_rows]
        north_halo = halos[2, :planes]
        south_halo = halos[3, :planes]
        if position == 0:
            west_wind = jnp.concatenate(
                [halos[0, planes:, :lat_rows, None], east_courant[:, :, :-1]], axis=2
            )
            partner_top = halos[2, planes:]
            south_wind = jnp.concatenate(
                [halos[3, planes:, None, :], north_courant[:, :-1, :]], axis=1
            )
            partner_pole = halos[3, planes:]
            upwind_west = -jnp.minimum(west_wind, 0.0)
            upwind_north = jnp.maximum(north_courant, 0.0) + jnp.where(
                at_top, -jnp.minimum(partner_top, 0.0)[:, None, :], 0.0
            )
            upwind_south = jnp.where(
                at_bottom,
                (jnp.maximum(pole_courant, 0.0) - jnp.minimum(partner_pole, 0.0))[:, None, :],
                -jnp.minimum(south_wind, 0.0),
            )
        east_side = jnp.concatenate(
            [adjoint[:, :, :, 1:], east_halo.reshape(tracers, lev_dev, lat_rows, 1)], axis=3
        )
        west_side = jnp.concatenate(
            [west_halo.reshape(tracers, lev_dev, lat_rows, 1), adjoint[:, :, :, :-1]], axis=3
        )
        north_side = jnp.concatenate(
            [adjoint[:, :, 1:, :], north_halo.reshape(tracers, lev_dev, 1, lon_cols)], axis=2
        )
        south_side = jnp.concatenate(
            [south_halo.reshape(tracers, lev_dev, 1, lon_cols), adjoint[:, :, :-1, :]], axis=2
        )
        adjoint = (
            adjoint
            + upwind_east * (east_side - adjoint)
            + upwind_west * (west_side - adjoint)
            + upwind_north * (north_side - adjoint)
            + upwind_south * (south_side - adjoint)
        )
    return adjoint


def solution(mesh):
    return jax.shard_map(
        on_device,
        mesh=mesh,
        in_specs=(
            P(None, "lev", "lat", "lon"),
            P("lev", "lat", "lon"),
            P("lev", "lat", "lon"),
            P("lev", "lon"),
            P("lev", "lat", "lon"),
            P("lev", "lat", "lon"),
            P(None, ("lon", "lat"), None),
            P(None, ("lon", "lat")),
            P(None, ("lon", "lat")),
            P(None, "lev", ("lon", "lat")),
        ),
        out_specs=P(None, "lev", "lat", "lon"),
        check_vma=False,
    )
```

```python
import functools

import jax
import jax.numpy as jnp
from jax import lax
from jax.experimental import pallas as pl
from jax.experimental.pallas import tpu as pltpu
from jax.sharding import PartitionSpec as P

MESH = pl.DeviceIdType.MESH


def lev_sum_body(n, part_ref, out_ref, pieces, reduced, sends, recvs, gsends, grecvs):
    lev = lax.axis_index("lev")
    barrier = pltpu.get_barrier_semaphore()
    for d in range(1, n):
        pl.semaphore_signal(
            barrier, inc=1, device_id={"lev": lax.rem(lev + d, n)}, device_id_type=MESH
        )
    pl.semaphore_wait(barrier, n - 1)
    scatter_start(n, part_ref, pieces, sends, recvs)
    scatter_finish_gather_start(n, part_ref, pieces, reduced, sends, recvs, gsends, grecvs)
    gather_finish(n, out_ref, reduced, gsends, grecvs)


def halo_body(lon_n, lat_n, col_last, col_first, row_last, row_first,
              west_out, east_out, north_out, south_out, cols, rows, send_sem, col_sem, row_sem):
    lon = lax.axis_index("lon")
    lat = lax.axis_index("lat")
    half = lon_n // 2
    top = lat // (lat_n - 1)
    inner = (lat + lat_n - 1) // lat_n
    east = {"lon": lax.rem(lon + 1, lon_n)}
    west = {"lon": lax.rem(lon + lon_n - 1, lon_n)}
    up = {"lon": lax.rem(lon + half * top, lon_n), "lat": lat + 1 - top}
    down = {"lon": lax.rem(lon + half * (1 - inner), lon_n), "lat": lat - inner}
    up_slot = 1 - top
    down_slot = 1 - inner
    barrier = pltpu.get_barrier_semaphore()
    for peer in (east, west, up, down):
        pl.semaphore_signal(barrier, inc=1, device_id=peer, device_id_type=MESH)
    pl.semaphore_wait(barrier, 4)
    plan = (
        (col_last, cols.at[0], col_sem.at[0], east),
        (col_first, cols.at[1], col_sem.at[1], west),
        (row_last, rows.at[up_slot], row_sem.at[up_slot], up),
        (row_first, rows.at[down_slot], row_sem.at[down_slot], down),
    )
    sends = []
    for i, (src, dst, sem, peer) in enumerate(plan):
        copy = pltpu.make_async_remote_copy(
            src_ref=src, dst_ref=dst, send_sem=send_sem.at[i], recv_sem=sem,
            device_id=peer, device_id_type=MESH,
        )
        copy.start()
        sends.append(copy)
    arrivals = (
        (col_last, cols.at[0], col_sem.at[0]),
        (col_first, cols.at[1], col_sem.at[1]),
        (row_last, rows.at[0], row_sem.at[0]),
        (row_first, rows.at[1], row_sem.at[1]),
    )
    for src, dst, sem in arrivals:
        pltpu.make_async_remote_copy(
            src_ref=src, dst_ref=dst, send_sem=send_sem.at[0], recv_sem=sem,
            device_id=east, device_id_type=MESH,
        ).wait_recv()
    for copy in sends:
        copy.wait_send()
    west_out[...] = cols[0]
    east_out[...] = cols[1]
    north_out[...] = rows[0]
    south_out[...] = rows[1]


def halo_swap(col_last, col_first, row_last, row_first, collective_id):
    lon_n, lat_n = lax.axis_size("lon"), lax.axis_size("lat")
    vmem = pl.BlockSpec(memory_space=pltpu.VMEM)
    return pl.pallas_call(
        functools.partial(halo_body, lon_n, lat_n),
        out_shape=(
            jax.ShapeDtypeStruct(col_last.shape, col_last.dtype),
            jax.ShapeDtypeStruct(col_last.shape, col_last.dtype),
            jax.ShapeDtypeStruct(row_last.shape, row_last.dtype),
            jax.ShapeDtypeStruct(row_last.shape, row_last.dtype),
        ),
        in_specs=[vmem] * 4,
        out_specs=(vmem,) * 4,
        scratch_shapes=[
            pltpu.VMEM((2,) + col_last.shape, col_last.dtype),
            pltpu.VMEM((2,) + row_last.shape, row_last.dtype),
            pltpu.SemaphoreType.DMA((4,)),
            pltpu.SemaphoreType.DMA((2,)),
            pltpu.SemaphoreType.DMA((2,)),
        ],
        compiler_params=pltpu.CompilerParams(
            collective_id=collective_id, has_side_effects=True
        ),
    )(col_last, col_first, row_last, row_first)


def lev_copy(src, dst, send, recv, peer):
    return pltpu.make_async_remote_copy(
        src_ref=src, dst_ref=dst, send_sem=send, recv_sem=recv,
        device_id={"lev": peer}, device_id_type=MESH,
    )


def scatter_start(n, part_ref, pieces, sends, recvs):
    lev = lax.axis_index("lev")
    rows = part_ref.shape[1] // n
    for d in range(1, n):
        peer = lax.rem(lev + d, n)
        lev_copy(
            part_ref.at[:, pl.ds(pl.multiple_of(peer * rows, rows), rows), :],
            pieces.at[lev], sends.at[d - 1], recvs.at[lev], peer,
        ).start()
    pieces[lev] = part_ref[:, pl.ds(pl.multiple_of(lev * rows, rows), rows), :]


def scatter_finish_gather_start(n, part_ref, pieces, reduced, sends, recvs, gsends, grecvs):
    lev = lax.axis_index("lev")
    rows = part_ref.shape[1] // n
    for d in range(1, n):
        sender = lax.rem(lev + n - d, n)
        peer = lax.rem(lev + d, n)
        lev_copy(
            part_ref.at[:, pl.ds(0, rows), :], pieces.at[sender],
            sends.at[d - 1], recvs.at[sender], sender,
        ).wait_recv()
        lev_copy(
            part_ref.at[:, pl.ds(0, rows), :], pieces.at[sender],
            sends.at[d - 1], recvs.at[sender], peer,
        ).wait_send()
    total = pieces[0]
    for s in range(1, n):
        total = total + pieces[s]
    reduced[lev] = total
    for d in range(1, n):
        peer = lax.rem(lev + d, n)
        lev_copy(reduced.at[lev], reduced.at[lev], gsends.at[d - 1], grecvs.at[lev], peer).start()


def gather_finish(n, out_ref, reduced, gsends, grecvs):
    lev = lax.axis_index("lev")
    rows = out_ref.shape[1] // n
    for d in range(1, n):
        sender = lax.rem(lev + n - d, n)
        lev_copy(reduced.at[sender], reduced.at[sender], gsends.at[d - 1], grecvs.at[sender], sender).wait_recv()
        lev_copy(reduced.at[lev], reduced.at[lev], gsends.at[d - 1], grecvs.at[lev], lax.rem(lev + d, n)).wait_send()
    for q in range(n):
        out_ref[:, q * rows:(q + 1) * rows, :] = reduced[q]


def lev_scratch(n, shape, dtype):
    piece = (shape[0], shape[1] // n, shape[2])
    return [
        pltpu.VMEM((n,) + piece, dtype),
        pltpu.VMEM((n,) + piece, dtype),
        pltpu.SemaphoreType.DMA((n - 1,)),
        pltpu.SemaphoreType.DMA((n,)),
        pltpu.SemaphoreType.DMA((n - 1,)),
        pltpu.SemaphoreType.DMA((n,)),
    ]


def exchange_body(lev_n, owners, lat_n, rows_ref, part_ref, rows_out, sum_out,
                  got, row_send, row_recv, pieces, reduced, sends, recvs, gsends, grecvs):
    lat = lax.axis_index("lat")
    lev = lax.axis_index("lev")
    me = lax.axis_index("lon") * lat_n + lat

    def place(peer):
        return {"lon": peer // lat_n, "lat": lax.rem(peer, lat_n)}

    barrier = pltpu.get_barrier_semaphore()

    def greet(d, carry):
        peer = lax.rem(me + d, owners)
        pl.semaphore_signal(barrier, inc=1, device_id=place(peer), device_id_type=MESH)
        return carry

    lax.fori_loop(1, owners, greet, 0)
    for d in range(1, lev_n):
        pl.semaphore_signal(
            barrier, inc=1, device_id={"lev": lax.rem(lev + d, lev_n)}, device_id_type=MESH
        )
    pl.semaphore_wait(barrier, owners - 1 + lev_n - 1)
    scatter_start(lev_n, part_ref, pieces, sends, recvs)

    def row_copy(peer, target):
        return pltpu.make_async_remote_copy(
            src_ref=rows_ref.at[pl.ds(peer, 1)],
            dst_ref=got.at[pl.ds(target, 1)],
            send_sem=row_send.at[peer],
            recv_sem=row_recv.at[target],
            device_id=place(peer),
            device_id_type=MESH,
        )

    def send(d, carry):
        row_copy(lax.rem(me + d, owners), me).start()
        return carry

    lax.fori_loop(1, owners, send, 0)
    got[pl.ds(me, 1), :] = rows_ref[pl.ds(me, 1), :]
    scatter_finish_gather_start(lev_n, part_ref, pieces, reduced, sends, recvs, gsends, grecvs)

    def finish(d, carry):
        source = lax.rem(me + owners - d, owners)
        row_copy(lax.rem(me + d, owners), me).wait_send()
        row_copy(source, source).wait_recv()
        return carry

    lax.fori_loop(1, owners, finish, 0)
    gather_finish(lev_n, sum_out, reduced, gsends, grecvs)
    rows_out[...] = got[...]


def exchange(rows, part, collective_id):
    lev_n = lax.axis_size("lev")
    lat_n = lax.axis_size("lat")
    owners = lax.axis_size("lon") * lat_n
    vmem = pl.BlockSpec(memory_space=pltpu.VMEM)
    return pl.pallas_call(
        functools.partial(exchange_body, lev_n, owners, lat_n),
        out_shape=(
            jax.ShapeDtypeStruct(rows.shape, rows.dtype),
            jax.ShapeDtypeStruct(part.shape, part.dtype),
        ),
        in_specs=[vmem, vmem],
        out_specs=(vmem, vmem),
        scratch_shapes=[
            pltpu.VMEM(rows.shape, rows.dtype),
            pltpu.SemaphoreType.DMA((owners,)),
            pltpu.SemaphoreType.DMA((owners,)),
        ] + lev_scratch(lev_n, part.shape, part.dtype),
        compiler_params=pltpu.CompilerParams(
            collective_id=collective_id, has_side_effects=True
        ),
    )(rows, part)


def lev_direct_body(n, part_ref, out_ref, slots, send_sem, recv_sem):
    me = lax.axis_index("lev")
    barrier = pltpu.get_barrier_semaphore()
    for d in range(1, n):
        pl.semaphore_signal(
            barrier, inc=1, device_id={"lev": lax.rem(me + d, n)}, device_id_type=MESH
        )
    pl.semaphore_wait(barrier, n - 1)
    for d in range(1, n):
        lev_copy(part_ref, slots.at[me], send_sem.at[d - 1], recv_sem.at[me], lax.rem(me + d, n)).start()
    slots[me] = part_ref[...]
    for d in range(1, n):
        sender = lax.rem(me + n - d, n)
        lev_copy(part_ref, slots.at[sender], send_sem.at[d - 1], recv_sem.at[sender], sender).wait_recv()
        lev_copy(part_ref, slots.at[sender], send_sem.at[d - 1], recv_sem.at[sender], lax.rem(me + d, n)).wait_send()
    total = slots[0]
    for s in range(1, n):
        total = total + slots[s]
    out_ref[...] = total


def lev_direct(x, collective_id):
    n = lax.axis_size("lev")
    return pl.pallas_call(
        functools.partial(lev_direct_body, n),
        out_shape=jax.ShapeDtypeStruct(x.shape, x.dtype),
        in_specs=[pl.BlockSpec(memory_space=pltpu.VMEM)],
        out_specs=pl.BlockSpec(memory_space=pltpu.VMEM),
        scratch_shapes=[
            pltpu.VMEM((n,) + x.shape, x.dtype),
            pltpu.SemaphoreType.DMA((n - 1,)),
            pltpu.SemaphoreType.DMA((n,)),
        ],
        compiler_params=pltpu.CompilerParams(
            collective_id=collective_id, has_side_effects=True
        ),
    )(x)


def halo_places(lon_n, lat_n):
    lon = lax.axis_index("lon")
    lat = lax.axis_index("lat")
    half = lon_n // 2
    top = lat // (lat_n - 1)
    inner = (lat + lat_n - 1) // lat_n
    east = {"lon": lax.rem(lon + 1, lon_n)}
    west = {"lon": lax.rem(lon + lon_n - 1, lon_n)}
    up = {"lon": lax.rem(lon + half * top, lon_n), "lat": lat + 1 - top}
    down = {"lon": lax.rem(lon + half * (1 - inner), lon_n), "lat": lat - inner}
    return east, west, up, down, 1 - top, 1 - inner


def mix_halo_body(lev_n, lon_n, lat_n, p_ref, st_ref, cs_out, halo_out,
                  pieces, reduced, sends, recvs, gsends, grecvs,
                  pe_slots, pe_send, pe_recv, mixed, got, h_send, h_recv):
    lev = lax.axis_index("lev")
    pe_ref = st_ref.at[0]
    east, west, up, down, up_slot, down_slot = halo_places(lon_n, lat_n)
    barrier = pltpu.get_barrier_semaphore()
    for d in range(1, lev_n):
        pl.semaphore_signal(
            barrier, inc=1, device_id={"lev": lax.rem(lev + d, lev_n)}, device_id_type=MESH
        )
    for peer in (east, west, up, down):
        pl.semaphore_signal(barrier, inc=1, device_id=peer, device_id_type=MESH)
    pl.semaphore_wait(barrier, lev_n - 1 + 4)
    scatter_start(lev_n, p_ref, pieces, sends, recvs)
    for d in range(1, lev_n):
        lev_copy(pe_ref, pe_slots.at[lev], pe_send.at[d - 1], pe_recv.at[lev], lax.rem(lev + d, lev_n)).start()
    pe_slots[lev] = pe_ref[...]
    scatter_finish_gather_start(lev_n, p_ref, pieces, reduced, sends, recvs, gsends, grecvs)
    for d in range(1, lev_n):
        sender = lax.rem(lev + lev_n - d, lev_n)
        lev_copy(pe_ref, pe_slots.at[sender], pe_send.at[d - 1], pe_recv.at[sender], sender).wait_recv()
        lev_copy(pe_ref, pe_slots.at[sender], pe_send.at[d - 1], pe_recv.at[sender], lax.rem(lev + d, lev_n)).wait_send()
    pe_sum = pe_slots[0]
    for s in range(1, lev_n):
        pe_sum = pe_sum + pe_slots[s]
    share = st_ref[2]
    mixed[...] = (1.0 - share) * st_ref[1] + share * (pe_sum / st_ref[3])
    plan = (
        (mixed.at[0], got.at[0], h_recv.at[0], east),
        (mixed.at[1], got.at[1], h_recv.at[1], west),
        (mixed.at[2], got.at[2 + up_slot], h_recv.at[2 + up_slot], up),
        (mixed.at[3], got.at[2 + down_slot], h_recv.at[2 + down_slot], down),
    )
    copies = []
    for i, (src, dst, sem, peer) in enumerate(plan):
        copy = pltpu.make_async_remote_copy(
            src_ref=src, dst_ref=dst, send_sem=h_send.at[i], recv_sem=sem,
            device_id=peer, device_id_type=MESH,
        )
        copy.start()
        copies.append(copy)
    gather_finish(lev_n, cs_out, reduced, gsends, grecvs)
    for i in range(4):
        pltpu.make_async_remote_copy(
            src_ref=mixed.at[i], dst_ref=got.at[i], send_sem=h_send.at[i], recv_sem=h_recv.at[i],
            device_id=east, device_id_type=MESH,
        ).wait_recv()
    for copy in copies:
        copy.wait_send()
    halo_out[...] = got[...]


def mix_halo(p, st, collective_id):
    lev_n, lon_n, lat_n = lax.axis_size("lev"), lax.axis_size("lon"), lax.axis_size("lat")
    vmem = pl.BlockSpec(memory_space=pltpu.VMEM)
    return pl.pallas_call(
        functools.partial(mix_halo_body, lev_n, lon_n, lat_n),
        out_shape=(
            jax.ShapeDtypeStruct(p.shape, p.dtype),
            jax.ShapeDtypeStruct(st.shape[1:], p.dtype),
        ),
        in_specs=[vmem] * 2,
        out_specs=(vmem, vmem),
        scratch_shapes=lev_scratch(lev_n, p.shape, p.dtype) + [
            pltpu.VMEM((lev_n,) + st.shape[1:], p.dtype),
            pltpu.SemaphoreType.DMA((lev_n - 1,)),
            pltpu.SemaphoreType.DMA((lev_n,)),
            pltpu.VMEM(st.shape[1:], p.dtype),
            pltpu.VMEM(st.shape[1:], p.dtype),
            pltpu.SemaphoreType.DMA((4,)),
            pltpu.SemaphoreType.DMA((4,)),
        ],
        compiler_params=pltpu.CompilerParams(
            collective_id=collective_id, has_side_effects=True
        ),
    )(p, st)


def lev_sum(x, collective_id):
    n = lax.axis_size("lev")
    return pl.pallas_call(
        functools.partial(lev_sum_body, n),
        out_shape=jax.ShapeDtypeStruct(x.shape, x.dtype),
        in_specs=[pl.BlockSpec(memory_space=pltpu.VMEM)],
        out_specs=pl.BlockSpec(memory_space=pltpu.VMEM),
        scratch_shapes=lev_scratch(n, x.shape, x.dtype),
        compiler_params=pltpu.CompilerParams(
            collective_id=collective_id, has_side_effects=True
        ),
        cost_estimate=pl.CostEstimate(
            flops=n * x.size, bytes_accessed=(2 * n + 2) * x.size * 4, transcendentals=0
        ),
    )(x)


def from_behind(value, axis, steps):
    count = lax.axis_size(axis)
    pairs = [(source, (source + steps) % count) for source in range(count)]
    return lax.ppermute(value, axis, pairs)


def from_behind_2(block, axis, distance):
    devices = range(lax.axis_size(axis))
    route = [(i - distance, i) for i in devices if i - distance in devices]
    return lax.ppermute(block, axis, route)


def extended(x, sides, width, wrap):
    for axis, dim in sides:
        size, length = (lax.axis_size(axis), x.shape[dim])
        up = [(i, (i + 1) % size) for i in range(size if wrap else size - 1)]
        down = [(j, i) for i, j in up]
        last = lax.slice_in_dim(x, length - width, length, axis=dim)
        initial = lax.slice_in_dim(x, 0, width, axis=dim)
        before = lax.ppermute(last, axis, up)
        after = lax.ppermute(initial, axis, down)
        x = jnp.concatenate([before, x, after], axis=dim)
    return x


def mix_sum(partial_sum):
    return lax.psum(partial_sum, "lev")


def on_device(
    adjoint_field,
    east_courant,
    north_courant,
    pole_courant,
    mix_fraction,
    detrain_share,
    sounding_owner,
    sounding_cell,
    sounding_count,
    sounding_forcing,
):
    lon_count = lax.axis_size("lon")
    lat_count = lax.axis_size("lat")
    lat_place = lax.axis_index("lat")
    owner_self = lax.axis_index("lon") * lat_count + lat_place
    tracers, lev_dev, lat_rows, lon_cols = adjoint_field.shape
    step_count = sounding_forcing.shape[0]
    slot_count = sounding_forcing.shape[2]
    grid_cells = lat_rows * lon_cols
    detrain_part = jnp.sum(detrain_share, axis=0)
    owner_count = lon_count * lat_count
    cap = 4
    live_slots = jnp.arange(slot_count, dtype=jnp.int32)[None, :] < sounding_count
    values = jnp.where(live_slots[:, None, :], sounding_forcing, 0.0)
    owner_ids = sounding_owner[:, :, 0]
    slot_iota = jnp.arange(slot_count, dtype=jnp.int32)
    earlier = slot_iota[None, :, None] < slot_iota[None, None, :]
    same_owner = owner_ids[:, :, None] == owner_ids[:, None, :]
    rank = jnp.sum(jnp.logical_and(earlier, same_owner), axis=1, dtype=jnp.int32)
    position = owner_ids * cap + rank
    bucket_iota = jnp.arange(owner_count * cap, dtype=jnp.int32)
    chosen = position[:, :, None] == bucket_iota[None, None, :]
    bucket_values = jnp.sum(
        jnp.where(chosen[:, None, :, :], values[:, :, :, None], 0.0), axis=2
    )
    bucket_cell = jnp.max(
        jnp.where(chosen, sounding_cell[:, :, None] + 1, 0), axis=1
    ).astype(jnp.float32) - 1.0
    packed = jnp.concatenate([bucket_values, bucket_cell[:, None, :]], axis=1)
    packed = packed.reshape(step_count, lev_dev + 1, owner_count, cap)
    packed = jnp.transpose(packed, (2, 0, 1, 3))
    row_width = step_count * (lev_dev + 1) * cap
    rows = jnp.pad(packed.reshape(owner_count, row_width), ((0, 0), (0, 128 - row_width)))
    early_part = jnp.concatenate(
        [jnp.sum(detrain_share[None] * adjoint_field, axis=1), detrain_part[None]], axis=0
    )
    arrived, early = exchange(rows, early_part, 0)
    arrived = arrived[:, :row_width].reshape(owner_count, step_count, lev_dev + 1, cap)
    arrived = jnp.transpose(arrived, (1, 2, 0, 3)).reshape(
        step_count, lev_dev + 1, owner_count * cap
    )
    cells = arrived[:, lev_dev, :].astype(jnp.int32)
    row_hit = (cells // lon_cols)[:, :, None] == jnp.arange(lat_rows, dtype=jnp.int32)
    col_hit = (cells % lon_cols)[:, :, None] == jnp.arange(lon_cols, dtype=jnp.int32)
    spread = jnp.where(row_hit[:, None, :, :], arrived[:, :lev_dev, :, None], 0.0)
    forcing_grid = jnp.einsum(
        "tker,tec->tkrc", spread, col_hit.astype(jnp.float32), precision=lax.Precision.HIGHEST
    )
    row_index = jnp.arange(lat_rows, dtype=jnp.int32)[None, :, None]
    at_top = jnp.logical_and(lat_place == lat_count - 1, row_index == lat_rows - 1)
    at_bottom = jnp.logical_and(lat_place == 0, row_index == 0)
    upwind_east = jnp.maximum(east_courant, 0.0)
    forcing_part = jnp.sum(detrain_share * forcing_grid[step_count - 1], axis=0)
    forcing_sum = lev_direct(forcing_part[None], 4)[0]
    adjoint = adjoint_field
    for position in range(step_count):
        step_now = step_count - 1 - position
        adjoint = adjoint + forcing_grid[step_now][None]
        if position == 0:
            column_sum = early[:tracers] + forcing_sum[None]
            total_detrain = early[tracers]
        else:
            partial_sum = jnp.sum(detrain_share[None] * adjoint, axis=1)
            planes = tracers * lev_dev

            def spread(x, width, fill=0.0):
                x = jnp.broadcast_to(x, (tracers, lev_dev, width)).reshape(planes, width)
                return jnp.pad(x, ((0, 0), (0, lon_cols - width)), constant_values=fill)

            def edges(x, fill=0.0):
                return jnp.stack([
                    spread(x[..., :, -1], lat_rows, fill), spread(x[..., :, 0], lat_rows, fill),
                    spread(x[..., -1, :], lon_cols), spread(x[..., 0, :], lon_cols),
                ])

            column_sum, halos = mix_halo(
                partial_sum,
                jnp.stack([
                    edges(partial_sum[:, None]),
                    edges(adjoint),
                    edges(mix_fraction[None]),
                    edges(total_detrain[None, None], 1.0),
                ]),
                5,
            )
        adjoint = (1.0 - mix_fraction)[None] * adjoint + mix_fraction[None] * (
            column_sum / total_detrain
        )[:, None]
        if position == 1:
            west_halo = halos[0, :, :lat_rows]
            east_halo = halos[1, :, :lat_rows]
            north_halo = halos[2]
            south_halo = halos[3]
        planes = tracers * lev_dev
        if position == 0:
            col_last = adjoint[:, :, :, -1].reshape(planes, lat_rows)
            col_first = adjoint[:, :, :, 0].reshape(planes, lat_rows)
            row_last = adjoint[:, :, -1, :].reshape(planes, lon_cols)
            row_first = adjoint[:, :, 0, :].reshape(planes, lon_cols)
            if position == 0:
                col_last = jnp.concatenate([col_last, east_courant[:, :, -1]], axis=0)
                col_first = jnp.concatenate([col_first, east_courant[:, :, 0]], axis=0)
                row_last = jnp.concatenate([row_last, north_courant[:, -1, :]], axis=0)
                row_first = jnp.concatenate([row_first, pole_courant], axis=0)
            west_halo, east_halo, north_halo, south_halo = halo_swap(
                col_last, col_first, row_last, row_first, 2 + position
            )
            if position == 0:
                west_wind = jnp.concatenate(
                    [west_halo[planes:, :, None], east_courant[:, :, :-1]], axis=2
                )
                partner_top = north_halo[planes:]
                south_wind = jnp.concatenate(
                    [south_halo[planes:, None, :], north_courant[:, :-1, :]], axis=1
                )
                partner_pole = south_halo[planes:]
                upwind_west = -jnp.minimum(west_wind, 0.0)
                upwind_north = jnp.maximum(north_courant, 0.0) + jnp.where(
                    at_top, -jnp.minimum(partner_top, 0.0)[:, None, :], 0.0
                )
                upwind_south = jnp.where(
                    at_bottom,
                    (jnp.maximum(pole_courant, 0.0) - jnp.minimum(partner_pole, 0.0))[:, None, :],
                    -jnp.minimum(south_wind, 0.0),
                )
                west_halo, east_halo = west_halo[:planes], east_halo[:planes]
                north_halo, south_halo = north_halo[:planes], south_halo[:planes]
        east_side = jnp.concatenate(
            [adjoint[:, :, :, 1:], east_halo.reshape(tracers, lev_dev, lat_rows, 1)], axis=3
        )
        west_side = jnp.concatenate(
            [west_halo.reshape(tracers, lev_dev, lat_rows, 1), adjoint[:, :, :, :-1]], axis=3
        )
        north_side = jnp.concatenate(
            [adjoint[:, :, 1:, :], north_halo.reshape(tracers, lev_dev, 1, lon_cols)], axis=2
        )
        south_side = jnp.concatenate(
            [south_halo.reshape(tracers, lev_dev, 1, lon_cols), adjoint[:, :, :-1, :]], axis=2
        )
        adjoint = (
            adjoint
            + upwind_east * (east_side - adjoint)
            + upwind_west * (west_side - adjoint)
            + upwind_north * (north_side - adjoint)
            + upwind_south * (south_side - adjoint)
        )
    return adjoint


def solution(mesh):
    return jax.shard_map(
        on_device,
        mesh=mesh,
        in_specs=(
            P(None, "lev", "lat", "lon"),
            P("lev", "lat", "lon"),
            P("lev", "lat", "lon"),
            P("lev", "lon"),
            P("lev", "lat", "lon"),
            P("lev", "lat", "lon"),
            P(None, ("lon", "lat"), None),
            P(None, ("lon", "lat")),
            P(None, ("lon", "lat")),
            P(None, "lev", ("lon", "lat")),
        ),
        out_specs=P(None, "lev", "lat", "lon"),
        check_vma=False,
    )
```

```python
import functools

import jax
import jax.numpy as jnp
from jax import lax
from jax.experimental import pallas as pl
from jax.experimental.pallas import tpu as pltpu
from jax.sharding import PartitionSpec as P

MESH = pl.DeviceIdType.MESH


def lev_sum_body(n, part_ref, out_ref, pieces, reduced, sends, recvs, gsends, grecvs):
    lev = lax.axis_index("lev")
    barrier = pltpu.get_barrier_semaphore()
    for d in range(1, n):
        pl.semaphore_signal(
            barrier, inc=1, device_id={"lev": lax.rem(lev + d, n)}, device_id_type=MESH
        )
    pl.semaphore_wait(barrier, n - 1)
    scatter_start(n, part_ref, pieces, sends, recvs)
    scatter_finish_gather_start(n, part_ref, pieces, reduced, sends, recvs, gsends, grecvs)
    gather_finish(n, out_ref, reduced, gsends, grecvs)


def halo_body(lon_n, lat_n, col_last, col_first, row_last, row_first,
              west_out, east_out, north_out, south_out, cols, rows, send_sem, col_sem, row_sem):
    lon = lax.axis_index("lon")
    lat = lax.axis_index("lat")
    half = lon_n // 2
    top = lat // (lat_n - 1)
    inner = (lat + lat_n - 1) // lat_n
    east = {"lon": lax.rem(lon + 1, lon_n)}
    west = {"lon": lax.rem(lon + lon_n - 1, lon_n)}
    up = {"lon": lax.rem(lon + half * top, lon_n), "lat": lat + 1 - top}
    down = {"lon": lax.rem(lon + half * (1 - inner), lon_n), "lat": lat - inner}
    up_slot = 1 - top
    down_slot = 1 - inner
    barrier = pltpu.get_barrier_semaphore()
    for peer in (east, west, up, down):
        pl.semaphore_signal(barrier, inc=1, device_id=peer, device_id_type=MESH)
    pl.semaphore_wait(barrier, 4)
    plan = (
        (col_last, cols.at[0], col_sem.at[0], east),
        (col_first, cols.at[1], col_sem.at[1], west),
        (row_last, rows.at[up_slot], row_sem.at[up_slot], up),
        (row_first, rows.at[down_slot], row_sem.at[down_slot], down),
    )
    sends = []
    for i, (src, dst, sem, peer) in enumerate(plan):
        copy = pltpu.make_async_remote_copy(
            src_ref=src, dst_ref=dst, send_sem=send_sem.at[i], recv_sem=sem,
            device_id=peer, device_id_type=MESH,
        )
        copy.start()
        sends.append(copy)
    arrivals = (
        (col_last, cols.at[0], col_sem.at[0]),
        (col_first, cols.at[1], col_sem.at[1]),
        (row_last, rows.at[0], row_sem.at[0]),
        (row_first, rows.at[1], row_sem.at[1]),
    )
    for src, dst, sem in arrivals:
        pltpu.make_async_remote_copy(
            src_ref=src, dst_ref=dst, send_sem=send_sem.at[0], recv_sem=sem,
            device_id=east, device_id_type=MESH,
        ).wait_recv()
    for copy in sends:
        copy.wait_send()
    west_out[...] = cols[0]
    east_out[...] = cols[1]
    north_out[...] = rows[0]
    south_out[...] = rows[1]


def halo_swap(col_last, col_first, row_last, row_first, collective_id):
    lon_n, lat_n = lax.axis_size("lon"), lax.axis_size("lat")
    vmem = pl.BlockSpec(memory_space=pltpu.VMEM)
    return pl.pallas_call(
        functools.partial(halo_body, lon_n, lat_n),
        out_shape=(
            jax.ShapeDtypeStruct(col_last.shape, col_last.dtype),
            jax.ShapeDtypeStruct(col_last.shape, col_last.dtype),
            jax.ShapeDtypeStruct(row_last.shape, row_last.dtype),
            jax.ShapeDtypeStruct(row_last.shape, row_last.dtype),
        ),
        in_specs=[vmem] * 4,
        out_specs=(vmem,) * 4,
        scratch_shapes=[
            pltpu.VMEM((2,) + col_last.shape, col_last.dtype),
            pltpu.VMEM((2,) + row_last.shape, row_last.dtype),
            pltpu.SemaphoreType.DMA((4,)),
            pltpu.SemaphoreType.DMA((2,)),
            pltpu.SemaphoreType.DMA((2,)),
        ],
        compiler_params=pltpu.CompilerParams(
            collective_id=collective_id, has_side_effects=True
        ),
    )(col_last, col_first, row_last, row_first)


def lev_copy(src, dst, send, recv, peer):
    return pltpu.make_async_remote_copy(
        src_ref=src, dst_ref=dst, send_sem=send, recv_sem=recv,
        device_id={"lev": peer}, device_id_type=MESH,
    )


def scatter_start(n, part_ref, pieces, sends, recvs):
    lev = lax.axis_index("lev")
    rows = part_ref.shape[1] // n
    for d in range(1, n):
        peer = lax.rem(lev + d, n)
        lev_copy(
            part_ref.at[:, pl.ds(pl.multiple_of(peer * rows, rows), rows), :],
            pieces.at[lev], sends.at[d - 1], recvs.at[lev], peer,
        ).start()
    pieces[lev] = part_ref[:, pl.ds(pl.multiple_of(lev * rows, rows), rows), :]


def scatter_finish_gather_start(n, part_ref, pieces, reduced, sends, recvs, gsends, grecvs):
    lev = lax.axis_index("lev")
    rows = part_ref.shape[1] // n
    for d in range(1, n):
        sender = lax.rem(lev + n - d, n)
        peer = lax.rem(lev + d, n)
        lev_copy(
            part_ref.at[:, pl.ds(0, rows), :], pieces.at[sender],
            sends.at[d - 1], recvs.at[sender], sender,
        ).wait_recv()
        lev_copy(
            part_ref.at[:, pl.ds(0, rows), :], pieces.at[sender],
            sends.at[d - 1], recvs.at[sender], peer,
        ).wait_send()
    total = pieces[0]
    for s in range(1, n):
        total = total + pieces[s]
    reduced[lev] = total
    for d in range(1, n):
        peer = lax.rem(lev + d, n)
        lev_copy(reduced.at[lev], reduced.at[lev], gsends.at[d - 1], grecvs.at[lev], peer).start()


def gather_finish(n, out_ref, reduced, gsends, grecvs):
    lev = lax.axis_index("lev")
    rows = out_ref.shape[1] // n
    for d in range(1, n):
        sender = lax.rem(lev + n - d, n)
        lev_copy(reduced.at[sender], reduced.at[sender], gsends.at[d - 1], grecvs.at[sender], sender).wait_recv()
        lev_copy(reduced.at[lev], reduced.at[lev], gsends.at[d - 1], grecvs.at[lev], lax.rem(lev + d, n)).wait_send()
    for q in range(n):
        out_ref[:, q * rows:(q + 1) * rows, :] = reduced[q]


def lev_scratch(n, shape, dtype):
    piece = (shape[0], shape[1] // n, shape[2])
    return [
        pltpu.VMEM((n,) + piece, dtype),
        pltpu.VMEM((n,) + piece, dtype),
        pltpu.SemaphoreType.DMA((n - 1,)),
        pltpu.SemaphoreType.DMA((n,)),
        pltpu.SemaphoreType.DMA((n - 1,)),
        pltpu.SemaphoreType.DMA((n,)),
    ]


def exchange_body(lev_n, owners, lat_n, rows_ref, part_ref, rows_out, sum_out,
                  got, row_send, row_recv, pieces, reduced, sends, recvs, gsends, grecvs):
    lat = lax.axis_index("lat")
    lev = lax.axis_index("lev")
    me = lax.axis_index("lon") * lat_n + lat

    def place(peer):
        return {"lon": peer // lat_n, "lat": lax.rem(peer, lat_n)}

    barrier = pltpu.get_barrier_semaphore()

    def greet(d, carry):
        peer = lax.rem(me + d, owners)
        pl.semaphore_signal(barrier, inc=1, device_id=place(peer), device_id_type=MESH)
        return carry

    lax.fori_loop(1, owners, greet, 0)
    for d in range(1, lev_n):
        pl.semaphore_signal(
            barrier, inc=1, device_id={"lev": lax.rem(lev + d, lev_n)}, device_id_type=MESH
        )
    pl.semaphore_wait(barrier, owners - 1 + lev_n - 1)
    scatter_start(lev_n, part_ref, pieces, sends, recvs)

    def row_copy(peer, target):
        return pltpu.make_async_remote_copy(
            src_ref=rows_ref.at[pl.ds(peer, 1)],
            dst_ref=got.at[pl.ds(target, 1)],
            send_sem=row_send.at[peer],
            recv_sem=row_recv.at[target],
            device_id=place(peer),
            device_id_type=MESH,
        )

    def send(d, carry):
        row_copy(lax.rem(me + d, owners), me).start()
        return carry

    lax.fori_loop(1, owners, send, 0)
    got[pl.ds(me, 1), :] = rows_ref[pl.ds(me, 1), :]
    scatter_finish_gather_start(lev_n, part_ref, pieces, reduced, sends, recvs, gsends, grecvs)

    def finish(d, carry):
        source = lax.rem(me + owners - d, owners)
        row_copy(lax.rem(me + d, owners), me).wait_send()
        row_copy(source, source).wait_recv()
        return carry

    lax.fori_loop(1, owners, finish, 0)
    gather_finish(lev_n, sum_out, reduced, gsends, grecvs)
    rows_out[...] = got[...]


def exchange(rows, part, collective_id):
    lev_n = lax.axis_size("lev")
    lat_n = lax.axis_size("lat")
    owners = lax.axis_size("lon") * lat_n
    vmem = pl.BlockSpec(memory_space=pltpu.VMEM)
    return pl.pallas_call(
        functools.partial(exchange_body, lev_n, owners, lat_n),
        out_shape=(
            jax.ShapeDtypeStruct(rows.shape, rows.dtype),
            jax.ShapeDtypeStruct(part.shape, part.dtype),
        ),
        in_specs=[vmem, vmem],
        out_specs=(vmem, vmem),
        scratch_shapes=[
            pltpu.VMEM(rows.shape, rows.dtype),
            pltpu.SemaphoreType.DMA((owners,)),
            pltpu.SemaphoreType.DMA((owners,)),
        ] + lev_scratch(lev_n, part.shape, part.dtype),
        compiler_params=pltpu.CompilerParams(
            collective_id=collective_id, has_side_effects=True
        ),
    )(rows, part)


def lev_direct_body(n, part_ref, out_ref, slots, send_sem, recv_sem):
    me = lax.axis_index("lev")
    barrier = pltpu.get_barrier_semaphore()
    for d in range(1, n):
        pl.semaphore_signal(
            barrier, inc=1, device_id={"lev": lax.rem(me + d, n)}, device_id_type=MESH
        )
    pl.semaphore_wait(barrier, n - 1)
    for d in range(1, n):
        lev_copy(part_ref, slots.at[me], send_sem.at[d - 1], recv_sem.at[me], lax.rem(me + d, n)).start()
    slots[me] = part_ref[...]
    for d in range(1, n):
        sender = lax.rem(me + n - d, n)
        lev_copy(part_ref, slots.at[sender], send_sem.at[d - 1], recv_sem.at[sender], sender).wait_recv()
        lev_copy(part_ref, slots.at[sender], send_sem.at[d - 1], recv_sem.at[sender], lax.rem(me + d, n)).wait_send()
    total = slots[0]
    for s in range(1, n):
        total = total + slots[s]
    out_ref[...] = total


def lev_direct(x, collective_id):
    n = lax.axis_size("lev")
    return pl.pallas_call(
        functools.partial(lev_direct_body, n),
        out_shape=jax.ShapeDtypeStruct(x.shape, x.dtype),
        in_specs=[pl.BlockSpec(memory_space=pltpu.VMEM)],
        out_specs=pl.BlockSpec(memory_space=pltpu.VMEM),
        scratch_shapes=[
            pltpu.VMEM((n,) + x.shape, x.dtype),
            pltpu.SemaphoreType.DMA((n - 1,)),
            pltpu.SemaphoreType.DMA((n,)),
        ],
        compiler_params=pltpu.CompilerParams(
            collective_id=collective_id, has_side_effects=True
        ),
    )(x)


def halo_places(lon_n, lat_n):
    lon = lax.axis_index("lon")
    lat = lax.axis_index("lat")
    half = lon_n // 2
    top = lat // (lat_n - 1)
    inner = (lat + lat_n - 1) // lat_n
    east = {"lon": lax.rem(lon + 1, lon_n)}
    west = {"lon": lax.rem(lon + lon_n - 1, lon_n)}
    up = {"lon": lax.rem(lon + half * top, lon_n), "lat": lat + 1 - top}
    down = {"lon": lax.rem(lon + half * (1 - inner), lon_n), "lat": lat - inner}
    return east, west, up, down, 1 - top, 1 - inner


def mix_halo_body(lev_n, lon_n, lat_n, p_ref, st_ref, cs_out, halo_out,
                  pieces, reduced, sends, recvs, gsends, grecvs,
                  pe_slots, pe_send, pe_recv, mixed, got, h_send, h_recv):
    lev = lax.axis_index("lev")
    pe_ref = st_ref.at[0]
    east, west, up, down, up_slot, down_slot = halo_places(lon_n, lat_n)
    barrier = pltpu.get_barrier_semaphore()
    for d in range(1, lev_n):
        pl.semaphore_signal(
            barrier, inc=1, device_id={"lev": lax.rem(lev + d, lev_n)}, device_id_type=MESH
        )
    for peer in (east, west, up, down):
        pl.semaphore_signal(barrier, inc=1, device_id=peer, device_id_type=MESH)
    pl.semaphore_wait(barrier, lev_n - 1 + 4)
    scatter_start(lev_n, p_ref, pieces, sends, recvs)
    for d in range(1, lev_n):
        lev_copy(pe_ref, pe_slots.at[lev], pe_send.at[d - 1], pe_recv.at[lev], lax.rem(lev + d, lev_n)).start()
    pe_slots[lev] = pe_ref[...]
    scatter_finish_gather_start(lev_n, p_ref, pieces, reduced, sends, recvs, gsends, grecvs)
    for d in range(1, lev_n):
        sender = lax.rem(lev + lev_n - d, lev_n)
        lev_copy(pe_ref, pe_slots.at[sender], pe_send.at[d - 1], pe_recv.at[sender], sender).wait_recv()
        lev_copy(pe_ref, pe_slots.at[sender], pe_send.at[d - 1], pe_recv.at[sender], lax.rem(lev + d, lev_n)).wait_send()
    pe_sum = pe_slots[0]
    for s in range(1, lev_n):
        pe_sum = pe_sum + pe_slots[s]
    share = st_ref[2]
    mixed[...] = (1.0 - share) * st_ref[1] + share * (pe_sum / st_ref[3])
    plan = (
        (mixed.at[0], got.at[0], h_recv.at[0], east),
        (mixed.at[1], got.at[1], h_recv.at[1], west),
        (mixed.at[2], got.at[2 + up_slot], h_recv.at[2 + up_slot], up),
        (mixed.at[3], got.at[2 + down_slot], h_recv.at[2 + down_slot], down),
    )
    copies = []
    for i, (src, dst, sem, peer) in enumerate(plan):
        copy = pltpu.make_async_remote_copy(
            src_ref=src, dst_ref=dst, send_sem=h_send.at[i], recv_sem=sem,
            device_id=peer, device_id_type=MESH,
        )
        copy.start()
        copies.append(copy)
    gather_finish(lev_n, cs_out, reduced, gsends, grecvs)
    for i in range(4):
        pltpu.make_async_remote_copy(
            src_ref=mixed.at[i], dst_ref=got.at[i], send_sem=h_send.at[i], recv_sem=h_recv.at[i],
            device_id=east, device_id_type=MESH,
        ).wait_recv()
    for copy in copies:
        copy.wait_send()
    halo_out[...] = got[...]


def mix_halo(p, st, collective_id):
    lev_n, lon_n, lat_n = lax.axis_size("lev"), lax.axis_size("lon"), lax.axis_size("lat")
    vmem = pl.BlockSpec(memory_space=pltpu.VMEM)
    return pl.pallas_call(
        functools.partial(mix_halo_body, lev_n, lon_n, lat_n),
        out_shape=(
            jax.ShapeDtypeStruct(p.shape, p.dtype),
            jax.ShapeDtypeStruct(st.shape[1:], p.dtype),
        ),
        in_specs=[vmem] * 2,
        out_specs=(vmem, vmem),
        scratch_shapes=lev_scratch(lev_n, p.shape, p.dtype) + [
            pltpu.VMEM((lev_n,) + st.shape[1:], p.dtype),
            pltpu.SemaphoreType.DMA((lev_n - 1,)),
            pltpu.SemaphoreType.DMA((lev_n,)),
            pltpu.VMEM(st.shape[1:], p.dtype),
            pltpu.VMEM(st.shape[1:], p.dtype),
            pltpu.SemaphoreType.DMA((4,)),
            pltpu.SemaphoreType.DMA((4,)),
        ],
        compiler_params=pltpu.CompilerParams(
            collective_id=collective_id, has_side_effects=True
        ),
    )(p, st)


def halo_pack_body(lon_n, lat_n, st_ref, out_ref, got, h_send, h_recv):
    east, west, up, down, up_slot, down_slot = halo_places(lon_n, lat_n)
    barrier = pltpu.get_barrier_semaphore()
    for peer in (east, west, up, down):
        pl.semaphore_signal(barrier, inc=1, device_id=peer, device_id_type=MESH)
    pl.semaphore_wait(barrier, 4)
    plan = (
        (st_ref.at[0], got.at[0], h_recv.at[0], east),
        (st_ref.at[1], got.at[1], h_recv.at[1], west),
        (st_ref.at[2], got.at[2 + up_slot], h_recv.at[2 + up_slot], up),
        (st_ref.at[3], got.at[2 + down_slot], h_recv.at[2 + down_slot], down),
    )
    copies = []
    for i, (src, dst, sem, peer) in enumerate(plan):
        copy = pltpu.make_async_remote_copy(
            src_ref=src, dst_ref=dst, send_sem=h_send.at[i], recv_sem=sem,
            device_id=peer, device_id_type=MESH,
        )
        copy.start()
        copies.append(copy)
    for i in range(4):
        pltpu.make_async_remote_copy(
            src_ref=st_ref.at[i], dst_ref=got.at[i], send_sem=h_send.at[i], recv_sem=h_recv.at[i],
            device_id=east, device_id_type=MESH,
        ).wait_recv()
    for copy in copies:
        copy.wait_send()
    out_ref[...] = got[...]


def halo_pack(st, collective_id):
    lon_n, lat_n = lax.axis_size("lon"), lax.axis_size("lat")
    vmem = pl.BlockSpec(memory_space=pltpu.VMEM)
    return pl.pallas_call(
        functools.partial(halo_pack_body, lon_n, lat_n),
        out_shape=jax.ShapeDtypeStruct(st.shape, st.dtype),
        in_specs=[vmem],
        out_specs=vmem,
        scratch_shapes=[
            pltpu.VMEM(st.shape, st.dtype),
            pltpu.SemaphoreType.DMA((4,)),
            pltpu.SemaphoreType.DMA((4,)),
        ],
        compiler_params=pltpu.CompilerParams(
            collective_id=collective_id, has_side_effects=True
        ),
    )(st)


def lev_sum(x, collective_id):
    n = lax.axis_size("lev")
    return pl.pallas_call(
        functools.partial(lev_sum_body, n),
        out_shape=jax.ShapeDtypeStruct(x.shape, x.dtype),
        in_specs=[pl.BlockSpec(memory_space=pltpu.VMEM)],
        out_specs=pl.BlockSpec(memory_space=pltpu.VMEM),
        scratch_shapes=lev_scratch(n, x.shape, x.dtype),
        compiler_params=pltpu.CompilerParams(
            collective_id=collective_id, has_side_effects=True
        ),
        cost_estimate=pl.CostEstimate(
            flops=n * x.size, bytes_accessed=(2 * n + 2) * x.size * 4, transcendentals=0
        ),
    )(x)


def from_behind(value, axis, steps):
    count = lax.axis_size(axis)
    pairs = [(source, (source + steps) % count) for source in range(count)]
    return lax.ppermute(value, axis, pairs)


def from_behind_2(block, axis, distance):
    devices = range(lax.axis_size(axis))
    route = [(i - distance, i) for i in devices if i - distance in devices]
    return lax.ppermute(block, axis, route)


def extended(x, sides, width, wrap):
    for axis, dim in sides:
        size, length = (lax.axis_size(axis), x.shape[dim])
        up = [(i, (i + 1) % size) for i in range(size if wrap else size - 1)]
        down = [(j, i) for i, j in up]
        last = lax.slice_in_dim(x, length - width, length, axis=dim)
        initial = lax.slice_in_dim(x, 0, width, axis=dim)
        before = lax.ppermute(last, axis, up)
        after = lax.ppermute(initial, axis, down)
        x = jnp.concatenate([before, x, after], axis=dim)
    return x


def mix_sum(partial_sum):
    return lax.psum(partial_sum, "lev")


def on_device(
    adjoint_field,
    east_courant,
    north_courant,
    pole_courant,
    mix_fraction,
    detrain_share,
    sounding_owner,
    sounding_cell,
    sounding_count,
    sounding_forcing,
):
    lon_count = lax.axis_size("lon")
    lat_count = lax.axis_size("lat")
    lat_place = lax.axis_index("lat")
    owner_self = lax.axis_index("lon") * lat_count + lat_place
    tracers, lev_dev, lat_rows, lon_cols = adjoint_field.shape
    step_count = sounding_forcing.shape[0]
    slot_count = sounding_forcing.shape[2]
    grid_cells = lat_rows * lon_cols
    detrain_part = jnp.sum(detrain_share, axis=0)
    owner_count = lon_count * lat_count
    cap = 4
    live_slots = jnp.arange(slot_count, dtype=jnp.int32)[None, :] < sounding_count
    values = jnp.where(live_slots[:, None, :], sounding_forcing, 0.0)
    owner_ids = sounding_owner[:, :, 0]
    slot_iota = jnp.arange(slot_count, dtype=jnp.int32)
    earlier = slot_iota[None, :, None] < slot_iota[None, None, :]
    same_owner = owner_ids[:, :, None] == owner_ids[:, None, :]
    rank = jnp.sum(jnp.logical_and(earlier, same_owner), axis=1, dtype=jnp.int32)
    position = owner_ids * cap + rank
    bucket_iota = jnp.arange(owner_count * cap, dtype=jnp.int32)
    chosen = position[:, :, None] == bucket_iota[None, None, :]
    bucket_values = jnp.sum(
        jnp.where(chosen[:, None, :, :], values[:, :, :, None], 0.0), axis=2
    )
    bucket_cell = jnp.max(
        jnp.where(chosen, sounding_cell[:, :, None] + 1, 0), axis=1
    ).astype(jnp.float32) - 1.0
    packed = jnp.concatenate([bucket_values, bucket_cell[:, None, :]], axis=1)
    packed = packed.reshape(step_count, lev_dev + 1, owner_count, cap)
    packed = jnp.transpose(packed, (2, 0, 1, 3))
    row_width = step_count * (lev_dev + 1) * cap
    rows = jnp.pad(packed.reshape(owner_count, row_width), ((0, 0), (0, 128 - row_width)))
    early_part = jnp.concatenate(
        [jnp.sum(detrain_share[None] * adjoint_field, axis=1), detrain_part[None]], axis=0
    )
    arrived, early = exchange(rows, early_part, 0)
    arrived = arrived[:, :row_width].reshape(owner_count, step_count, lev_dev + 1, cap)
    arrived = jnp.transpose(arrived, (1, 2, 0, 3)).reshape(
        step_count, lev_dev + 1, owner_count * cap
    )
    cells = arrived[:, lev_dev, :].astype(jnp.int32)
    row_hit = (cells // lon_cols)[:, :, None] == jnp.arange(lat_rows, dtype=jnp.int32)
    col_hit = (cells % lon_cols)[:, :, None] == jnp.arange(lon_cols, dtype=jnp.int32)
    spread = jnp.where(row_hit[:, None, :, :], arrived[:, :lev_dev, :, None], 0.0)
    forcing_grid = jnp.einsum(
        "tker,tec->tkrc", spread, col_hit.astype(jnp.float32), precision=lax.Precision.HIGHEST
    )
    row_index = jnp.arange(lat_rows, dtype=jnp.int32)[None, :, None]
    at_top = jnp.logical_and(lat_place == lat_count - 1, row_index == lat_rows - 1)
    at_bottom = jnp.logical_and(lat_place == 0, row_index == 0)
    upwind_east = jnp.maximum(east_courant, 0.0)
    forcing_part = jnp.sum(detrain_share * forcing_grid[step_count - 1], axis=0)
    forcing_sum = lev_direct(forcing_part[None], 4)[0]
    adjoint = adjoint_field
    for position in range(step_count):
        step_now = step_count - 1 - position
        adjoint = adjoint + forcing_grid[step_now][None]
        if position == 0:
            column_sum = early[:tracers] + forcing_sum[None]
            total_detrain = early[tracers]
        else:
            partial_sum = jnp.sum(detrain_share[None] * adjoint, axis=1)
            planes = tracers * lev_dev

            def spread(x, width, fill=0.0):
                x = jnp.broadcast_to(x, (tracers, lev_dev, width)).reshape(planes, width)
                return jnp.pad(x, ((0, 0), (0, lon_cols - width)), constant_values=fill)

            def edges(x, fill=0.0):
                return jnp.stack([
                    spread(x[..., :, -1], lat_rows, fill), spread(x[..., :, 0], lat_rows, fill),
                    spread(x[..., -1, :], lon_cols), spread(x[..., 0, :], lon_cols),
                ])

            column_sum, halos = mix_halo(
                partial_sum,
                jnp.stack([
                    edges(partial_sum[:, None]),
                    edges(adjoint),
                    edges(mix_fraction[None]),
                    edges(total_detrain[None, None], 1.0),
                ]),
                5,
            )
        adjoint = (1.0 - mix_fraction)[None] * adjoint + mix_fraction[None] * (
            column_sum / total_detrain
        )[:, None]
        if position == 1:
            west_halo = halos[0, :, :lat_rows]
            east_halo = halos[1, :, :lat_rows]
            north_halo = halos[2]
            south_halo = halos[3]
        planes = tracers * lev_dev
        if position == 0:
            col_last = adjoint[:, :, :, -1].reshape(planes, lat_rows)
            col_first = adjoint[:, :, :, 0].reshape(planes, lat_rows)
            row_last = adjoint[:, :, -1, :].reshape(planes, lon_cols)
            row_first = adjoint[:, :, 0, :].reshape(planes, lon_cols)
            if position == 0:
                col_last = jnp.concatenate([col_last, east_courant[:, :, -1]], axis=0)
                col_first = jnp.concatenate([col_first, east_courant[:, :, 0]], axis=0)
                row_last = jnp.concatenate([row_last, north_courant[:, -1, :]], axis=0)
                row_first = jnp.concatenate([row_first, pole_courant], axis=0)
            pad_lanes = ((0, 0), (0, lon_cols - lat_rows))
            got = halo_pack(
                jnp.stack([
                    jnp.pad(col_last, pad_lanes), jnp.pad(col_first, pad_lanes),
                    row_last, row_first,
                ]),
                2,
            )
            west_halo, east_halo = got[0, :, :lat_rows], got[1, :, :lat_rows]
            north_halo, south_halo = got[2], got[3]
            if position == 0:
                west_wind = jnp.concatenate(
                    [west_halo[planes:, :, None], east_courant[:, :, :-1]], axis=2
                )
                partner_top = north_halo[planes:]
                south_wind = jnp.concatenate(
                    [south_halo[planes:, None, :], north_courant[:, :-1, :]], axis=1
                )
                partner_pole = south_halo[planes:]
                upwind_west = -jnp.minimum(west_wind, 0.0)
                upwind_north = jnp.maximum(north_courant, 0.0) + jnp.where(
                    at_top, -jnp.minimum(partner_top, 0.0)[:, None, :], 0.0
                )
                upwind_south = jnp.where(
                    at_bottom,
                    (jnp.maximum(pole_courant, 0.0) - jnp.minimum(partner_pole, 0.0))[:, None, :],
                    -jnp.minimum(south_wind, 0.0),
                )
                west_halo, east_halo = west_halo[:planes], east_halo[:planes]
                north_halo, south_halo = north_halo[:planes], south_halo[:planes]
        east_side = jnp.concatenate(
            [adjoint[:, :, :, 1:], east_halo.reshape(tracers, lev_dev, lat_rows, 1)], axis=3
        )
        west_side = jnp.concatenate(
            [west_halo.reshape(tracers, lev_dev, lat_rows, 1), adjoint[:, :, :, :-1]], axis=3
        )
        north_side = jnp.concatenate(
            [adjoint[:, :, 1:, :], north_halo.reshape(tracers, lev_dev, 1, lon_cols)], axis=2
        )
        south_side = jnp.concatenate(
            [south_halo.reshape(tracers, lev_dev, 1, lon_cols), adjoint[:, :, :-1, :]], axis=2
        )
        adjoint = (
            adjoint
            + upwind_east * (east_side - adjoint)
            + upwind_west * (west_side - adjoint)
            + upwind_north * (north_side - adjoint)
            + upwind_south * (south_side - adjoint)
        )
    return adjoint


def solution(mesh):
    return jax.shard_map(
        on_device,
        mesh=mesh,
        in_specs=(
            P(None, "lev", "lat", "lon"),
            P("lev", "lat", "lon"),
            P("lev", "lat", "lon"),
            P("lev", "lon"),
            P("lev", "lat", "lon"),
            P("lev", "lat", "lon"),
            P(None, ("lon", "lat"), None),
            P(None, ("lon", "lat")),
            P(None, ("lon", "lat")),
            P(None, "lev", ("lon", "lat")),
        ),
        out_specs=P(None, "lev", "lat", "lon"),
        check_vma=False,
    )
```

```python
import functools

import jax
import jax.numpy as jnp
from jax import lax
from jax.experimental import pallas as pl
from jax.experimental.pallas import tpu as pltpu
from jax.sharding import PartitionSpec as P

MESH = pl.DeviceIdType.MESH


def lev_sum_body(n, part_ref, out_ref, pieces, reduced, sends, recvs, gsends, grecvs):
    lev = lax.axis_index("lev")
    barrier = pltpu.get_barrier_semaphore()
    for d in range(1, n):
        pl.semaphore_signal(
            barrier, inc=1, device_id={"lev": lax.rem(lev + d, n)}, device_id_type=MESH
        )
    pl.semaphore_wait(barrier, n - 1)
    scatter_start(n, part_ref, pieces, sends, recvs)
    scatter_finish_gather_start(n, part_ref, pieces, reduced, sends, recvs, gsends, grecvs)
    gather_finish(n, out_ref, reduced, gsends, grecvs)


def halo_body(lon_n, lat_n, col_last, col_first, row_last, row_first,
              west_out, east_out, north_out, south_out, cols, rows, send_sem, col_sem, row_sem):
    lon = lax.axis_index("lon")
    lat = lax.axis_index("lat")
    half = lon_n // 2
    top = lat // (lat_n - 1)
    inner = (lat + lat_n - 1) // lat_n
    east = {"lon": lax.rem(lon + 1, lon_n)}
    west = {"lon": lax.rem(lon + lon_n - 1, lon_n)}
    up = {"lon": lax.rem(lon + half * top, lon_n), "lat": lat + 1 - top}
    down = {"lon": lax.rem(lon + half * (1 - inner), lon_n), "lat": lat - inner}
    up_slot = 1 - top
    down_slot = 1 - inner
    barrier = pltpu.get_barrier_semaphore()
    for peer in (east, west, up, down):
        pl.semaphore_signal(barrier, inc=1, device_id=peer, device_id_type=MESH)
    pl.semaphore_wait(barrier, 4)
    plan = (
        (col_last, cols.at[0], col_sem.at[0], east),
        (col_first, cols.at[1], col_sem.at[1], west),
        (row_last, rows.at[up_slot], row_sem.at[up_slot], up),
        (row_first, rows.at[down_slot], row_sem.at[down_slot], down),
    )
    sends = []
    for i, (src, dst, sem, peer) in enumerate(plan):
        copy = pltpu.make_async_remote_copy(
            src_ref=src, dst_ref=dst, send_sem=send_sem.at[i], recv_sem=sem,
            device_id=peer, device_id_type=MESH,
        )
        copy.start()
        sends.append(copy)
    arrivals = (
        (col_last, cols.at[0], col_sem.at[0]),
        (col_first, cols.at[1], col_sem.at[1]),
        (row_last, rows.at[0], row_sem.at[0]),
        (row_first, rows.at[1], row_sem.at[1]),
    )
    for src, dst, sem in arrivals:
        pltpu.make_async_remote_copy(
            src_ref=src, dst_ref=dst, send_sem=send_sem.at[0], recv_sem=sem,
            device_id=east, device_id_type=MESH,
        ).wait_recv()
    for copy in sends:
        copy.wait_send()
    west_out[...] = cols[0]
    east_out[...] = cols[1]
    north_out[...] = rows[0]
    south_out[...] = rows[1]


def halo_swap(col_last, col_first, row_last, row_first, collective_id):
    lon_n, lat_n = lax.axis_size("lon"), lax.axis_size("lat")
    vmem = pl.BlockSpec(memory_space=pltpu.VMEM)
    return pl.pallas_call(
        functools.partial(halo_body, lon_n, lat_n),
        out_shape=(
            jax.ShapeDtypeStruct(col_last.shape, col_last.dtype),
            jax.ShapeDtypeStruct(col_last.shape, col_last.dtype),
            jax.ShapeDtypeStruct(row_last.shape, row_last.dtype),
            jax.ShapeDtypeStruct(row_last.shape, row_last.dtype),
        ),
        in_specs=[vmem] * 4,
        out_specs=(vmem,) * 4,
        scratch_shapes=[
            pltpu.VMEM((2,) + col_last.shape, col_last.dtype),
            pltpu.VMEM((2,) + row_last.shape, row_last.dtype),
            pltpu.SemaphoreType.DMA((4,)),
            pltpu.SemaphoreType.DMA((2,)),
            pltpu.SemaphoreType.DMA((2,)),
        ],
        compiler_params=pltpu.CompilerParams(
            collective_id=collective_id, has_side_effects=True
        ),
    )(col_last, col_first, row_last, row_first)


def lev_copy(src, dst, send, recv, peer):
    return pltpu.make_async_remote_copy(
        src_ref=src, dst_ref=dst, send_sem=send, recv_sem=recv,
        device_id={"lev": peer}, device_id_type=MESH,
    )


def scatter_start(n, part_ref, pieces, sends, recvs):
    lev = lax.axis_index("lev")
    rows = part_ref.shape[1] // n
    for d in range(1, n):
        peer = lax.rem(lev + d, n)
        lev_copy(
            part_ref.at[:, pl.ds(pl.multiple_of(peer * rows, rows), rows), :],
            pieces.at[lev], sends.at[d - 1], recvs.at[lev], peer,
        ).start()
    pieces[lev] = part_ref[:, pl.ds(pl.multiple_of(lev * rows, rows), rows), :]


def scatter_finish_gather_start(n, part_ref, pieces, reduced, sends, recvs, gsends, grecvs):
    lev = lax.axis_index("lev")
    rows = part_ref.shape[1] // n
    for d in range(1, n):
        sender = lax.rem(lev + n - d, n)
        peer = lax.rem(lev + d, n)
        lev_copy(
            part_ref.at[:, pl.ds(0, rows), :], pieces.at[sender],
            sends.at[d - 1], recvs.at[sender], sender,
        ).wait_recv()
        lev_copy(
            part_ref.at[:, pl.ds(0, rows), :], pieces.at[sender],
            sends.at[d - 1], recvs.at[sender], peer,
        ).wait_send()
    total = pieces[0]
    for s in range(1, n):
        total = total + pieces[s]
    reduced[lev] = total
    for d in range(1, n):
        peer = lax.rem(lev + d, n)
        lev_copy(reduced.at[lev], reduced.at[lev], gsends.at[d - 1], grecvs.at[lev], peer).start()


def gather_finish(n, out_ref, reduced, gsends, grecvs):
    lev = lax.axis_index("lev")
    rows = out_ref.shape[1] // n
    for d in range(1, n):
        sender = lax.rem(lev + n - d, n)
        lev_copy(reduced.at[sender], reduced.at[sender], gsends.at[d - 1], grecvs.at[sender], sender).wait_recv()
        lev_copy(reduced.at[lev], reduced.at[lev], gsends.at[d - 1], grecvs.at[lev], lax.rem(lev + d, n)).wait_send()
    for q in range(n):
        out_ref[:, q * rows:(q + 1) * rows, :] = reduced[q]


def lev_scratch(n, shape, dtype):
    piece = (shape[0], shape[1] // n, shape[2])
    return [
        pltpu.VMEM((n,) + piece, dtype),
        pltpu.VMEM((n,) + piece, dtype),
        pltpu.SemaphoreType.DMA((n - 1,)),
        pltpu.SemaphoreType.DMA((n,)),
        pltpu.SemaphoreType.DMA((n - 1,)),
        pltpu.SemaphoreType.DMA((n,)),
    ]


def exchange_body(lev_n, owners, lat_n, rows_ref, part_ref, rows_out, sum_out,
                  got, row_send, row_recv, pieces, reduced, sends, recvs, gsends, grecvs):
    lat = lax.axis_index("lat")
    lev = lax.axis_index("lev")
    me = lax.axis_index("lon") * lat_n + lat

    def place(peer):
        return {"lon": peer // lat_n, "lat": lax.rem(peer, lat_n)}

    barrier = pltpu.get_barrier_semaphore()

    def greet(d, carry):
        peer = lax.rem(me + d, owners)
        pl.semaphore_signal(barrier, inc=1, device_id=place(peer), device_id_type=MESH)
        return carry

    lax.fori_loop(1, owners, greet, 0)
    for d in range(1, lev_n):
        pl.semaphore_signal(
            barrier, inc=1, device_id={"lev": lax.rem(lev + d, lev_n)}, device_id_type=MESH
        )
    pl.semaphore_wait(barrier, owners - 1 + lev_n - 1)
    scatter_start(lev_n, part_ref, pieces, sends, recvs)

    def row_copy(peer, target):
        return pltpu.make_async_remote_copy(
            src_ref=rows_ref.at[pl.ds(peer, 1)],
            dst_ref=got.at[pl.ds(target, 1)],
            send_sem=row_send.at[peer],
            recv_sem=row_recv.at[target],
            device_id=place(peer),
            device_id_type=MESH,
        )

    def send(d, carry):
        row_copy(lax.rem(me + d, owners), me).start()
        return carry

    lax.fori_loop(1, owners, send, 0)
    got[pl.ds(me, 1), :] = rows_ref[pl.ds(me, 1), :]
    scatter_finish_gather_start(lev_n, part_ref, pieces, reduced, sends, recvs, gsends, grecvs)

    def finish(d, carry):
        source = lax.rem(me + owners - d, owners)
        row_copy(lax.rem(me + d, owners), me).wait_send()
        row_copy(source, source).wait_recv()
        return carry

    lax.fori_loop(1, owners, finish, 0)
    gather_finish(lev_n, sum_out, reduced, gsends, grecvs)
    rows_out[...] = got[...]


def exchange(rows, part, collective_id):
    lev_n = lax.axis_size("lev")
    lat_n = lax.axis_size("lat")
    owners = lax.axis_size("lon") * lat_n
    vmem = pl.BlockSpec(memory_space=pltpu.VMEM)
    return pl.pallas_call(
        functools.partial(exchange_body, lev_n, owners, lat_n),
        out_shape=(
            jax.ShapeDtypeStruct(rows.shape, rows.dtype),
            jax.ShapeDtypeStruct(part.shape, part.dtype),
        ),
        in_specs=[vmem, vmem],
        out_specs=(vmem, vmem),
        scratch_shapes=[
            pltpu.VMEM(rows.shape, rows.dtype),
            pltpu.SemaphoreType.DMA((owners,)),
            pltpu.SemaphoreType.DMA((owners,)),
        ] + lev_scratch(lev_n, part.shape, part.dtype),
        compiler_params=pltpu.CompilerParams(
            collective_id=collective_id, has_side_effects=True
        ),
    )(rows, part)


def lev_direct_body(n, part_ref, out_ref, slots, send_sem, recv_sem):
    me = lax.axis_index("lev")
    barrier = pltpu.get_barrier_semaphore()
    for d in range(1, n):
        pl.semaphore_signal(
            barrier, inc=1, device_id={"lev": lax.rem(me + d, n)}, device_id_type=MESH
        )
    pl.semaphore_wait(barrier, n - 1)
    for d in range(1, n):
        lev_copy(part_ref, slots.at[me], send_sem.at[d - 1], recv_sem.at[me], lax.rem(me + d, n)).start()
    slots[me] = part_ref[...]
    for d in range(1, n):
        sender = lax.rem(me + n - d, n)
        lev_copy(part_ref, slots.at[sender], send_sem.at[d - 1], recv_sem.at[sender], sender).wait_recv()
        lev_copy(part_ref, slots.at[sender], send_sem.at[d - 1], recv_sem.at[sender], lax.rem(me + d, n)).wait_send()
    total = slots[0]
    for s in range(1, n):
        total = total + slots[s]
    out_ref[...] = total


def lev_direct(x, collective_id):
    n = lax.axis_size("lev")
    return pl.pallas_call(
        functools.partial(lev_direct_body, n),
        out_shape=jax.ShapeDtypeStruct(x.shape, x.dtype),
        in_specs=[pl.BlockSpec(memory_space=pltpu.VMEM)],
        out_specs=pl.BlockSpec(memory_space=pltpu.VMEM),
        scratch_shapes=[
            pltpu.VMEM((n,) + x.shape, x.dtype),
            pltpu.SemaphoreType.DMA((n - 1,)),
            pltpu.SemaphoreType.DMA((n,)),
        ],
        compiler_params=pltpu.CompilerParams(
            collective_id=collective_id, has_side_effects=True
        ),
    )(x)


def halo_places(lon_n, lat_n):
    lon = lax.axis_index("lon")
    lat = lax.axis_index("lat")
    half = lon_n // 2
    top = lat // (lat_n - 1)
    inner = (lat + lat_n - 1) // lat_n
    east = {"lon": lax.rem(lon + 1, lon_n)}
    west = {"lon": lax.rem(lon + lon_n - 1, lon_n)}
    up = {"lon": lax.rem(lon + half * top, lon_n), "lat": lat + 1 - top}
    down = {"lon": lax.rem(lon + half * (1 - inner), lon_n), "lat": lat - inner}
    return east, west, up, down, 1 - top, 1 - inner


def mix_halo_body(lev_n, lon_n, lat_n, p_ref, pe_ref, st_ref, cs_out, halo_out,
                  pieces, reduced, sends, recvs, gsends, grecvs,
                  pe_slots, pe_send, pe_recv, spread, mixed, got, h_send, h_recv):
    lev = lax.axis_index("lev")
    east, west, up, down, up_slot, down_slot = halo_places(lon_n, lat_n)
    barrier = pltpu.get_barrier_semaphore()
    for d in range(1, lev_n):
        pl.semaphore_signal(
            barrier, inc=1, device_id={"lev": lax.rem(lev + d, lev_n)}, device_id_type=MESH
        )
    for peer in (east, west, up, down):
        pl.semaphore_signal(barrier, inc=1, device_id=peer, device_id_type=MESH)
    pl.semaphore_wait(barrier, lev_n - 1 + 4)
    scatter_start(lev_n, p_ref, pieces, sends, recvs)
    for d in range(1, lev_n):
        lev_copy(pe_ref, pe_slots.at[lev], pe_send.at[d - 1], pe_recv.at[lev], lax.rem(lev + d, lev_n)).start()
    pe_slots[lev] = pe_ref[...]
    scatter_finish_gather_start(lev_n, p_ref, pieces, reduced, sends, recvs, gsends, grecvs)
    for d in range(1, lev_n):
        sender = lax.rem(lev + lev_n - d, lev_n)
        lev_copy(pe_ref, pe_slots.at[sender], pe_send.at[d - 1], pe_recv.at[sender], sender).wait_recv()
        lev_copy(pe_ref, pe_slots.at[sender], pe_send.at[d - 1], pe_recv.at[sender], lax.rem(lev + d, lev_n)).wait_send()
    pe_sum = pe_slots[0]
    for s in range(1, lev_n):
        pe_sum = pe_sum + pe_slots[s]
    tracers = pe_ref.shape[1]
    copies_k = spread.shape[1] // tracers
    for k in range(copies_k):
        spread[:, pl.ds(k, tracers, stride=copies_k), :] = pe_sum
    share = st_ref[1]
    mixed[...] = (1.0 - share) * st_ref[0] + share * (spread[...] / st_ref[2])
    plan = (
        (mixed.at[0], got.at[0], h_recv.at[0], east),
        (mixed.at[0], got.at[1], h_recv.at[1], west),
        (mixed.at[1], got.at[2 + up_slot], h_recv.at[2 + up_slot], up),
        (mixed.at[2], got.at[2 + down_slot], h_recv.at[2 + down_slot], down),
    )
    copies = []
    for i, (src, dst, sem, peer) in enumerate(plan):
        copy = pltpu.make_async_remote_copy(
            src_ref=src, dst_ref=dst, send_sem=h_send.at[i], recv_sem=sem,
            device_id=peer, device_id_type=MESH,
        )
        copy.start()
        copies.append(copy)
    gather_finish(lev_n, cs_out, reduced, gsends, grecvs)
    for i in range(4):
        pltpu.make_async_remote_copy(
            src_ref=mixed.at[0], dst_ref=got.at[i], send_sem=h_send.at[i], recv_sem=h_recv.at[i],
            device_id=east, device_id_type=MESH,
        ).wait_recv()
    for copy in copies:
        copy.wait_send()
    halo_out[...] = got[...]


def mix_halo(p, pe, st, collective_id):
    lev_n, lon_n, lat_n = lax.axis_size("lev"), lax.axis_size("lon"), lax.axis_size("lat")
    vmem = pl.BlockSpec(memory_space=pltpu.VMEM)
    edge_shape = st.shape[1:]
    halo_shape = (4,) + edge_shape[1:]
    return pl.pallas_call(
        functools.partial(mix_halo_body, lev_n, lon_n, lat_n),
        out_shape=(
            jax.ShapeDtypeStruct(p.shape, p.dtype),
            jax.ShapeDtypeStruct(halo_shape, p.dtype),
        ),
        in_specs=[vmem] * 3,
        out_specs=(vmem, vmem),
        scratch_shapes=lev_scratch(lev_n, p.shape, p.dtype) + [
            pltpu.VMEM((lev_n,) + pe.shape, p.dtype),
            pltpu.SemaphoreType.DMA((lev_n - 1,)),
            pltpu.SemaphoreType.DMA((lev_n,)),
            pltpu.VMEM(edge_shape, p.dtype),
            pltpu.VMEM(edge_shape, p.dtype),
            pltpu.VMEM(halo_shape, p.dtype),
            pltpu.SemaphoreType.DMA((4,)),
            pltpu.SemaphoreType.DMA((4,)),
        ],
        compiler_params=pltpu.CompilerParams(
            collective_id=collective_id, has_side_effects=True
        ),
    )(p, pe, st)


def lev_sum(x, collective_id):
    n = lax.axis_size("lev")
    return pl.pallas_call(
        functools.partial(lev_sum_body, n),
        out_shape=jax.ShapeDtypeStruct(x.shape, x.dtype),
        in_specs=[pl.BlockSpec(memory_space=pltpu.VMEM)],
        out_specs=pl.BlockSpec(memory_space=pltpu.VMEM),
        scratch_shapes=lev_scratch(n, x.shape, x.dtype),
        compiler_params=pltpu.CompilerParams(
            collective_id=collective_id, has_side_effects=True
        ),
        cost_estimate=pl.CostEstimate(
            flops=n * x.size, bytes_accessed=(2 * n + 2) * x.size * 4, transcendentals=0
        ),
    )(x)


def from_behind(value, axis, steps):
    count = lax.axis_size(axis)
    pairs = [(source, (source + steps) % count) for source in range(count)]
    return lax.ppermute(value, axis, pairs)


def from_behind_2(block, axis, distance):
    devices = range(lax.axis_size(axis))
    route = [(i - distance, i) for i in devices if i - distance in devices]
    return lax.ppermute(block, axis, route)


def extended(x, sides, width, wrap):
    for axis, dim in sides:
        size, length = (lax.axis_size(axis), x.shape[dim])
        up = [(i, (i + 1) % size) for i in range(size if wrap else size - 1)]
        down = [(j, i) for i, j in up]
        last = lax.slice_in_dim(x, length - width, length, axis=dim)
        initial = lax.slice_in_dim(x, 0, width, axis=dim)
        before = lax.ppermute(last, axis, up)
        after = lax.ppermute(initial, axis, down)
        x = jnp.concatenate([before, x, after], axis=dim)
    return x


def mix_sum(partial_sum):
    return lax.psum(partial_sum, "lev")


def on_device(
    adjoint_field,
    east_courant,
    north_courant,
    pole_courant,
    mix_fraction,
    detrain_share,
    sounding_owner,
    sounding_cell,
    sounding_count,
    sounding_forcing,
):
    lon_count = lax.axis_size("lon")
    lat_count = lax.axis_size("lat")
    lat_place = lax.axis_index("lat")
    owner_self = lax.axis_index("lon") * lat_count + lat_place
    tracers, lev_dev, lat_rows, lon_cols = adjoint_field.shape
    step_count = sounding_forcing.shape[0]
    slot_count = sounding_forcing.shape[2]
    grid_cells = lat_rows * lon_cols
    detrain_part = jnp.sum(detrain_share, axis=0)
    owner_count = lon_count * lat_count
    cap = 4
    live_slots = jnp.arange(slot_count, dtype=jnp.int32)[None, :] < sounding_count
    values = jnp.where(live_slots[:, None, :], sounding_forcing, 0.0)
    owner_ids = sounding_owner[:, :, 0]
    slot_iota = jnp.arange(slot_count, dtype=jnp.int32)
    earlier = slot_iota[None, :, None] < slot_iota[None, None, :]
    same_owner = owner_ids[:, :, None] == owner_ids[:, None, :]
    rank = jnp.sum(jnp.logical_and(earlier, same_owner), axis=1, dtype=jnp.int32)
    position = owner_ids * cap + rank
    bucket_iota = jnp.arange(owner_count * cap, dtype=jnp.int32)
    chosen = position[:, :, None] == bucket_iota[None, None, :]
    bucket_values = jnp.sum(
        jnp.where(chosen[:, None, :, :], values[:, :, :, None], 0.0), axis=2
    )
    bucket_cell = jnp.max(
        jnp.where(chosen, sounding_cell[:, :, None] + 1, 0), axis=1
    ).astype(jnp.float32) - 1.0
    packed = jnp.concatenate([bucket_values, bucket_cell[:, None, :]], axis=1)
    packed = packed.reshape(step_count, lev_dev + 1, owner_count, cap)
    packed = jnp.transpose(packed, (2, 0, 1, 3))
    row_width = step_count * (lev_dev + 1) * cap
    rows = jnp.pad(packed.reshape(owner_count, row_width), ((0, 0), (0, 128 - row_width)))
    early_part = jnp.concatenate(
        [jnp.sum(detrain_share[None] * adjoint_field, axis=1), detrain_part[None]], axis=0
    )
    arrived, early = exchange(rows, early_part, 0)
    arrived = arrived[:, :row_width].reshape(owner_count, step_count, lev_dev + 1, cap)
    arrived = jnp.transpose(arrived, (1, 2, 0, 3)).reshape(
        step_count, lev_dev + 1, owner_count * cap
    )
    cells = arrived[:, lev_dev, :].astype(jnp.int32)
    row_hit = (cells // lon_cols)[:, :, None] == jnp.arange(lat_rows, dtype=jnp.int32)
    col_hit = (cells % lon_cols)[:, :, None] == jnp.arange(lon_cols, dtype=jnp.int32)
    spread = jnp.where(row_hit[:, None, :, :], arrived[:, :lev_dev, :, None], 0.0)
    forcing_grid = jnp.einsum(
        "tker,tec->tkrc", spread, col_hit.astype(jnp.float32), precision=lax.Precision.HIGHEST
    )
    row_index = jnp.arange(lat_rows, dtype=jnp.int32)[None, :, None]
    at_top = jnp.logical_and(lat_place == lat_count - 1, row_index == lat_rows - 1)
    at_bottom = jnp.logical_and(lat_place == 0, row_index == 0)
    upwind_east = jnp.maximum(east_courant, 0.0)
    forcing_part = jnp.sum(detrain_share * forcing_grid[step_count - 1], axis=0)
    forcing_sum = lev_direct(forcing_part[None], 4)[0]
    adjoint = adjoint_field
    for position in range(step_count):
        step_now = step_count - 1 - position
        adjoint = adjoint + forcing_grid[step_now][None]
        if position == 0:
            column_sum = early[:tracers] + forcing_sum[None]
            total_detrain = early[tracers]
        else:
            partial_sum = jnp.sum(detrain_share[None] * adjoint, axis=1)
            planes = tracers * lev_dev

            def packed(x, fill=0.0):
                x = jnp.broadcast_to(x, (tracers, lev_dev) + x.shape[2:]).reshape(
                    (planes,) + x.shape[2:]
                )
                return x

            def edge_set(x, fill=0.0):
                rest = jnp.full((planes, lon_cols - 2 * lat_rows), fill, jnp.float32)
                cols = jnp.concatenate(
                    [packed(x[..., :, -1]), packed(x[..., :, 0]), rest], axis=1
                )
                return jnp.stack([cols, packed(x[..., -1, :]), packed(x[..., 0, :])])

            part_rest = jnp.zeros((tracers, lon_cols - 2 * lat_rows), jnp.float32)
            part_edges = jnp.stack([
                jnp.concatenate([partial_sum[:, :, -1], partial_sum[:, :, 0], part_rest], axis=1),
                partial_sum[:, -1, :],
                partial_sum[:, 0, :],
            ])
            column_sum, halos = mix_halo(
                partial_sum,
                part_edges,
                jnp.stack([
                    edge_set(adjoint),
                    edge_set(mix_fraction[None]),
                    edge_set(total_detrain[None, None], 1.0),
                ]),
                5,
            )
        adjoint = (1.0 - mix_fraction)[None] * adjoint + mix_fraction[None] * (
            column_sum / total_detrain
        )[:, None]
        if position == 1:
            west_halo = halos[0, :, :lat_rows]
            east_halo = halos[1, :, lat_rows:2 * lat_rows]
            north_halo = halos[2]
            south_halo = halos[3]
        planes = tracers * lev_dev
        if position == 0:
            col_last = adjoint[:, :, :, -1].reshape(planes, lat_rows)
            col_first = adjoint[:, :, :, 0].reshape(planes, lat_rows)
            row_last = adjoint[:, :, -1, :].reshape(planes, lon_cols)
            row_first = adjoint[:, :, 0, :].reshape(planes, lon_cols)
            if position == 0:
                col_last = jnp.concatenate([col_last, east_courant[:, :, -1]], axis=0)
                col_first = jnp.concatenate([col_first, east_courant[:, :, 0]], axis=0)
                row_last = jnp.concatenate([row_last, north_courant[:, -1, :]], axis=0)
                row_first = jnp.concatenate([row_first, pole_courant], axis=0)
            west_halo, east_halo, north_halo, south_halo = halo_swap(
                col_last, col_first, row_last, row_first, 2 + position
            )
            if position == 0:
                west_wind = jnp.concatenate(
                    [west_halo[planes:, :, None], east_courant[:, :, :-1]], axis=2
                )
                partner_top = north_halo[planes:]
                south_wind = jnp.concatenate(
                    [south_halo[planes:, None, :], north_courant[:, :-1, :]], axis=1
                )
                partner_pole = south_halo[planes:]
                upwind_west = -jnp.minimum(west_wind, 0.0)
                upwind_north = jnp.maximum(north_courant, 0.0) + jnp.where(
                    at_top, -jnp.minimum(partner_top, 0.0)[:, None, :], 0.0
                )
                upwind_south = jnp.where(
                    at_bottom,
                    (jnp.maximum(pole_courant, 0.0) - jnp.minimum(partner_pole, 0.0))[:, None, :],
                    -jnp.minimum(south_wind, 0.0),
                )
                west_halo, east_halo = west_halo[:planes], east_halo[:planes]
                north_halo, south_halo = north_halo[:planes], south_halo[:planes]
        east_side = jnp.concatenate(
            [adjoint[:, :, :, 1:], east_halo.reshape(tracers, lev_dev, lat_rows, 1)], axis=3
        )
        west_side = jnp.concatenate(
            [west_halo.reshape(tracers, lev_dev, lat_rows, 1), adjoint[:, :, :, :-1]], axis=3
        )
        north_side = jnp.concatenate(
            [adjoint[:, :, 1:, :], north_halo.reshape(tracers, lev_dev, 1, lon_cols)], axis=2
        )
        south_side = jnp.concatenate(
            [south_halo.reshape(tracers, lev_dev, 1, lon_cols), adjoint[:, :, :-1, :]], axis=2
        )
        adjoint = (
            adjoint
            + upwind_east * (east_side - adjoint)
            + upwind_west * (west_side - adjoint)
            + upwind_north * (north_side - adjoint)
            + upwind_south * (south_side - adjoint)
        )
    return adjoint


def solution(mesh):
    return jax.shard_map(
        on_device,
        mesh=mesh,
        in_specs=(
            P(None, "lev", "lat", "lon"),
            P("lev", "lat", "lon"),
            P("lev", "lat", "lon"),
            P("lev", "lon"),
            P("lev", "lat", "lon"),
            P("lev", "lat", "lon"),
            P(None, ("lon", "lat"), None),
            P(None, ("lon", "lat")),
            P(None, ("lon", "lat")),
            P(None, "lev", ("lon", "lat")),
        ),
        out_specs=P(None, "lev", "lat", "lon"),
        check_vma=False,
    )
```

```python
import functools

import jax
import jax.numpy as jnp
from jax import lax
from jax.experimental import pallas as pl
from jax.experimental.pallas import tpu as pltpu
from jax.sharding import PartitionSpec as P

MESH = pl.DeviceIdType.MESH


def lev_sum_body(n, part_ref, out_ref, pieces, reduced, sends, recvs, gsends, grecvs):
    lev = lax.axis_index("lev")
    barrier = pltpu.get_barrier_semaphore()
    for d in range(1, n):
        pl.semaphore_signal(
            barrier, inc=1, device_id={"lev": lax.rem(lev + d, n)}, device_id_type=MESH
        )
    pl.semaphore_wait(barrier, n - 1)
    scatter_start(n, part_ref, pieces, sends, recvs)
    scatter_finish_gather_start(n, part_ref, pieces, reduced, sends, recvs, gsends, grecvs)
    gather_finish(n, out_ref, reduced, gsends, grecvs)


def halo_body(lon_n, lat_n, col_last, col_first, row_last, row_first,
              west_out, east_out, north_out, south_out, cols, rows, send_sem, col_sem, row_sem):
    lon = lax.axis_index("lon")
    lat = lax.axis_index("lat")
    half = lon_n // 2
    top = lat // (lat_n - 1)
    inner = (lat + lat_n - 1) // lat_n
    east = {"lon": lax.rem(lon + 1, lon_n)}
    west = {"lon": lax.rem(lon + lon_n - 1, lon_n)}
    up = {"lon": lax.rem(lon + half * top, lon_n), "lat": lat + 1 - top}
    down = {"lon": lax.rem(lon + half * (1 - inner), lon_n), "lat": lat - inner}
    up_slot = 1 - top
    down_slot = 1 - inner
    barrier = pltpu.get_barrier_semaphore()
    for peer in (east, west, up, down):
        pl.semaphore_signal(barrier, inc=1, device_id=peer, device_id_type=MESH)
    pl.semaphore_wait(barrier, 4)
    plan = (
        (col_last, cols.at[0], col_sem.at[0], east),
        (col_first, cols.at[1], col_sem.at[1], west),
        (row_last, rows.at[up_slot], row_sem.at[up_slot], up),
        (row_first, rows.at[down_slot], row_sem.at[down_slot], down),
    )
    sends = []
    for i, (src, dst, sem, peer) in enumerate(plan):
        copy = pltpu.make_async_remote_copy(
            src_ref=src, dst_ref=dst, send_sem=send_sem.at[i], recv_sem=sem,
            device_id=peer, device_id_type=MESH,
        )
        copy.start()
        sends.append(copy)
    arrivals = (
        (col_last, cols.at[0], col_sem.at[0]),
        (col_first, cols.at[1], col_sem.at[1]),
        (row_last, rows.at[0], row_sem.at[0]),
        (row_first, rows.at[1], row_sem.at[1]),
    )
    for src, dst, sem in arrivals:
        pltpu.make_async_remote_copy(
            src_ref=src, dst_ref=dst, send_sem=send_sem.at[0], recv_sem=sem,
            device_id=east, device_id_type=MESH,
        ).wait_recv()
    for copy in sends:
        copy.wait_send()
    west_out[...] = cols[0]
    east_out[...] = cols[1]
    north_out[...] = rows[0]
    south_out[...] = rows[1]


def halo_swap(col_last, col_first, row_last, row_first, collective_id):
    lon_n, lat_n = lax.axis_size("lon"), lax.axis_size("lat")
    vmem = pl.BlockSpec(memory_space=pltpu.VMEM)
    return pl.pallas_call(
        functools.partial(halo_body, lon_n, lat_n),
        out_shape=(
            jax.ShapeDtypeStruct(col_last.shape, col_last.dtype),
            jax.ShapeDtypeStruct(col_last.shape, col_last.dtype),
            jax.ShapeDtypeStruct(row_last.shape, row_last.dtype),
            jax.ShapeDtypeStruct(row_last.shape, row_last.dtype),
        ),
        in_specs=[vmem] * 4,
        out_specs=(vmem,) * 4,
        scratch_shapes=[
            pltpu.VMEM((2,) + col_last.shape, col_last.dtype),
            pltpu.VMEM((2,) + row_last.shape, row_last.dtype),
            pltpu.SemaphoreType.DMA((4,)),
            pltpu.SemaphoreType.DMA((2,)),
            pltpu.SemaphoreType.DMA((2,)),
        ],
        compiler_params=pltpu.CompilerParams(
            collective_id=collective_id, has_side_effects=True
        ),
    )(col_last, col_first, row_last, row_first)


def lev_copy(src, dst, send, recv, peer):
    return pltpu.make_async_remote_copy(
        src_ref=src, dst_ref=dst, send_sem=send, recv_sem=recv,
        device_id={"lev": peer}, device_id_type=MESH,
    )


def scatter_start(n, part_ref, pieces, sends, recvs):
    lev = lax.axis_index("lev")
    rows = part_ref.shape[1] // n
    for d in range(1, n):
        peer = lax.rem(lev + d, n)
        lev_copy(
            part_ref.at[:, pl.ds(pl.multiple_of(peer * rows, rows), rows), :],
            pieces.at[lev], sends.at[d - 1], recvs.at[lev], peer,
        ).start()
    pieces[lev] = part_ref[:, pl.ds(pl.multiple_of(lev * rows, rows), rows), :]


def scatter_finish_gather_start(n, part_ref, pieces, reduced, sends, recvs, gsends, grecvs):
    lev = lax.axis_index("lev")
    rows = part_ref.shape[1] // n
    for d in range(1, n):
        sender = lax.rem(lev + n - d, n)
        peer = lax.rem(lev + d, n)
        lev_copy(
            part_ref.at[:, pl.ds(0, rows), :], pieces.at[sender],
            sends.at[d - 1], recvs.at[sender], sender,
        ).wait_recv()
        lev_copy(
            part_ref.at[:, pl.ds(0, rows), :], pieces.at[sender],
            sends.at[d - 1], recvs.at[sender], peer,
        ).wait_send()
    total = pieces[0]
    for s in range(1, n):
        total = total + pieces[s]
    reduced[lev] = total
    for d in range(1, n):
        peer = lax.rem(lev + d, n)
        lev_copy(reduced.at[lev], reduced.at[lev], gsends.at[d - 1], grecvs.at[lev], peer).start()


def gather_finish(n, out_ref, reduced, gsends, grecvs):
    lev = lax.axis_index("lev")
    rows = out_ref.shape[1] // n
    for d in range(1, n):
        sender = lax.rem(lev + n - d, n)
        lev_copy(reduced.at[sender], reduced.at[sender], gsends.at[d - 1], grecvs.at[sender], sender).wait_recv()
        lev_copy(reduced.at[lev], reduced.at[lev], gsends.at[d - 1], grecvs.at[lev], lax.rem(lev + d, n)).wait_send()
    for q in range(n):
        out_ref[:, q * rows:(q + 1) * rows, :] = reduced[q]


def lev_scratch(n, shape, dtype):
    piece = (shape[0], shape[1] // n, shape[2])
    return [
        pltpu.VMEM((n,) + piece, dtype),
        pltpu.VMEM((n,) + piece, dtype),
        pltpu.SemaphoreType.DMA((n - 1,)),
        pltpu.SemaphoreType.DMA((n,)),
        pltpu.SemaphoreType.DMA((n - 1,)),
        pltpu.SemaphoreType.DMA((n,)),
    ]


def exchange_body(lev_n, owners, lat_n, rows_ref, part_ref, rows_out, sum_out,
                  got, row_send, row_recv, pieces, reduced, sends, recvs, gsends, grecvs):
    lat = lax.axis_index("lat")
    lev = lax.axis_index("lev")
    me = lax.axis_index("lon") * lat_n + lat

    def place(peer):
        return {"lon": peer // lat_n, "lat": lax.rem(peer, lat_n)}

    barrier = pltpu.get_barrier_semaphore()

    def greet(d, carry):
        peer = lax.rem(me + d, owners)
        pl.semaphore_signal(barrier, inc=1, device_id=place(peer), device_id_type=MESH)
        return carry

    lax.fori_loop(1, owners, greet, 0)
    for d in range(1, lev_n):
        pl.semaphore_signal(
            barrier, inc=1, device_id={"lev": lax.rem(lev + d, lev_n)}, device_id_type=MESH
        )
    pl.semaphore_wait(barrier, owners - 1 + lev_n - 1)
    scatter_start(lev_n, part_ref, pieces, sends, recvs)

    def row_copy(peer, target):
        return pltpu.make_async_remote_copy(
            src_ref=rows_ref.at[pl.ds(peer, 1)],
            dst_ref=got.at[pl.ds(target, 1)],
            send_sem=row_send.at[peer],
            recv_sem=row_recv.at[target],
            device_id=place(peer),
            device_id_type=MESH,
        )

    def send(d, carry):
        row_copy(lax.rem(me + d, owners), me).start()
        return carry

    lax.fori_loop(1, owners, send, 0)
    got[pl.ds(me, 1), :] = rows_ref[pl.ds(me, 1), :]
    scatter_finish_gather_start(lev_n, part_ref, pieces, reduced, sends, recvs, gsends, grecvs)

    def finish(d, carry):
        source = lax.rem(me + owners - d, owners)
        row_copy(lax.rem(me + d, owners), me).wait_send()
        row_copy(source, source).wait_recv()
        return carry

    lax.fori_loop(1, owners, finish, 0)
    gather_finish(lev_n, sum_out, reduced, gsends, grecvs)
    rows_out[...] = got[...]


def exchange(rows, part, collective_id):
    lev_n = lax.axis_size("lev")
    lat_n = lax.axis_size("lat")
    owners = lax.axis_size("lon") * lat_n
    vmem = pl.BlockSpec(memory_space=pltpu.VMEM)
    return pl.pallas_call(
        functools.partial(exchange_body, lev_n, owners, lat_n),
        out_shape=(
            jax.ShapeDtypeStruct(rows.shape, rows.dtype),
            jax.ShapeDtypeStruct(part.shape, part.dtype),
        ),
        in_specs=[vmem, vmem],
        out_specs=(vmem, vmem),
        scratch_shapes=[
            pltpu.VMEM(rows.shape, rows.dtype),
            pltpu.SemaphoreType.DMA((owners,)),
            pltpu.SemaphoreType.DMA((owners,)),
        ] + lev_scratch(lev_n, part.shape, part.dtype),
        compiler_params=pltpu.CompilerParams(
            collective_id=collective_id, has_side_effects=True
        ),
    )(rows, part)


def lev_direct_body(n, part_ref, out_ref, slots, send_sem, recv_sem):
    me = lax.axis_index("lev")
    barrier = pltpu.get_barrier_semaphore()
    for d in range(1, n):
        pl.semaphore_signal(
            barrier, inc=1, device_id={"lev": lax.rem(me + d, n)}, device_id_type=MESH
        )
    pl.semaphore_wait(barrier, n - 1)
    for d in range(1, n):
        lev_copy(part_ref, slots.at[me], send_sem.at[d - 1], recv_sem.at[me], lax.rem(me + d, n)).start()
    slots[me] = part_ref[...]
    for d in range(1, n):
        sender = lax.rem(me + n - d, n)
        lev_copy(part_ref, slots.at[sender], send_sem.at[d - 1], recv_sem.at[sender], sender).wait_recv()
        lev_copy(part_ref, slots.at[sender], send_sem.at[d - 1], recv_sem.at[sender], lax.rem(me + d, n)).wait_send()
    total = slots[0]
    for s in range(1, n):
        total = total + slots[s]
    out_ref[...] = total


def lev_direct(x, collective_id):
    n = lax.axis_size("lev")
    return pl.pallas_call(
        functools.partial(lev_direct_body, n),
        out_shape=jax.ShapeDtypeStruct(x.shape, x.dtype),
        in_specs=[pl.BlockSpec(memory_space=pltpu.VMEM)],
        out_specs=pl.BlockSpec(memory_space=pltpu.VMEM),
        scratch_shapes=[
            pltpu.VMEM((n,) + x.shape, x.dtype),
            pltpu.SemaphoreType.DMA((n - 1,)),
            pltpu.SemaphoreType.DMA((n,)),
        ],
        compiler_params=pltpu.CompilerParams(
            collective_id=collective_id, has_side_effects=True
        ),
    )(x)


def halo_places(lon_n, lat_n):
    lon = lax.axis_index("lon")
    lat = lax.axis_index("lat")
    half = lon_n // 2
    top = lat // (lat_n - 1)
    inner = (lat + lat_n - 1) // lat_n
    east = {"lon": lax.rem(lon + 1, lon_n)}
    west = {"lon": lax.rem(lon + lon_n - 1, lon_n)}
    up = {"lon": lax.rem(lon + half * top, lon_n), "lat": lat + 1 - top}
    down = {"lon": lax.rem(lon + half * (1 - inner), lon_n), "lat": lat - inner}
    return east, west, up, down, 1 - top, 1 - inner


def mix_halo_body(lev_n, lon_n, lat_n, p_ref, pe_ref, st_ref, cs_out, halo_out,
                  pieces, reduced, sends, recvs, gsends, grecvs,
                  pe_slots, pe_send, pe_recv, spread, mixed, got, h_send, h_recv):
    lev = lax.axis_index("lev")
    east, west, up, down, up_slot, down_slot = halo_places(lon_n, lat_n)
    barrier = pltpu.get_barrier_semaphore()
    for d in range(1, lev_n):
        pl.semaphore_signal(
            barrier, inc=1, device_id={"lev": lax.rem(lev + d, lev_n)}, device_id_type=MESH
        )
    for peer in (east, west, up, down):
        pl.semaphore_signal(barrier, inc=1, device_id=peer, device_id_type=MESH)
    pl.semaphore_wait(barrier, lev_n - 1 + 4)
    scatter_start(lev_n, p_ref, pieces, sends, recvs)
    for d in range(1, lev_n):
        lev_copy(pe_ref, pe_slots.at[lev], pe_send.at[d - 1], pe_recv.at[lev], lax.rem(lev + d, lev_n)).start()
    pe_slots[lev] = pe_ref[...]
    scatter_finish_gather_start(lev_n, p_ref, pieces, reduced, sends, recvs, gsends, grecvs)
    for d in range(1, lev_n):
        sender = lax.rem(lev + lev_n - d, lev_n)
        lev_copy(pe_ref, pe_slots.at[sender], pe_send.at[d - 1], pe_recv.at[sender], sender).wait_recv()
        lev_copy(pe_ref, pe_slots.at[sender], pe_send.at[d - 1], pe_recv.at[sender], lax.rem(lev + d, lev_n)).wait_send()
    pe_sum = pe_slots[0]
    for s in range(1, lev_n):
        pe_sum = pe_sum + pe_slots[s]
    tracers = pe_ref.shape[1]
    copies_k = spread.shape[1] // tracers
    for k in range(copies_k):
        spread[:, pl.ds(k, tracers, stride=copies_k), :] = pe_sum
    share = st_ref[1]
    mixed[...] = (1.0 - share) * st_ref[0] + share * (spread[...] / st_ref[2])
    plan = (
        (mixed.at[0], got.at[0], h_recv.at[0], east),
        (mixed.at[0], got.at[1], h_recv.at[1], west),
        (mixed.at[1], got.at[2 + up_slot], h_recv.at[2 + up_slot], up),
        (mixed.at[2], got.at[2 + down_slot], h_recv.at[2 + down_slot], down),
    )
    copies = []
    for i, (src, dst, sem, peer) in enumerate(plan):
        copy = pltpu.make_async_remote_copy(
            src_ref=src, dst_ref=dst, send_sem=h_send.at[i], recv_sem=sem,
            device_id=peer, device_id_type=MESH,
        )
        copy.start()
        copies.append(copy)
    gather_finish(lev_n, cs_out, reduced, gsends, grecvs)
    for i in range(4):
        pltpu.make_async_remote_copy(
            src_ref=mixed.at[0], dst_ref=got.at[i], send_sem=h_send.at[i], recv_sem=h_recv.at[i],
            device_id=east, device_id_type=MESH,
        ).wait_recv()
    for copy in copies:
        copy.wait_send()
    halo_out[...] = got[...]


def mix_halo(p, pe, st, collective_id):
    lev_n, lon_n, lat_n = lax.axis_size("lev"), lax.axis_size("lon"), lax.axis_size("lat")
    vmem = pl.BlockSpec(memory_space=pltpu.VMEM)
    edge_shape = st.shape[1:]
    halo_shape = (4,) + edge_shape[1:]
    return pl.pallas_call(
        functools.partial(mix_halo_body, lev_n, lon_n, lat_n),
        out_shape=(
            jax.ShapeDtypeStruct(p.shape, p.dtype),
            jax.ShapeDtypeStruct(halo_shape, p.dtype),
        ),
        in_specs=[vmem] * 3,
        out_specs=(vmem, vmem),
        scratch_shapes=lev_scratch(lev_n, p.shape, p.dtype) + [
            pltpu.VMEM((lev_n,) + pe.shape, p.dtype),
            pltpu.SemaphoreType.DMA((lev_n - 1,)),
            pltpu.SemaphoreType.DMA((lev_n,)),
            pltpu.VMEM(edge_shape, p.dtype),
            pltpu.VMEM(edge_shape, p.dtype),
            pltpu.VMEM(halo_shape, p.dtype),
            pltpu.SemaphoreType.DMA((4,)),
            pltpu.SemaphoreType.DMA((4,)),
        ],
        compiler_params=pltpu.CompilerParams(
            collective_id=collective_id, has_side_effects=True
        ),
    )(p, pe, st)


def lev_sum(x, collective_id):
    n = lax.axis_size("lev")
    return pl.pallas_call(
        functools.partial(lev_sum_body, n),
        out_shape=jax.ShapeDtypeStruct(x.shape, x.dtype),
        in_specs=[pl.BlockSpec(memory_space=pltpu.VMEM)],
        out_specs=pl.BlockSpec(memory_space=pltpu.VMEM),
        scratch_shapes=lev_scratch(n, x.shape, x.dtype),
        compiler_params=pltpu.CompilerParams(
            collective_id=collective_id, has_side_effects=True
        ),
        cost_estimate=pl.CostEstimate(
            flops=n * x.size, bytes_accessed=(2 * n + 2) * x.size * 4, transcendentals=0
        ),
    )(x)


def from_behind(value, axis, steps):
    count = lax.axis_size(axis)
    pairs = [(source, (source + steps) % count) for source in range(count)]
    return lax.ppermute(value, axis, pairs)


def from_behind_2(block, axis, distance):
    devices = range(lax.axis_size(axis))
    route = [(i - distance, i) for i in devices if i - distance in devices]
    return lax.ppermute(block, axis, route)


def extended(x, sides, width, wrap):
    for axis, dim in sides:
        size, length = (lax.axis_size(axis), x.shape[dim])
        up = [(i, (i + 1) % size) for i in range(size if wrap else size - 1)]
        down = [(j, i) for i, j in up]
        last = lax.slice_in_dim(x, length - width, length, axis=dim)
        initial = lax.slice_in_dim(x, 0, width, axis=dim)
        before = lax.ppermute(last, axis, up)
        after = lax.ppermute(initial, axis, down)
        x = jnp.concatenate([before, x, after], axis=dim)
    return x


def mix_sum(partial_sum):
    return lax.psum(partial_sum, "lev")


def on_device(
    adjoint_field,
    east_courant,
    north_courant,
    pole_courant,
    mix_fraction,
    detrain_share,
    sounding_owner,
    sounding_cell,
    sounding_count,
    sounding_forcing,
):
    lon_count = lax.axis_size("lon")
    lat_count = lax.axis_size("lat")
    lat_place = lax.axis_index("lat")
    owner_self = lax.axis_index("lon") * lat_count + lat_place
    tracers, lev_dev, lat_rows, lon_cols = adjoint_field.shape
    step_count = sounding_forcing.shape[0]
    slot_count = sounding_forcing.shape[2]
    grid_cells = lat_rows * lon_cols
    detrain_part = jnp.sum(detrain_share, axis=0)
    owner_count = lon_count * lat_count
    cap = 4
    live_slots = jnp.arange(slot_count, dtype=jnp.int32)[None, :] < sounding_count
    values = jnp.where(live_slots[:, None, :], sounding_forcing, 0.0)
    owner_ids = sounding_owner[:, :, 0]
    slot_iota = jnp.arange(slot_count, dtype=jnp.int32)
    earlier = slot_iota[None, :, None] < slot_iota[None, None, :]
    same_owner = owner_ids[:, :, None] == owner_ids[:, None, :]
    rank = jnp.sum(jnp.logical_and(earlier, same_owner), axis=1, dtype=jnp.int32)
    position = owner_ids * cap + rank
    bucket_iota = jnp.arange(owner_count * cap, dtype=jnp.int32)
    chosen = position[:, :, None] == bucket_iota[None, None, :]
    bucket_values = jnp.sum(
        jnp.where(chosen[:, None, :, :], values[:, :, :, None], 0.0), axis=2
    )
    bucket_cell = jnp.max(
        jnp.where(chosen, sounding_cell[:, :, None] + 1, 0), axis=1
    ).astype(jnp.float32) - 1.0
    packed = jnp.concatenate([bucket_values, bucket_cell[:, None, :]], axis=1)
    packed = packed.reshape(step_count, lev_dev + 1, owner_count, cap)
    packed = jnp.transpose(packed, (2, 0, 1, 3))
    row_width = step_count * (lev_dev + 1) * cap
    rows = packed.reshape(owner_count, row_width)
    early_part = jnp.concatenate(
        [jnp.sum(detrain_share[None] * adjoint_field, axis=1), detrain_part[None]], axis=0
    )
    arrived, early = exchange(rows, early_part, 0)
    arrived = arrived.reshape(owner_count, step_count, lev_dev + 1, cap)
    arrived = jnp.transpose(arrived, (1, 2, 0, 3)).reshape(
        step_count, lev_dev + 1, owner_count * cap
    )
    cells = arrived[:, lev_dev, :].astype(jnp.int32)
    row_hit = (cells // lon_cols)[:, :, None] == jnp.arange(lat_rows, dtype=jnp.int32)
    col_hit = (cells % lon_cols)[:, :, None] == jnp.arange(lon_cols, dtype=jnp.int32)
    spread = jnp.where(row_hit[:, None, :, :], arrived[:, :lev_dev, :, None], 0.0)
    forcing_grid = jnp.einsum(
        "tker,tec->tkrc", spread, col_hit.astype(jnp.float32), precision=lax.Precision.HIGHEST
    )
    row_index = jnp.arange(lat_rows, dtype=jnp.int32)[None, :, None]
    at_top = jnp.logical_and(lat_place == lat_count - 1, row_index == lat_rows - 1)
    at_bottom = jnp.logical_and(lat_place == 0, row_index == 0)
    upwind_east = jnp.maximum(east_courant, 0.0)
    forcing_part = jnp.sum(detrain_share * forcing_grid[step_count - 1], axis=0)
    forcing_sum = lev_direct(forcing_part[None], 4)[0]
    adjoint = adjoint_field
    for position in range(step_count):
        step_now = step_count - 1 - position
        adjoint = adjoint + forcing_grid[step_now][None]
        if position == 0:
            column_sum = early[:tracers] + forcing_sum[None]
            total_detrain = early[tracers]
        else:
            partial_sum = jnp.sum(detrain_share[None] * adjoint, axis=1)
            planes = tracers * lev_dev

            def packed(x, fill=0.0):
                x = jnp.broadcast_to(x, (tracers, lev_dev) + x.shape[2:]).reshape(
                    (planes,) + x.shape[2:]
                )
                return x

            def edge_set(x, fill=0.0):
                rest = jnp.full((planes, lon_cols - 2 * lat_rows), fill, jnp.float32)
                cols = jnp.concatenate(
                    [packed(x[..., :, -1]), packed(x[..., :, 0]), rest], axis=1
                )
                return jnp.stack([cols, packed(x[..., -1, :]), packed(x[..., 0, :])])

            part_rest = jnp.zeros((tracers, lon_cols - 2 * lat_rows), jnp.float32)
            part_edges = jnp.stack([
                jnp.concatenate([partial_sum[:, :, -1], partial_sum[:, :, 0], part_rest], axis=1),
                partial_sum[:, -1, :],
                partial_sum[:, 0, :],
            ])
            column_sum, halos = mix_halo(
                partial_sum,
                part_edges,
                jnp.stack([
                    edge_set(adjoint),
                    edge_set(mix_fraction[None]),
                    edge_set(total_detrain[None, None], 1.0),
                ]),
                5,
            )
        adjoint = (1.0 - mix_fraction)[None] * adjoint + mix_fraction[None] * (
            column_sum / total_detrain
        )[:, None]
        if position == 1:
            west_halo = halos[0, :, :lat_rows]
            east_halo = halos[1, :, lat_rows:2 * lat_rows]
            north_halo = halos[2]
            south_halo = halos[3]
        planes = tracers * lev_dev
        if position == 0:
            col_last = adjoint[:, :, :, -1].reshape(planes, lat_rows)
            col_first = adjoint[:, :, :, 0].reshape(planes, lat_rows)
            row_last = adjoint[:, :, -1, :].reshape(planes, lon_cols)
            row_first = adjoint[:, :, 0, :].reshape(planes, lon_cols)
            if position == 0:
                col_last = jnp.concatenate([col_last, east_courant[:, :, -1]], axis=0)
                col_first = jnp.concatenate([col_first, east_courant[:, :, 0]], axis=0)
                row_last = jnp.concatenate([row_last, north_courant[:, -1, :]], axis=0)
                row_first = jnp.concatenate([row_first, pole_courant], axis=0)
            west_halo, east_halo, north_halo, south_halo = halo_swap(
                col_last, col_first, row_last, row_first, 2 + position
            )
            if position == 0:
                west_wind = jnp.concatenate(
                    [west_halo[planes:, :, None], east_courant[:, :, :-1]], axis=2
                )
                partner_top = north_halo[planes:]
                south_wind = jnp.concatenate(
                    [south_halo[planes:, None, :], north_courant[:, :-1, :]], axis=1
                )
                partner_pole = south_halo[planes:]
                upwind_west = -jnp.minimum(west_wind, 0.0)
                upwind_north = jnp.maximum(north_courant, 0.0) + jnp.where(
                    at_top, -jnp.minimum(partner_top, 0.0)[:, None, :], 0.0
                )
                upwind_south = jnp.where(
                    at_bottom,
                    (jnp.maximum(pole_courant, 0.0) - jnp.minimum(partner_pole, 0.0))[:, None, :],
                    -jnp.minimum(south_wind, 0.0),
                )
                west_halo, east_halo = west_halo[:planes], east_halo[:planes]
                north_halo, south_halo = north_halo[:planes], south_halo[:planes]
        east_side = jnp.concatenate(
            [adjoint[:, :, :, 1:], east_halo.reshape(tracers, lev_dev, lat_rows, 1)], axis=3
        )
        west_side = jnp.concatenate(
            [west_halo.reshape(tracers, lev_dev, lat_rows, 1), adjoint[:, :, :, :-1]], axis=3
        )
        north_side = jnp.concatenate(
            [adjoint[:, :, 1:, :], north_halo.reshape(tracers, lev_dev, 1, lon_cols)], axis=2
        )
        south_side = jnp.concatenate(
            [south_halo.reshape(tracers, lev_dev, 1, lon_cols), adjoint[:, :, :-1, :]], axis=2
        )
        adjoint = (
            adjoint
            + upwind_east * (east_side - adjoint)
            + upwind_west * (west_side - adjoint)
            + upwind_north * (north_side - adjoint)
            + upwind_south * (south_side - adjoint)
        )
    return adjoint


def solution(mesh):
    return jax.shard_map(
        on_device,
        mesh=mesh,
        in_specs=(
            P(None, "lev", "lat", "lon"),
            P("lev", "lat", "lon"),
            P("lev", "lat", "lon"),
            P("lev", "lon"),
            P("lev", "lat", "lon"),
            P("lev", "lat", "lon"),
            P(None, ("lon", "lat"), None),
            P(None, ("lon", "lat")),
            P(None, ("lon", "lat")),
            P(None, "lev", ("lon", "lat")),
        ),
        out_specs=P(None, "lev", "lat", "lon"),
        check_vma=False,
    )
```
